32 devices in a mesh: fsdp: 4 (over x, core), ctx: 8 (over z, y).
Axes of the slice: x: 2, y: 2, z: 4, core: 2. Of those that a mesh axis runs over, the one named last changes fastest.
Arguments:
- hidden: bfloat16 [4, 1024, 768], P('fsdp', 'ctx'), may hold values from -6 to 6
- encoded: bfloat16 [4, 256, 768], P('fsdp', 'ctx'), may hold values from -6 to 6
- cotangent: bfloat16 [4, 1024, 768], P('fsdp', 'ctx'), may hold values from -6 to 6
- dec_seg: int32 [4, 1024], P('fsdp', 'ctx'), may hold values from 0 to 15, as said below
- enc_seg: int32 [4, 256], P('fsdp', 'ctx'), may hold values from 0 to 15, as said below
- self_qkv: float32 [768, 2304], P('fsdp'), may hold values from -0.21875 to 0.21875
- self_out: float32 [768, 768], P('fsdp'), may hold values from -1.75 to 1.75
- cross_q: float32 [768, 768], P('fsdp'), may hold values from -0.21875 to 0.21875
- cross_kv: float32 [768, 1536], P('fsdp'), may hold values from -0.21875 to 0.21875
- cross_out: float32 [768, 768], P('fsdp'), may hold values from -0.875 to 0.875
- ffn_in: float32 [768, 3072], P('fsdp'), may hold values from -0.21875 to 0.21875
- ffn_out: float32 [3072, 768], P('fsdp'), may hold values from -0.109375 to 0.109375
- biases: float32 [10, 768], P(None, 'fsdp'), may hold values from -3 to 3
- gains: float32 [3, 768], P(None, 'fsdp'), may hold values from 0.25 to 1.75
- ffn_bias: float32 [3072], P('fsdp'), may hold values from -3 to 3
Outputs:
- output: bfloat16 [4, 1024, 768], P('fsdp', 'ctx')
- d_hidden: float32 [4, 1024, 768], P('fsdp', 'ctx')
- d_encoded: float32 [4, 256, 768], P('fsdp', 'ctx')
- d_self_qkv: float32 [768, 2304], P('fsdp')
- d_self_out: float32 [768, 768], P('fsdp')
- d_cross_q: float32 [768, 768], P('fsdp')
- d_cross_kv: float32 [768, 1536], P('fsdp')
- d_cross_out: float32 [768, 768], P('fsdp')
- d_ffn_in: float32 [768, 3072], P('fsdp')
- d_ffn_out: float32 [3072, 768], P('fsdp')
- d_biases: float32 [10, 768], P(None, 'fsdp')
- d_gains: float32 [3, 768], P(None, 'fsdp')
- d_ffn_bias: float32 [3072], P('fsdp')
The draws below stay inside these ranges and needn't reach their ends.
Inputs may be any that keep to these rules, and one draw needn't show every extreme that they name: `dec_seg`: within a sequence the numbers never fall and each of 0 to 15 appears. `enc_seg`: within a sequence the numbers never fall and each of 0 to 15 appears, so every document of dec_seg has encoder rows.
All inputs are finite; a program needn't handle non-finite values.
Results may differ from the reference program's by a relative error of at most 0.025.
Values may be sent and summed in bfloat16 or wider, within the bound.
No kernel may reach another device: no remote copies, remote signals or barrier semaphores. Data moves between devices by JAX's collectives and lax.ppermute only.
A program may use at most 320 MiB of HBM per device.

```python
import jax
import jax.numpy as jnp
from jax import lax

D = 768
H = 12
FF = 3072
HD = 64
TOK_DEV = 128
ENC_DEV = 32
NDOC = 16
NBIAS = 10
SEQS = 4
LEN = 1024
ENC_LEN = 256


def end_cuts(seq_key, salt, per_device, total, chosen):
    early = jax.random.permutation(jax.random.fold_in(seq_key, salt), per_device - 1)[:NDOC - 1] + 1
    late = jax.random.permutation(jax.random.fold_in(seq_key, salt + 1), per_device - 1)[:NDOC - 1] + (total - per_device + 1)
    slots = jnp.arange(NDOC - 1, dtype=jnp.int32)
    later = jnp.clip(slots - chosen, 0, NDOC - 2)
    return jnp.where(slots < chosen, early, late[later]).astype(jnp.int32)


def document_weights(seq_key):
    powers = jax.random.randint(jax.random.fold_in(seq_key, 401), (NDOC,), 0, 8)
    leading = jax.random.randint(jax.random.fold_in(seq_key, 402), (NDOC,), 1, 9)
    return (leading * jnp.left_shift(jnp.ones((NDOC,), jnp.int32), powers)).astype(jnp.int32)


def spread_cuts(weights, total):
    spare = total - NDOC
    running = jnp.cumsum(weights)[:NDOC - 1]
    whole = jnp.sum(weights)
    slots = jnp.arange(NDOC - 1, dtype=jnp.int32)
    return (slots + 1 + running * spare // whole).astype(jnp.int32)


def document_ids(key, salt, per_device, total):
    spanning = jax.random.randint(jax.random.fold_in(key, 77), (), 0, SEQS)

    def one_sequence(index):
        seq_key = jax.random.fold_in(jax.random.fold_in(key, index), salt)
        chosen = jax.random.randint(jax.random.fold_in(seq_key, 101), (), 0, NDOC)
        ends = end_cuts(seq_key, salt, per_device, total, chosen)
        spread = spread_cuts(document_weights(seq_key), total)
        cuts = jnp.where(index == spanning, ends, spread)
        places = jnp.arange(total, dtype=jnp.int32)
        return jnp.sum((places[:, None] >= cuts[None, :]).astype(jnp.int32), axis=1).astype(jnp.int32)
    return jax.vmap(one_sequence)(jnp.arange(SEQS, dtype=jnp.int32))


def draw_dec_seg(key, part):
    return document_ids(key, 201, TOK_DEV, LEN)


def draw_enc_seg(key, part):
    return document_ids(key, 301, ENC_DEV, ENC_LEN)


def block_scale(own_key, extent, shards, least, largest):
    loudness, own = 1.0, jax.random.fold_in(own_key, 6)
    for position, shards_of in shards:
        heights = jnp.exp(jax.random.uniform(jax.random.fold_in(own, position), (shards_of,), jnp.float32, least / len(shards), largest / len(shards)))
        loudness = loudness * jnp.repeat(heights, extent[position] // shards_of).reshape([-1 if axis == position else 1 for axis in range(len(extent))])
    return loudness


def bell_draw(key, shape, scale, bound, shards=(), kind=jnp.bfloat16):
    values = scale * jax.random.normal(key, shape, jnp.float32)
    if shards:
        values = values * block_scale(key, shape, shards, -0.22, 0.18)
    return jnp.clip(values, -bound, bound).astype(kind)


def setup_inputs(seed: int = 0) -> dict:
    seeds = jax.random.split(jax.random.key(seed), 16)
    return {
        "hidden": bell_draw(seeds[0], (SEQS, LEN, D), 1.0, 6.0, ((0, 4), (1, 8))),
        "encoded": bell_draw(seeds[1], (SEQS, ENC_LEN, D), 1.0, 6.0, ((0, 4), (1, 8))),
        "cotangent": bell_draw(seeds[2], (SEQS, LEN, D), 1.0, 6.0, ((0, 4), (1, 8))),
        "dec_seg": draw_dec_seg(jax.random.fold_in(seeds[15], 71), 0),
        "enc_seg": draw_enc_seg(jax.random.fold_in(seeds[15], 71), 0),
        "self_qkv": bell_draw(seeds[5], (D, 3 * D), D ** -0.5, 0.21875, ((0, 4),), jnp.float32),
        "self_out": bell_draw(seeds[6], (D, D), (max(1, D * 16 // LEN)) ** -0.5, 1.75, ((0, 4),), jnp.float32),
        "cross_q": bell_draw(seeds[7], (D, D), D ** -0.5, 0.21875, ((0, 4),), jnp.float32),
        "cross_kv": bell_draw(seeds[8], (D, 2 * D), D ** -0.5, 0.21875, ((0, 4),), jnp.float32),
        "cross_out": bell_draw(seeds[9], (D, D), (max(1, D * 16 // ENC_LEN)) ** -0.5, 0.875, ((0, 4),), jnp.float32),
        "ffn_in": bell_draw(seeds[10], (D, FF), D ** -0.5, 0.21875, ((0, 4),), jnp.float32),
        "ffn_out": bell_draw(seeds[11], (FF, D), FF ** -0.5, 0.109375, ((0, 4),), jnp.float32),
        "biases": bell_draw(seeds[12], (NBIAS, D), 0.5, 3.0, ((1, 4),), jnp.float32),
        "gains": jnp.clip(1.0 + 0.15 * jax.random.normal(seeds[13], (3, D), jnp.float32), 0.25, 1.75),
        "ffn_bias": bell_draw(seeds[14], (FF,), 0.5, 3.0, ((0, 4),), jnp.float32),
    }


EPSILON = 1e-05
FLOOR_SCORE = -1e+30
HIGHEST = lax.Precision.HIGHEST

@jax.custom_vjp
def low(v):
    return lax.optimization_barrier(v.astype(jnp.bfloat16)).astype(jnp.float32)

@jax.custom_vjp
def low_back(v):
    return v

def low_keep(v):
    return (low(v), None)

def low_pass(kept, grad):
    return (grad,)

def back_keep(v):
    return (v, None)

def back_low(kept, grad):
    return (low(grad),)
low.defvjp(low_keep, low_pass)
low_back.defvjp(back_keep, back_low)

def layer_norm(values, gain, shift):
    center = values - lax.optimization_barrier(jnp.mean(values, axis=-1, keepdims=True))
    spread = lax.optimization_barrier(jnp.mean(center * center, axis=-1, keepdims=True))
    return center * lax.rsqrt(spread + EPSILON) * gain + shift

def matmul(left, right):
    return jnp.dot(left, right, precision=HIGHEST)

def attend(queries, keys, values, query_segments, key_segments, causal):
    count = queries.shape[0]
    block = 512 if count % 512 == 0 else count
    blocks = count // block
    key_places = jnp.arange(keys.shape[0], dtype=jnp.int32)
    query_blocks = queries.reshape(blocks, block, H, HD)
    segment_blocks = query_segments.reshape(blocks, block)
    starts = jnp.arange(blocks, dtype=jnp.int32) * block

    def one_block(items):
        query_block, segment_block, first = items
        scores = low_back(jnp.einsum('qhd,khd->hqk', query_block, keys, precision=HIGHEST))
        allowed = segment_block[:, None] == key_segments[None, :]
        if causal:
            places = first + jnp.arange(block, dtype=jnp.int32)
            allowed = allowed & (key_places[None, :] <= places[:, None])
        scores = jnp.where(allowed[None], scores, FLOOR_SCORE)
        top = lax.optimization_barrier(jnp.max(scores, axis=2, keepdims=True))
        weights = jnp.exp(scores - top)
        probs = weights / lax.optimization_barrier(jnp.sum(weights, axis=2, keepdims=True))
        return jnp.einsum('hqk,khd->qhd', low(probs), values, precision=HIGHEST)
    result = lax.map(jax.checkpoint(one_block), (query_blocks, segment_blocks, starts))
    return result.reshape(count, H * HD)

def layer(inputs, sources, segments, source_segments, w_qkv, w_so, w_cq, w_ckv, w_co, w_fi, w_fo, bias_rows, gain_rows, inner_bias):
    scale = HD ** (-0.5)
    w_qkv = low(w_qkv)
    w_so = low(w_so)
    w_cq = low(w_cq)
    w_ckv = low(w_ckv)
    w_co = low(w_co)
    w_fi = low(w_fi)
    w_fo = low(w_fo)
    bias = low(bias_rows)
    gain = low(gain_rows)
    inner_bias = low(inner_bias)
    count = inputs.shape[0]
    projected = matmul(inputs, w_qkv)
    queries = low_back(low((projected[:, :D] + bias[3]) * scale))
    keys = low_back(low(projected[:, D:2 * D]))
    values = low_back(low(projected[:, 2 * D:] + bias[4]))
    attended = attend(queries.reshape(count, H, HD), keys.reshape(count, H, HD), values.reshape(count, H, HD), segments, segments, True)
    attended = low_back(low(attended))
    self_branch = low_back(matmul(attended, w_so) + bias[5])
    first = layer_norm(inputs + self_branch, gain[0], bias[0])
    first_low = low(first)
    cross_queries = low_back(low((matmul(first_low, w_cq) + bias[6]) * scale))
    source_proj = matmul(sources, w_ckv)
    source_keys = low_back(low(source_proj[:, :D]))
    source_values = low_back(low(source_proj[:, D:] + bias[7]))
    rows = sources.shape[0]
    crossed = attend(cross_queries.reshape(count, H, HD), source_keys.reshape(rows, H, HD), source_values.reshape(rows, H, HD), segments, source_segments, False)
    crossed = low_back(low(crossed))
    cross_branch = low_back(matmul(crossed, w_co) + bias[8])
    second = layer_norm(first + cross_branch, gain[1], bias[1])
    inner_pre = low_back(matmul(low(second), w_fi) + inner_bias)
    activated = low(jax.nn.gelu(inner_pre, approximate=False))
    ffn_branch = low_back(matmul(activated, w_fo) + bias[9])
    return layer_norm(second + ffn_branch, gain[2], bias[2])

def reference(hidden, encoded, cotangent, dec_seg, enc_seg, self_qkv, self_out, cross_q, cross_kv, cross_out, ffn_in, ffn_out, biases, gains, ffn_bias):
    weights = (self_qkv.astype(jnp.float32), self_out.astype(jnp.float32), cross_q.astype(jnp.float32), cross_kv.astype(jnp.float32), cross_out.astype(jnp.float32), ffn_in.astype(jnp.float32), ffn_out.astype(jnp.float32), biases.astype(jnp.float32), gains.astype(jnp.float32), ffn_bias.astype(jnp.float32))

    def one_sequence(totals, items):
        inputs, sources, grads_in, segments, source_segments = items

        def forward(inputs_f, sources_f, *params):
            return layer(inputs_f, sources_f, segments, source_segments, *params)
        result, pullback = jax.vjp(forward, inputs.astype(jnp.float32), sources.astype(jnp.float32), *weights)
        grads = pullback(grads_in.astype(jnp.float32))
        totals = tuple((total + grad for total, grad in zip(totals, grads[2:])))
        return (totals, (result.astype(jnp.bfloat16), grads[0], grads[1]))
    zeros = tuple((jnp.zeros_like(weight) for weight in weights))
    totals, (outputs, input_grads, source_grads) = lax.scan(one_sequence, zeros, (hidden, encoded, cotangent, dec_seg, enc_seg))
    return (outputs, input_grads, source_grads, totals[0], totals[1], totals[2], totals[3], totals[4], totals[5], totals[6], totals[7], totals[8], totals[9])
```

```python
import jax
import jax.numpy as jnp
from jax import lax
from jax.sharding import PartitionSpec as P

H = 12
HD = 64
EPSILON = 1e-05
FLOOR_SCORE = -1e30
LOW = jnp.bfloat16
WIDE = jnp.float32


def mm(left, right):
    return jnp.dot(left, right, preferred_element_type=WIDE)


def mm_tn(left, right):
    return lax.dot_general(left, right, (((0,), (0,)), ((), ())), preferred_element_type=WIDE)


def mm_nt(left, right):
    return lax.dot_general(left, right, (((1,), (1,)), ((), ())), preferred_element_type=WIDE)


def flip_model(value, bit):
    count = lax.axis_size("fsdp")
    return lax.ppermute(value, "fsdp", [(i, i ^ bit) for i in range(count)])


def flip_ctx(value, bit):
    count = lax.axis_size("ctx")
    return lax.ppermute(value, "ctx", [(i, i ^ bit) for i in range(count)])


def swap_places(value):
    model = lax.axis_size("fsdp")
    ctx = lax.axis_size("ctx")
    lines = ctx // model
    route = []
    for f in range(model):
        for z in range(model):
            for r in range(lines):
                route.append((f * ctx + z * lines + r, z * ctx + f * lines + r))
    return lax.ppermute(value, ("fsdp", "ctx"), route)


def line_bits():
    lines = lax.axis_size("ctx") // lax.axis_size("fsdp")
    bits = []
    bit = 1
    while bit < lines:
        bits.append(bit)
        bit *= 2
    return bits


def ctx_bits():
    bits = []
    bit = 1
    while bit < lax.axis_size("ctx"):
        bits.append(bit)
        bit *= 2
    return bits


def gather_plane(block):
    part = jnp.stack([block, flip_model(block, 2)])[None]
    for bit in line_bits():
        part = jnp.concatenate([part, flip_ctx(part, bit)], axis=0)
    return jnp.stack([part, flip_model(part, 1)], axis=1)


def normalize(values):
    center = values - jnp.mean(values, axis=-1, keepdims=True)
    spread = jnp.mean(center * center, axis=-1, keepdims=True)
    rate = lax.rsqrt(spread + EPSILON)
    return center * rate, rate


def normalize_back(grad, normal, rate, gain):
    up = grad * gain
    mean_up = jnp.mean(up, axis=-1, keepdims=True)
    mean_both = jnp.mean(up * normal, axis=-1, keepdims=True)
    return rate * (up - mean_up - normal * mean_both)


def tensor_sum(partial):
    rows = partial.shape[0] // 2
    half = rows // 2
    mine = partial[:rows] + flip_model(partial[rows:].astype(LOW), 1).astype(WIDE)
    other = flip_model(mine.astype(LOW), 2)
    other = jnp.concatenate([other[half:], other[:half]], axis=0)
    return mine + other.astype(WIDE)


def spread_rows(half):
    return jnp.concatenate([half, flip_model(half, 1)], axis=0)


def pick(stacked, index):
    return lax.dynamic_index_in_dim(stacked, index, 0, keepdims=False)


def to_columns(blocks, own):
    far = flip_model(jnp.stack([blocks[2], blocks[3]]), 2)
    near = flip_model(jnp.stack([blocks[1], far[1]]), 1)
    relative = jnp.stack([blocks[0], near[0], far[0], near[1]])
    return [pick(relative, own ^ j) for j in range(4)]


def sum_ctx(grad, ctx_index, to_rows, own):
    bits = ctx_bits()
    scatter = bits[:2]
    for bit in scatter:
        half = grad.shape[1] // 2
        side = (ctx_index // bit) % 2
        keep = lax.dynamic_slice_in_dim(grad, side * half, half, axis=1)
        send = lax.dynamic_slice_in_dim(grad, (1 - side) * half, half, axis=1)
        grad = keep + flip_ctx(send.astype(LOW), bit).astype(WIDE)
    for bit in bits[2:]:
        low = grad.astype(LOW)
        grad = low.astype(WIDE) + flip_ctx(low, bit).astype(WIDE)
    low = grad.astype(LOW)
    if to_rows:
        columns = to_columns([pick(low, own ^ k) for k in range(4)], own)
        low = jnp.stack(columns, axis=1)
        low = low.reshape(1, low.shape[0], -1)
    for bit in reversed(scatter):
        side = (ctx_index // bit) % 2
        other = flip_ctx(low, bit)
        first = jnp.where(side == 0, low, other)
        second = jnp.where(side == 0, other, low)
        low = jnp.concatenate([first, second], axis=1)
    return low[0].astype(WIDE)


def attend(queries, keys, values, allowed):
    heads = queries.shape[1] // HD
    outs = []
    probs = []
    for h in range(heads):
        cols = slice(h * HD, (h + 1) * HD)
        scores = mm_nt(queries[:, cols], keys[:, cols])
        scores = jnp.where(allowed, scores, FLOOR_SCORE)
        top = jnp.max(scores, axis=1, keepdims=True)
        weights = jnp.exp(scores - top)
        prob = weights / jnp.sum(weights, axis=1, keepdims=True)
        probs.append(prob)
        outs.append(mm(prob.astype(LOW), values[:, cols]))
    return jnp.concatenate(outs, axis=1).astype(LOW), probs


def attend_back(queries, keys, values, probs, grad):
    heads = queries.shape[1] // HD
    query_grads, key_grads, value_grads = [], [], []
    for h in range(heads):
        cols = slice(h * HD, (h + 1) * HD)
        prob = probs[h]
        prob_grad = mm_nt(grad[:, cols], values[:, cols])
        inner = jnp.sum(prob * prob_grad, axis=1, keepdims=True)
        score_grad = (prob * (prob_grad - inner)).astype(LOW)
        query_grads.append(mm(score_grad, keys[:, cols]))
        key_grads.append(mm_tn(score_grad, queries[:, cols]))
        value_grads.append(mm_tn(prob.astype(LOW), grad[:, cols]))
    return (
        jnp.concatenate(query_grads, axis=1),
        jnp.concatenate(key_grads + value_grads, axis=1),
    )


def sum_lines(value):
    for bit in reversed(line_bits()):
        mine = value[:bit]
        value = mine + flip_ctx(value[bit:].astype(LOW), bit).astype(WIDE)
    return value[0]


def body(
    hidden,
    encoded,
    cotangent,
    dec_seg,
    enc_seg,
    self_qkv,
    self_out,
    cross_q,
    cross_kv,
    cross_out,
    ffn_in,
    ffn_out,
    biases,
    gains,
    ffn_bias,
):
    tokens = hidden.shape[1]
    width = hidden.shape[2]
    sources = encoded.shape[1]
    model = lax.axis_size("fsdp")
    lines = lax.axis_size("ctx") // model
    own = lax.axis_index("fsdp")
    ctx_index = lax.axis_index("ctx")
    line = ctx_index % lines
    local = width // model
    scale = float(HD) ** (-0.5)
    rows = 4 * tokens
    half = 2 * tokens

    marks = jnp.concatenate([dec_seg[0], enc_seg[0]]).astype(LOW)
    marks = jnp.pad(marks, (0, width - tokens - sources))[None]
    block = jnp.concatenate([hidden[0], jnp.pad(marks, ((0, 15), (0, 0)))], axis=0)
    plane = gather_plane(swap_places(block))
    inputs = plane[..., :tokens, :].reshape(lines * rows, width)
    segments = plane[..., tokens, :tokens].reshape(lines * rows).astype(jnp.int32)
    source_segments = plane[..., tokens, tokens : tokens + sources].reshape(-1).astype(jnp.int32)
    source_rows = gather_plane(swap_places(encoded[0])).reshape(-1, width)
    out_grad = swap_places(cotangent[0])
    out_grad = jnp.concatenate([out_grad, flip_model(out_grad, 2)], axis=0).astype(WIDE)

    line_ids = line ^ jnp.arange(lines, dtype=jnp.int32)[:, None]
    model_ids = own ^ jnp.array([0, 2, 1, 3], jnp.int32)[None, :]
    starts = (model_ids * lines + line_ids) * tokens
    places = (starts[:, :, None] + jnp.arange(tokens, dtype=jnp.int32)).reshape(-1)

    qkv_low = self_qkv.astype(LOW).reshape(local, 3, model, local)
    cq_low = cross_q.astype(LOW).reshape(local, model, local)
    ckv_low = cross_kv.astype(LOW).reshape(local, 2, model, local)
    fi_low = ffn_in.astype(LOW).reshape(local, model, -1)

    def qkv_block(k):
        piece = lax.dynamic_index_in_dim(qkv_low, own ^ k, 2, keepdims=False)
        return piece.reshape(local, -1)

    def rest_block(k):
        piece_q = lax.dynamic_index_in_dim(cq_low, own ^ k, 1, keepdims=False)
        piece_kv = lax.dynamic_index_in_dim(ckv_low, own ^ k, 2, keepdims=False)
        piece_fi = lax.dynamic_index_in_dim(fi_low, own ^ k, 1, keepdims=False)
        return jnp.concatenate([piece_q, piece_kv.reshape(local, -1), piece_fi], axis=1)

    w_qkv = jnp.concatenate(to_columns([qkv_block(k) for k in range(4)], own), axis=0)
    w_rest = jnp.concatenate(to_columns([rest_block(k) for k in range(4)], own), axis=0)
    w_cq = w_rest[:, :local]
    w_ckv = w_rest[:, local : 3 * local]
    w_fi = w_rest[:, 3 * local :]
    w_so = self_out.astype(LOW)
    w_co = cross_out.astype(LOW)
    w_fo = ffn_out.astype(LOW)
    small = jnp.concatenate([biases, gains], axis=0).astype(LOW)
    small_all = lax.all_gather(small, "fsdp", axis=1, tiled=True).astype(WIDE)
    bias = small_all[:10]
    gain = small_all[10:]
    bias_own = biases.astype(LOW).astype(WIDE)
    inner_bias = ffn_bias.astype(LOW).astype(WIDE)

    queries = ((mm(inputs[:rows], w_qkv[:, :local]) + bias_own[3]) * scale).astype(LOW)
    pair = mm(inputs, w_qkv[:, local:])
    keys = pair[:, :local].astype(LOW)
    values = (pair[:, local:] + bias_own[4]).astype(LOW)
    allowed = (segments[:rows, None] == segments[None, :]) & (places[None, :] <= places[:rows, None])
    attended, self_probs = attend(queries, keys, values, allowed)
    residual = inputs[:half].astype(WIDE)
    first_sum = residual + tensor_sum(mm(attended, w_so)) + bias[5]
    first_normal, first_rate = normalize(first_sum)
    first = first_normal * gain[0] + bias[0]
    first_low = spread_rows(first.astype(LOW))

    cross_queries = ((mm(first_low, w_cq) + bias_own[6]) * scale).astype(LOW)
    source_pair = mm(source_rows, w_ckv)
    source_keys = source_pair[:, :local].astype(LOW)
    source_values = (source_pair[:, local:] + bias_own[7]).astype(LOW)
    cross_allowed = segments[:rows, None] == source_segments[None, :]
    crossed, cross_probs = attend(cross_queries, source_keys, source_values, cross_allowed)
    second_sum = first + tensor_sum(mm(crossed, w_co)) + bias[8]
    second_normal, second_rate = normalize(second_sum)
    second = second_normal * gain[1] + bias[1]
    second_low = spread_rows(second.astype(LOW))

    inner_pre = mm(second_low, w_fi) + inner_bias
    bell = 0.5 * (1.0 + lax.erf(inner_pre * (0.5**0.5)))
    activated = (inner_pre * bell).astype(LOW)
    third_sum = second + tensor_sum(mm(activated, w_fo)) + bias[9]
    third_normal, third_rate = normalize(third_sum)
    result = third_normal[:tokens] * gain[2] + bias[2]
    output = swap_places(result.astype(LOW))[None]

    third_grad = normalize_back(out_grad, third_normal, third_rate, gain[2])
    ffn_grad = spread_rows(third_grad.astype(LOW))
    slope = bell + inner_pre * jnp.exp(-0.5 * inner_pre * inner_pre) * 0.3989422804014327
    inner_grad = (mm_nt(ffn_grad, w_fo) * slope).astype(LOW)
    second_grad = third_grad + tensor_sum(mm_nt(inner_grad, w_fi))
    d_fo = mm_tn(activated, ffn_grad)
    d_fi = mm_tn(second_low, inner_grad)
    g_fo = sum_ctx(d_fo[None], ctx_index, False, own)
    g_fi = sum_ctx(d_fi.reshape(model, local, -1), ctx_index, True, own)

    sum_two_grad = normalize_back(second_grad, second_normal, second_rate, gain[1])
    cross_branch = spread_rows(sum_two_grad.astype(LOW))
    crossed_grad = mm_nt(cross_branch, w_co).astype(LOW)
    cross_query_grad, source_grad = attend_back(
        cross_queries, source_keys, source_values, cross_probs, crossed_grad
    )
    cross_query_pre = (cross_query_grad.astype(LOW).astype(WIDE) * scale).astype(LOW)
    first_grad = sum_two_grad + tensor_sum(mm_nt(cross_query_pre, w_cq))
    d_co = mm_tn(crossed, cross_branch)
    d_cq = mm_tn(first_low, cross_query_pre)
    source_low = source_grad.astype(LOW)
    d_ckv = mm_tn(source_rows, source_low)
    source_own = sum_lines(source_grad.reshape(lines, 4 * sources, 2 * local)).astype(LOW)
    encoded_part = mm_nt(source_own, w_ckv)
    encoded_part = encoded_part[: 2 * sources] + flip_model(
        encoded_part[2 * sources :].astype(LOW), 1
    ).astype(WIDE)
    encoded_part = encoded_part[:sources] + flip_model(
        encoded_part[sources:].astype(LOW), 2
    ).astype(WIDE)
    encoded_grad = swap_places(encoded_part.astype(LOW)).astype(WIDE)[None]

    sum_one_grad = normalize_back(first_grad, first_normal, first_rate, gain[0])
    self_branch = spread_rows(sum_one_grad.astype(LOW))
    attended_grad = mm_nt(self_branch, w_so).astype(LOW)
    self_query_grad, pair_grad = attend_back(queries, keys, values, self_probs, attended_grad)
    self_query_pre = (self_query_grad.astype(LOW).astype(WIDE) * scale).astype(LOW)
    d_so = mm_tn(attended, self_branch)
    pair_low = pair_grad.astype(LOW)
    d_q = mm_tn(inputs[:rows], self_query_pre)
    d_kv = mm_tn(inputs, pair_low)
    d_qkv = jnp.concatenate([d_q, d_kv], axis=1)
    pair_own = sum_lines(pair_grad.reshape(lines, rows, 2 * local)).astype(LOW)
    projected_grad = jnp.concatenate([self_query_pre, pair_own], axis=1)
    input_part = mm_nt(projected_grad, w_qkv)
    input_part = input_part[:half] + flip_model(input_part[half:].astype(LOW), 1).astype(WIDE)
    input_part = input_part[:tokens] + flip_model(input_part[tokens:].astype(LOW), 2).astype(WIDE)
    input_grad = sum_one_grad[:tokens] + input_part
    hidden_grad = swap_places(input_grad.astype(LOW)).astype(WIDE)[None]

    row_kinds = jnp.concatenate([d_so, d_co], axis=1)[None]
    g_row = sum_ctx(row_kinds, ctx_index, False, own)
    column_kinds = jnp.concatenate([d_cq, d_ckv], axis=1).reshape(model, local, -1)
    g_col = sum_ctx(column_kinds, ctx_index, True, own).reshape(local, model, 3, local)
    g_qkv = sum_ctx(d_qkv.reshape(model, local, -1), ctx_index, True, own)
    g_qkv = g_qkv.reshape(local, model, 3, local).transpose(0, 2, 1, 3).reshape(local, 3 * width)
    g_so = g_row[:, :width]
    g_co = g_row[:, width:]
    g_cq = g_col[:, :, 0].reshape(local, width)
    g_ckv = g_col[:, :, 1:].transpose(0, 2, 1, 3).reshape(local, 2 * width)

    def columns(value):
        return jnp.sum(value.astype(WIDE), axis=0)

    wide_rows = jnp.stack(
        [
            columns(first_grad[:tokens]),
            columns(second_grad[:tokens]),
            columns(out_grad[:tokens]),
            columns((first_grad * first_normal)[:tokens]),
            columns((second_grad * second_normal)[:tokens]),
            columns((out_grad * third_normal)[:tokens]),
            columns(self_branch[:tokens]),
            columns(cross_branch[:tokens]),
            columns(ffn_grad[:tokens]),
        ]
    )
    for bit in (1, 2):
        wide_rows = wide_rows + flip_model(wide_rows, bit)
    wide_rows = lax.dynamic_slice_in_dim(wide_rows, own * local, local, axis=1)
    own_rows = jnp.stack(
        [
            columns(self_query_pre),
            columns(pair_low[:, local:]),
            columns(cross_query_pre),
            columns(source_low[:, local:]),
        ]
    )
    vectors = jnp.concatenate([wide_rows, own_rows, columns(inner_grad).reshape(-1, local)], axis=0)
    for bit in ctx_bits():
        vectors = vectors + flip_ctx(vectors, bit)
    d_bias = jnp.stack([vectors[i] for i in (0, 1, 2, 9, 10, 6, 11, 12, 7, 8)])
    d_gain = vectors[3:6]
    d_inner = vectors[13:].reshape(-1)
    return (
        output,
        hidden_grad,
        encoded_grad,
        g_qkv,
        g_so,
        g_cq,
        g_ckv,
        g_co,
        g_fi.reshape(local, -1),
        g_fo,
        d_bias,
        d_gain,
        d_inner,
    )


def solution(mesh):
    whole = P("fsdp", "ctx", None)
    matrix = P("fsdp", None)
    ids = P("fsdp", "ctx")
    table = P(None, "fsdp")
    return jax.shard_map(
        body,
        mesh=mesh,
        in_specs=(whole, whole, whole, ids, ids) + (matrix,) * 7 + (table, table, P("fsdp")),
        out_specs=(whole,) * 3 + (matrix,) * 7 + (table, table, P("fsdp")),
        check_vma=False,
    )
```

```python
import jax
import jax.numpy as jnp
from jax import lax
from jax.experimental import pallas as pl
from jax.experimental.pallas import tpu as pltpu
from jax.sharding import PartitionSpec as P

H = 12
HD = 64
EPSILON = 1e-05
FLOOR_SCORE = -1e30
SCALE = float(HD) ** (-0.5)
LOW = jnp.bfloat16
WIDE = jnp.float32


def mm(left, right):
    return jnp.dot(left, right, preferred_element_type=WIDE)


def mm_tn(left, right):
    return lax.dot_general(left, right, (((0,), (0,)), ((), ())), preferred_element_type=WIDE)


def mm_nt(left, right):
    return lax.dot_general(left, right, (((1,), (1,)), ((), ())), preferred_element_type=WIDE)


def flip_model(value, bit):
    count = lax.axis_size("fsdp")
    return lax.ppermute(value, "fsdp", [(i, i ^ bit) for i in range(count)])


def flip_ctx(value, bit):
    count = lax.axis_size("ctx")
    return lax.ppermute(value, "ctx", [(i, i ^ bit) for i in range(count)])


def swap_places(value):
    model = lax.axis_size("fsdp")
    ctx = lax.axis_size("ctx")
    lines = ctx // model
    route = []
    for f in range(model):
        for z in range(model):
            for r in range(lines):
                route.append((f * ctx + z * lines + r, z * ctx + f * lines + r))
    return lax.ppermute(value, ("fsdp", "ctx"), route)


def powers(limit):
    bits = []
    bit = 1
    while bit < limit:
        bits.append(bit)
        bit *= 2
    return bits


def line_bits():
    return powers(lax.axis_size("ctx") // lax.axis_size("fsdp"))


def after(value, *others):
    return lax.optimization_barrier((value,) + others)[0]


def shape(dims, kind):
    return jax.ShapeDtypeStruct(tuple(dims), kind)


def cost(flops, *arrays):
    count = 0
    for array in arrays:
        count += array.size * array.dtype.itemsize
    return pl.CostEstimate(flops=flops, transcendentals=0, bytes_accessed=count)


def call(kernel, outs, spot, operands, flops=0, scratch=(), limit=12, piped=False):
    many = isinstance(outs, tuple)
    listed = outs if many else (outs,)
    if piped:
        place = lambda value: pl.BlockSpec(value.shape, lambda i, spot: (0,) * len(value.shape))
        spec = dict(
            grid_spec=pltpu.PrefetchScalarGridSpec(
                num_scalar_prefetch=1,
                grid=(1,),
                in_specs=[place(value) for value in operands],
                out_specs=tuple(place(value) for value in listed) if many else place(outs),
                scratch_shapes=list(scratch),
            )
        )
        limit = limit + 12
    else:
        place = pl.BlockSpec(memory_space=pltpu.VMEM)
        spec = dict(
            in_specs=[pl.BlockSpec(memory_space=pltpu.SMEM)] + [place] * len(operands),
            out_specs=tuple(place for _ in listed) if many else place,
            scratch_shapes=list(scratch),
        )
    return pl.pallas_call(
        kernel,
        out_shape=outs,
        cost_estimate=cost(flops, *operands, *listed),
        compiler_params=pltpu.CompilerParams(vmem_limit_bytes=limit << 20),
        **spec,
    )(spot, *operands)


def prepare_qkv(spot, weight, small):
    rows = weight.shape[0]

    def kernel(spot_ref, w_ref, small_ref, own_ref, near_ref, far_ref, all_ref):
        me = spot_ref[0]
        side = spot_ref[2]
        small = small_ref[...].astype(LOW)
        tail = jnp.zeros((16, 2 * rows), LOW)
        for d in range(4):
            for p in range(3):
                piece = w_ref[:, p * 4 * rows + d * rows : p * 4 * rows + (d + 1) * rows]
                all_ref[me ^ d, :, p * rows : (p + 1) * rows] = piece.astype(LOW)
        own_ref[:rows] = all_ref[0]
        near_ref[:rows] = all_ref[1]
        far_ref[:rows] = all_ref[2 + side]
        for ref in (own_ref, near_ref, far_ref):
            ref[rows:, :rows] = small
            ref[rows:, rows:] = tail

    piece = (rows + 16, 3 * rows)
    return call(
        kernel,
        (shape(piece, LOW),) * 3,
        spot,
        (weight, small),
        scratch=[pltpu.VMEM((4, rows, 3 * rows), LOW)],
    )


def prepare_rest(spot, cross_q, cross_kv, ffn_in, self_out, cross_out, ffn_out):
    rows = cross_q.shape[0]
    wide = ffn_in.shape[1] // 4
    piece = (rows, 3 * rows + wide)

    def kernel(spot_ref, q_ref, kv_ref, fi_ref, so_ref, co_ref, fo_ref, *outs):
        own_ref, near_ref, far_ref, so_out, co_out, fo_out, all_ref = outs
        me = spot_ref[0]
        side = spot_ref[2]
        for d in range(4):
            all_ref[me ^ d, :, :rows] = q_ref[:, d * rows : (d + 1) * rows].astype(LOW)
            for p in range(2):
                part = kv_ref[:, (p * 4 + d) * rows : (p * 4 + d + 1) * rows]
                all_ref[me ^ d, :, (1 + p) * rows : (2 + p) * rows] = part.astype(LOW)
            all_ref[me ^ d, :, 3 * rows :] = fi_ref[:, d * wide : (d + 1) * wide].astype(LOW)
        own_ref[...] = all_ref[0]
        near_ref[...] = all_ref[1]
        far_ref[...] = all_ref[2 + side]
        so_out[...] = so_ref[...].astype(LOW)
        co_out[...] = co_ref[...].astype(LOW)
        fo_out[...] = fo_ref[...].astype(LOW)

    return call(
        kernel,
        (shape(piece, LOW),) * 3
        + (shape(self_out.shape, LOW), shape(cross_out.shape, LOW), shape(ffn_out.shape, LOW)),
        spot,
        (cross_q, cross_kv, ffn_in, self_out, cross_out, ffn_out),
        scratch=[pltpu.VMEM((4,) + piece, LOW)],
        limit=16,
        piped=True,
    )


def ordered_blocks(spot_ref, refs, pair_ref):
    side = spot_ref[2]
    pair_ref[0, side] = refs[2][...]
    pair_ref[0, 1 - side] = refs[3][...]
    pair_ref[1, side] = refs[4][...]
    pair_ref[1, 1 - side] = refs[5][...]
    return refs[0][...], refs[1][...], pair_ref[0, 0], pair_ref[1, 1]


def arrange_rest(spot, blocks, source_rows, table):
    rows = blocks[0].shape[0]
    wide = blocks[0].shape[1] - 3 * rows
    count, width = source_rows.shape

    def kernel(spot_ref, *refs):
        x_ref, table_ref, q_ref, kv_ref, fi_ref, keys_ref, values_ref, rel_ref, pair_ref = refs[6:]
        me = spot_ref[0]
        parts = ordered_blocks(spot_ref, refs[:6], pair_ref)
        for k in range(4):
            start = pl.multiple_of((me ^ k) * rows, 64)
            q_ref[pl.ds(start, rows), :] = parts[k][:, :rows]
            kv_ref[pl.ds(start, rows), :] = parts[k][:, rows : 3 * rows]
            fi_ref[pl.ds(start, rows), :] = parts[k][:, 3 * rows :]
        for j in range(4):
            rel_ref[j] = table_ref[:, j * rows : (j + 1) * rows]
        shift = rel_ref[me][7:8]
        out = mm(x_ref[...], kv_ref[...])
        keys_ref[...] = out[:, :rows].astype(LOW)
        values_ref[...] = (out[:, rows:] + shift).astype(LOW)

    return call(
        kernel,
        (
            shape((4 * rows, rows), LOW),
            shape((4 * rows, 2 * rows), LOW),
            shape((4 * rows, wide), LOW),
            shape((count, rows), LOW),
            shape((count, rows), LOW),
        ),
        spot,
        tuple(blocks) + (source_rows, table),
        flops=4 * count * width * rows,
        scratch=[pltpu.VMEM((4, 16, rows), WIDE), pltpu.VMEM((2, 2) + blocks[0].shape, LOW)],
        limit=16,
    )


def project(spot, near_rows, far_rows, blocks, tokens, sources):
    lines = near_rows.shape[0]
    width = near_rows.shape[-1]
    local = width // 4
    span = near_rows.shape[2]
    rows = 4 * tokens

    def kernel(spot_ref, a_ref, b_ref, *refs):
        x_ref, e_ref, q_ref, k_ref, v_ref, wq_ref, wkv_ref, table_ref, *outs = refs[6:]
        marks_ref, emarks_ref, rel_ref, w_ref, pair_ref = outs
        me = spot_ref[0]

        @pl.when(pl.program_id(0) == 0)
        def _():
            parts = ordered_blocks(spot_ref, refs[:6], pair_ref)
            for k in range(4):
                start = pl.multiple_of((me ^ k) * local, 64)
                w_ref[pl.ds(start, local), :] = parts[k][:local]
                rel_ref[k] = parts[k][local:, :local].astype(WIDE)
            for j in range(4):
                table_ref[:, j * local : (j + 1) * local] = rel_ref[me ^ j]
            wq_ref[...] = w_ref[:, :local]
            wkv_ref[...] = w_ref[:, local:]

        lane = lax.broadcasted_iota(jnp.int32, (1, 128), 1)
        emarks = jnp.zeros((1, 128), WIDE)
        for kc, ref in enumerate((a_ref, b_ref)):
            for kx in range(2):
                at = 2 * kc + kx
                start = at * tokens
                x_ref[start : start + tokens, :] = ref[0, kx, :tokens, :]
                e_ref[at * sources : (at + 1) * sources, :] = ref[0, kx, tokens : tokens + sources, :]
                marks = ref[0, kx, tokens + sources : tokens + sources + 16, :256].astype(WIDE)
                marks_ref[:, start : start + tokens] = marks[0:1, :tokens]
                moved = pltpu.roll(marks[:8, 128:], at * sources, 1)[0:1]
                emarks = emarks + jnp.where((lane // sources) == at, moved, 0.0)
        emarks_ref[...] = emarks
        own_small = rel_ref[0]
        out = mm(x_ref[...], w_ref[...])
        k_ref[...] = out[:, local : 2 * local].astype(LOW)
        v_ref[...] = (out[:, 2 * local :] + own_small[4:5]).astype(LOW)

        @pl.when(pl.program_id(0) == 0)
        def _():
            q_ref[...] = ((out[:, :local] + own_small[3:4]) * SCALE).astype(LOW)

    full = lambda *dims: pl.BlockSpec(dims, lambda i, spot: (0,) * len(dims))
    band = lambda w: pl.BlockSpec((rows, w), lambda i, spot: (i, 0))
    part = pl.BlockSpec((1, 2, span, width), lambda i, spot: (i, 0, 0, 0))
    piece = (local + 16, 3 * local)
    outs = (
        shape((lines * rows, width), LOW),
        shape((lines * 4 * sources, width), LOW),
        shape((rows, local), LOW),
        shape((lines * rows, local), LOW),
        shape((lines * rows, local), LOW),
        shape((width, local), LOW),
        shape((width, 2 * local), LOW),
        shape((16, width), WIDE),
        shape((1, lines * rows), WIDE),
        shape((1, lines * 4 * sources), WIDE),
    )
    operands = (near_rows, far_rows) + tuple(blocks)
    return pl.pallas_call(
        kernel,
        out_shape=outs,
        grid_spec=pltpu.PrefetchScalarGridSpec(
            num_scalar_prefetch=1,
            grid=(lines,),
            in_specs=[part, part] + [full(*piece)] * 6,
            out_specs=(
                band(width),
                pl.BlockSpec((4 * sources, width), lambda i, spot: (i, 0)),
                full(rows, local),
                band(local),
                band(local),
                full(width, local),
                full(width, 2 * local),
                full(16, width),
                pl.BlockSpec((1, rows), lambda i, spot: (0, i)),
                pl.BlockSpec((1, 4 * sources), lambda i, spot: (0, i)),
            ),
            scratch_shapes=[
                pltpu.VMEM((4, 16, local), WIDE),
                pltpu.VMEM((width, 3 * local), LOW),
                pltpu.VMEM((2, 2) + piece, LOW),
            ],
        ),
        cost_estimate=cost(6 * lines * rows * width * local, *operands, *outs),
        compiler_params=pltpu.CompilerParams(vmem_limit_bytes=20 << 20),
    )(spot, *operands)


def block_start(spot_ref, index, tokens, lines):
    me = spot_ref[0]
    line = spot_ref[3]
    kr, kc, kx = index // 4, (index // 2) % 2, index % 2
    return ((me ^ (kc + 2 * kx)) * lines + (line ^ kr)) * tokens


def upright(row):
    return jnp.transpose(jnp.broadcast_to(row, (128, row.shape[1])))


def self_floor(spot_ref, marks_ref, query_blocks, tokens, turned):
    blocks = marks_ref.shape[1] // tokens
    lines = blocks // 4
    down = lax.broadcasted_iota(jnp.int32, (tokens, tokens), 0)
    right = lax.broadcasted_iota(jnp.int32, (tokens, tokens), 1)
    outer, inner = (range(blocks), query_blocks) if turned else (query_blocks, range(blocks))
    table = []
    for i in outer:
        tall = upright(marks_ref[:, i * tokens : (i + 1) * tokens])
        line = []
        for j in inner:
            flat = marks_ref[:, j * tokens : (j + 1) * tokens]
            gap = block_start(spot_ref, j, tokens, lines) - block_start(spot_ref, i, tokens, lines)
            ahead = (right + gap) - down
            near = (ahead >= 0) if turned else (ahead <= 0)
            line.append(jnp.where((tall == flat) & near, 0.0, FLOOR_SCORE))
        table.append(jnp.concatenate(line, axis=1))
    return jnp.concatenate(table, axis=0)


def head_lanes(value, head):
    lane = lax.broadcasted_iota(jnp.int32, (1, value.shape[1]), 1) // HD
    return jnp.where(lane == head, value, jnp.zeros_like(value))


def attend_rows(queries, keys, values, floor):
    heads = queries.shape[1] // HD
    total = None
    for h in range(heads):
        scores = mm_nt(head_lanes(queries, h), keys) + floor
        top = jnp.max(scores, axis=1, keepdims=True)
        weights = jnp.exp(scores - top)
        prob = weights / jnp.sum(weights, axis=1, keepdims=True)
        part = head_lanes(mm(prob.astype(LOW), values), h)
        total = part if total is None else total + part
    return total.astype(LOW)


def attend_rows_back(queries, keys, values, grads, floor):
    heads = queries.shape[1] // HD
    query_grad = key_grad = value_grad = None
    for h in range(heads):
        own_queries = head_lanes(queries, h)
        own_grads = head_lanes(grads, h)
        scores = mm_nt(keys, own_queries) + floor
        top = jnp.max(scores, axis=0, keepdims=True)
        weights = jnp.exp(scores - top)
        prob = weights / jnp.sum(weights, axis=0, keepdims=True)
        prob_grad = mm_nt(values, own_grads)
        inner = jnp.sum(prob * prob_grad, axis=0, keepdims=True)
        score_grad = (prob * (prob_grad - inner)).astype(LOW)
        part_q = head_lanes(mm_tn(score_grad, keys), h)
        part_k = mm(score_grad, own_queries)
        part_v = mm(prob.astype(LOW), own_grads)
        query_grad = part_q if query_grad is None else query_grad + part_q
        key_grad = part_k if key_grad is None else key_grad + part_k
        value_grad = part_v if value_grad is None else value_grad + part_v
    return query_grad, key_grad, value_grad


def block_rows(keys):
    return 256 if keys <= 1024 else 128


def self_forward(spot, marks, queries, keys, values, weight, tokens):
    rows, local = queries.shape
    width = weight.shape[1]
    size = block_rows(keys.shape[0])

    def kernel(spot_ref, marks_ref, q_ref, k_ref, v_ref, w_ref, o_ref, keep_ref, send_ref):
        for begin in range(0, rows, size):
            blocks = range(begin // tokens, (begin + size) // tokens)
            floor = self_floor(spot_ref, marks_ref, blocks, tokens, False)
            low = attend_rows(q_ref[begin : begin + size], k_ref[...], v_ref[...], floor)
            o_ref[begin : begin + size] = low
            part = mm(low, w_ref[...])
            if begin < rows // 2:
                keep_ref[begin : begin + size] = part
            else:
                send_ref[begin - rows // 2 : begin - rows // 2 + size] = part.astype(LOW)

    return call(
        kernel,
        (shape((rows, local), LOW), shape((rows // 2, width), WIDE), shape((rows // 2, width), LOW)),
        spot,
        (marks, queries, keys, values, weight),
        flops=4 * rows * keys.size + 2 * rows * weight.size,
        limit=20,
    )


def plain_floor(marks, places, rows):
    same = marks.reshape(-1)[:rows, None] == marks
    return jnp.where(same & (places[None, :] <= places[:rows, None]), 0.0, FLOOR_SCORE)


def plain_forward(marks, places, queries, keys, values, weight):
    rows = queries.shape[0]
    low = attend_rows(queries, keys, values, plain_floor(marks, places, rows))
    part = mm(low, weight)
    return low, part[: rows // 2], part[rows // 2 :].astype(LOW)


def plain_back(marks, places, low, other, w_so, queries, keys, values):
    grads = mm_nt(jnp.concatenate([low, other], axis=0), w_so).astype(LOW)
    floor = plain_floor(marks, places, queries.shape[0])
    dq, dk, dv = attend_rows_back(queries, keys, values, grads, floor.T)
    pre = (dq.astype(LOW).astype(WIDE) * SCALE).astype(LOW)
    sums = jnp.concatenate(column_rows(pre, dv), axis=0)
    return pre, jnp.concatenate([dk, dv], axis=1).astype(LOW), sums


def norm_rows(values):
    center = values - jnp.mean(values, axis=-1, keepdims=True)
    spread = jnp.mean(center * center, axis=-1, keepdims=True)
    rate = lax.rsqrt(spread + EPSILON)
    return center * rate, rate


def turned_halves(ref):
    half = ref.shape[0] // 2
    return jnp.concatenate([ref[half:], ref[:half]], axis=0).astype(WIDE)


def residual_norm(residual, mine, other, table, bias_row, norm_row):
    rows, width = mine.shape

    def kernel(spot_ref, r_ref, mine_ref, other_ref, table_ref, h_ref, low_ref, n_ref, rate_ref):
        total = r_ref[:rows].astype(WIDE) + mine_ref[...] + turned_halves(other_ref)
        normal, rate = norm_rows(total + table_ref[bias_row : bias_row + 1])
        gain = table_ref[10 + norm_row : 11 + norm_row]
        result = normal * gain + table_ref[norm_row : norm_row + 1]
        h_ref[...] = result
        low_ref[...] = result.astype(LOW)
        n_ref[...] = normal
        rate_ref[...] = rate

    return call(
        kernel,
        (
            shape((rows, width), WIDE),
            shape((rows, width), LOW),
            shape((rows, width), WIDE),
            shape((rows, 1), WIDE),
        ),
        jnp.zeros((1,), jnp.int32),
        (residual, mine, other, table),
    )


def cross_forward(spot, marks, emarks, low, other, w_cq, keys, values, w_co, small, tokens):
    half, width = low.shape
    local = w_cq.shape[1]

    def kernel(spot_ref, marks_ref, emarks_ref, a_ref, b_ref, w_ref, k_ref, v_ref, o_ref, small_ref, *outs):
        q_out, c_out, keep_ref, send_ref = outs
        for place, ref in enumerate((a_ref, b_ref)):
            at = slice(place * half, (place + 1) * half)
            low = ((mm(ref[...], w_ref[...]) + small_ref[6:7]) * SCALE).astype(LOW)
            q_out[at] = low
            tall = []
            for i in range(place * half // tokens, (place + 1) * half // tokens):
                tall.append(upright(marks_ref[:, i * tokens : (i + 1) * tokens])[:, :1])
            tall = jnp.concatenate(tall, axis=0)
            floor = jnp.where(tall == emarks_ref[...], 0.0, FLOOR_SCORE)
            crossed = attend_rows(low, k_ref[...], v_ref[...], floor)
            c_out[at] = crossed
            part = mm(crossed, o_ref[...])
            if place == 0:
                keep_ref[...] = part
            else:
                send_ref[...] = part.astype(LOW)

    return call(
        kernel,
        (
            shape((2 * half, local), LOW),
            shape((2 * half, local), LOW),
            shape((half, width), WIDE),
            shape((half, width), LOW),
        ),
        spot,
        (marks, emarks, low, other, w_cq, keys, values, w_co, small),
        flops=8 * half * width * local,
        limit=16,
    )


def ffn_forward(low, other, w_fi, w_fo, shift):
    half, width = low.shape
    wide = w_fi.shape[1]

    def kernel(spot_ref, a_ref, b_ref, w_ref, o_ref, shift_ref, g_ref, slope_ref, keep_ref, send_ref):
        for place, ref in enumerate((a_ref, b_ref)):
            at = slice(place * half, (place + 1) * half)
            pre = mm(ref[...], w_ref[...]) + shift_ref[...]
            bell = 0.5 * (1.0 + lax.erf(pre * (0.5**0.5)))
            act = (pre * bell).astype(LOW)
            g_ref[at] = act
            slope_ref[at] = bell + pre * jnp.exp(-0.5 * pre * pre) * 0.3989422804014327
            part = mm(act, o_ref[...])
            if place == 0:
                keep_ref[...] = part
            else:
                send_ref[...] = part.astype(LOW)

    return call(
        kernel,
        (
            shape((2 * half, wide), LOW),
            shape((2 * half, wide), WIDE),
            shape((half, width), WIDE),
            shape((half, width), LOW),
        ),
        jnp.zeros((1,), jnp.int32),
        (low, other, w_fi, w_fo, shift),
        flops=8 * half * width * wide,
    )


def norm_back(grad, normal, rate, gain):
    up = grad * gain
    mean_up = jnp.mean(up, axis=-1, keepdims=True)
    mean_both = jnp.mean(up * normal, axis=-1, keepdims=True)
    return rate * (up - mean_up - normal * mean_both)


def column_rows(*values):
    rows = [jnp.sum(value.astype(WIDE), axis=0, keepdims=True) for value in values]
    return rows


def turn_around(residual, mine, other, table, own_grad, other_grad, tokens):
    rows, width = mine.shape

    def kernel(spot_ref, r_ref, mine_ref, other_ref, table_ref, a_ref, b_ref, out_ref, d_ref, low_ref, sum_ref):
        total = r_ref[...] + mine_ref[...] + turned_halves(other_ref) + table_ref[9:10]
        normal, rate = norm_rows(total)
        gain = table_ref[12:13]
        out_ref[...] = (normal[:tokens] * gain + table_ref[2:3]).astype(LOW)
        grad = jnp.concatenate([a_ref[:tokens], b_ref[:tokens]], axis=0).astype(WIDE)
        back = norm_back(grad, normal, rate, gain)
        low = back.astype(LOW)
        d_ref[...] = back
        low_ref[...] = low
        rows = column_rows(grad[:tokens], (grad * normal)[:tokens], low[:tokens])
        for i in range(3):
            sum_ref[i : i + 1] = rows[i]

    return call(
        kernel,
        (
            shape((tokens, width), LOW),
            shape((rows, width), WIDE),
            shape((rows, width), LOW),
            shape((3, width), WIDE),
        ),
        jnp.zeros((1,), jnp.int32),
        (residual, mine, other, table, own_grad, other_grad),
        piped=True,
    )


def residual_back(previous, mine, other, normal, rate, table, norm_row, tokens):
    rows, width = mine.shape

    def kernel(spot_ref, p_ref, mine_ref, other_ref, n_ref, rate_ref, table_ref, d_ref, low_ref, sum_ref):
        grad = p_ref[...] + mine_ref[...] + turned_halves(other_ref)
        normal = n_ref[...]
        back = norm_back(grad, normal, rate_ref[...], table_ref[10 + norm_row : 11 + norm_row])
        low = back.astype(LOW)
        d_ref[...] = back
        low_ref[...] = low
        rows = column_rows(grad[:tokens], (grad * normal)[:tokens], low[:tokens])
        for i in range(3):
            sum_ref[i : i + 1] = rows[i]

    return call(
        kernel,
        (shape((rows, width), WIDE), shape((rows, width), LOW), shape((3, width), WIDE)),
        jnp.zeros((1,), jnp.int32),
        (previous, mine, other, normal, rate, table),
        piped=True,
    )


def ffn_back(low, other, w_fo, w_fi, slope):
    half, width = low.shape
    wide = w_fi.shape[1]

    def kernel(spot_ref, a_ref, b_ref, o_ref, w_ref, slope_ref, u_ref, keep_ref, send_ref, sum_ref):
        total = None
        for place, ref in enumerate((a_ref, b_ref)):
            at = slice(place * half, (place + 1) * half)
            inner = (mm_nt(ref[...], o_ref[...]) * slope_ref[at]).astype(LOW)
            u_ref[at] = inner
            row = column_rows(inner)[0]
            total = row if total is None else total + row
            part = mm_nt(inner, w_ref[...])
            if place == 0:
                keep_ref[...] = part
            else:
                send_ref[...] = part.astype(LOW)
        sum_ref[...] = total

    return call(
        kernel,
        (
            shape((2 * half, wide), LOW),
            shape((half, width), WIDE),
            shape((half, width), LOW),
            shape((1, wide), WIDE),
        ),
        jnp.zeros((1,), jnp.int32),
        (low, other, w_fo, w_fi, slope),
        flops=8 * half * width * wide,
        piped=True,
    )


def cross_back(spot, marks, emarks, low, other, w_co, queries, keys, values, w_cq, tokens):
    half, width = low.shape
    count, local = keys.shape

    def kernel(spot_ref, marks_ref, emarks_ref, a_ref, b_ref, co_ref, q_ref, k_ref, v_ref, cq_ref, *outs):
        dq_ref, dkv_ref, keep_ref, send_ref, sum_ref = outs
        key_grad = value_grad = None
        tall = []
        for i in range(count // 128):
            tall.append(upright(emarks_ref[:, i * 128 : (i + 1) * 128])[:, :1])
        tall = jnp.concatenate(tall, axis=0)
        totals = None
        for place, ref in enumerate((a_ref, b_ref)):
            at = slice(place * half, (place + 1) * half)
            grads = mm_nt(ref[...], co_ref[...]).astype(LOW)
            floor = jnp.where(tall == marks_ref[:, at], 0.0, FLOOR_SCORE)
            dq, dk, dv = attend_rows_back(q_ref[at], k_ref[...], v_ref[...], grads, floor)
            pre = (dq.astype(LOW).astype(WIDE) * SCALE).astype(LOW)
            dq_ref[at] = pre
            key_grad = dk if key_grad is None else key_grad + dk
            value_grad = dv if value_grad is None else value_grad + dv
            row = column_rows(pre)[0]
            totals = row if totals is None else totals + row
            part = mm_nt(pre, cq_ref[...])
            if place == 0:
                keep_ref[...] = part
            else:
                send_ref[...] = part.astype(LOW)
        dkv_ref[:, :local] = key_grad.astype(LOW)
        dkv_ref[:, local:] = value_grad.astype(LOW)
        sum_ref[0:1] = totals
        sum_ref[1:2] = column_rows(value_grad)[0]

    return call(
        kernel,
        (
            shape((2 * half, local), LOW),
            shape((count, 2 * local), LOW),
            shape((half, width), WIDE),
            shape((half, width), LOW),
            shape((2, local), WIDE),
        ),
        spot,
        (marks, emarks, low, other, w_co, queries, keys, values, w_cq),
        flops=8 * half * width * local,
        limit=16,
        piped=True,
    )


def self_back(spot, marks, low, other, w_so, queries, keys, values, tokens):
    half, width = low.shape
    count, local = keys.shape
    rows = 2 * half
    size = block_rows(count)

    def kernel(spot_ref, marks_ref, a_ref, b_ref, so_ref, q_ref, k_ref, v_ref, dq_ref, dkv_ref, sum_ref, dk_ref, dv_ref):
        totals = None
        for begin in range(0, rows, size):
            source = a_ref if begin < half else b_ref
            local_at = begin % half
            grads = mm_nt(source[local_at : local_at + size], so_ref[...]).astype(LOW)
            blocks = range(begin // tokens, (begin + size) // tokens)
            floor = self_floor(spot_ref, marks_ref, blocks, tokens, True)
            at = slice(begin, begin + size)
            dq, dk, dv = attend_rows_back(q_ref[at], k_ref[...], v_ref[...], grads, floor)
            pre = (dq.astype(LOW).astype(WIDE) * SCALE).astype(LOW)
            dq_ref[at] = pre
            row = column_rows(pre)[0]
            totals = row if totals is None else totals + row
            if begin == 0:
                dk_ref[...] = dk
                dv_ref[...] = dv
            else:
                dk_ref[...] += dk
                dv_ref[...] += dv
        dkv_ref[:, :local] = dk_ref[...].astype(LOW)
        dkv_ref[:, local:] = dv_ref[...].astype(LOW)
        sum_ref[0:1] = totals
        sum_ref[1:2] = column_rows(dv_ref[...])[0]

    return call(
        kernel,
        (shape((rows, local), LOW), shape((count, 2 * local), LOW), shape((2, local), WIDE)),
        spot,
        (marks, low, other, w_so, queries, keys, values),
        flops=10 * rows * keys.size,
        scratch=[pltpu.VMEM((count, local), WIDE), pltpu.VMEM((count, local), WIDE)],
        limit=24,
        piped=True,
    )


def input_back(query_grad, pair_grad, w_q, w_kv):
    rows = query_grad.shape[0]
    width = w_q.shape[0]

    def kernel(spot_ref, q_ref, kv_ref, wq_ref, wkv_ref, keep_ref, send_ref):
        part = mm_nt(q_ref[...], wq_ref[...]) + mm_nt(kv_ref[...], wkv_ref[...])
        keep_ref[...] = part[: rows // 2]
        send_ref[...] = part[rows // 2 :].astype(LOW)

    return call(
        kernel,
        (shape((rows // 2, width), WIDE), shape((rows // 2, width), LOW)),
        jnp.zeros((1,), jnp.int32),
        (query_grad, pair_grad, w_q, w_kv),
        flops=2 * rows * (w_q.size + w_kv.size),
        piped=True,
    )


def produce_ffn(spot, activated, grad_low, grad_other, low, other, inner_grad):
    wide = activated.shape[1]
    half, width = grad_low.shape
    part = width // 16

    def kernel(spot_ref, a_ref, g0_ref, g1_ref, x0_ref, x1_ref, u_ref, *refs):
        outs, all_ref = refs[:4], refs[4]
        me = spot_ref[0]
        high = spot_ref[1]
        low = spot_ref[2]
        for place in range(2):
            if place == 0:
                result = mm_tn(a_ref[:half], g0_ref[...]) + mm_tn(a_ref[half:], g1_ref[...])
            else:
                result = mm_tn(x0_ref[...], u_ref[:half]) + mm_tn(x1_ref[...], u_ref[half:])
            for d in range(4):
                for z in range(2):
                    for y in range(2):
                        at = (4 * d + 2 * z + y) * part
                        piece = result[at : at + part]
                        if place == 0:
                            all_ref[low ^ y, high ^ z, d] = piece
                        else:
                            all_ref[high ^ z, low ^ y, me ^ d] = piece
            outs[2 * place][...] = all_ref[0]
            outs[2 * place + 1][...] = all_ref[1].astype(LOW)

    piece = (2, 4, part, width)
    return call(
        kernel,
        (shape(piece, WIDE), shape(piece, LOW)) * 2,
        spot,
        (activated, grad_low, grad_other, low, other, inner_grad),
        flops=8 * half * width * wide,
        scratch=[pltpu.VMEM((2,) + piece, WIDE)],
        limit=16,
        piped=True,
    )


def finish_ffn(spot, out_pieces, in_pieces):
    part, width = out_pieces[0].shape[1:]
    rows = 4 * part

    def kernel(spot_ref, oa_ref, ob_ref, oc_ref, ia_ref, ib_ref, ic_ref, fo_ref, fi_ref):
        me = spot_ref[0]
        high = spot_ref[1]
        low = spot_ref[2]
        for kz in range(2):
            for ky in range(2):
                quarter = ((kz ^ high) * 2 + (ky ^ low)) * part
                source = oc_ref.at[kz] if ky else (ob_ref if kz else oa_ref)
                for d in range(4):
                    row = pl.multiple_of(d * rows + quarter, 16)
                    fo_ref[pl.ds(row, part), :] = source[d].astype(WIDE)
                source = ic_ref.at[ky] if kz else (ib_ref if ky else ia_ref)
                row = pl.multiple_of(quarter, 16)
                for j in range(4):
                    fi_ref[pl.ds(row, part), j * width : (j + 1) * width] = source[me ^ j].astype(WIDE)

    return call(
        kernel,
        (shape((4 * rows, width), WIDE), shape((rows, 4 * width), WIDE)),
        spot,
        tuple(out_pieces) + tuple(in_pieces),
        limit=16,
        piped=True,
    )


def produce_mixed(spot, one_ins, one_grad, two_in, two_grad, heads, grad_low, grad_other):
    local = one_grad.shape[1]
    half, width = grad_low.shape
    part = local // 4
    count = len(one_ins)

    def kernel(spot_ref, *refs):
        a_refs, refs = refs[:count], refs[count:]
        ag_ref, b_ref, bg_ref, o_ref, g0_ref, g1_ref, keep_ref, send_ref, all_ref = refs
        me = spot_ref[0]
        high = spot_ref[1]
        low = spot_ref[2]
        if count == 2:
            one = mm_tn(a_refs[0][...], ag_ref[:half]) + mm_tn(a_refs[1][...], ag_ref[half:])
        else:
            one = mm_tn(a_refs[0][: 2 * half], ag_ref[...])
        two = mm_tn(b_ref[...], bg_ref[...])
        three = mm_tn(o_ref[:half], g0_ref[...]) + mm_tn(o_ref[half:], g1_ref[...])
        for z in range(2):
            for y in range(2):
                quarter = (2 * z + y) * part
                for d in range(4):
                    at = d * local + quarter
                    all_ref[low ^ y, high ^ z, me ^ d, :, :local] = one[at : at + part]
                    all_ref[low ^ y, high ^ z, me ^ d, :, local : 3 * local] = two[at : at + part]
                    piece = three[quarter : quarter + part, d * local : (d + 1) * local]
                    all_ref[low ^ y, high ^ z, d, :, 3 * local :] = piece
        keep_ref[...] = all_ref[0]
        send_ref[...] = all_ref[1].astype(LOW)

    operands = tuple(one_ins) + (one_grad, two_in, two_grad, heads, grad_low, grad_other)
    return call(
        kernel,
        (shape((2, 4, part, width), WIDE), shape((2, 4, part, width), LOW)),
        spot,
        operands,
        flops=2 * width * (one_grad.size + two_grad.size + heads.size),
        scratch=[pltpu.VMEM((2, 2, 4, part, width), WIDE)],
        piped=True,
    )


def finish_mixed(spot, own_piece, first_piece, last_pieces, fused):
    part, width = own_piece.shape[1:]
    local = 4 * part

    def kernel(spot_ref, a_ref, b_ref, c_ref, *outs):
        me = spot_ref[0]
        high = spot_ref[1]
        low = spot_ref[2]
        for kz in range(2):
            for ky in range(2):
                row = pl.multiple_of(((kz ^ high) * 2 + (ky ^ low)) * part, 16)
                early, late = (kz, ky) if fused else (ky, kz)
                ref = c_ref.at[early] if late else (b_ref if early else a_ref)
                for j in range(4):
                    block = ref[me ^ j].astype(WIDE)
                    for p in range(3):
                        piece = block[:, p * local : (p + 1) * local]
                        if fused:
                            out, at = outs[0], p * width + j * local
                        elif p == 0:
                            out, at = outs[0], j * local
                        else:
                            out, at = outs[1], (p - 1) * width + j * local
                        out[pl.ds(row, part), at : at + local] = piece
                    flat = ref[j, :, 3 * local :].astype(WIDE)
                    outs[-1][pl.ds(row, part), j * local : (j + 1) * local] = flat

    widths = (3 * width, width) if fused else (width, 2 * width, width)
    return call(
        kernel,
        tuple(shape((local, w), WIDE) for w in widths),
        spot,
        (own_piece, first_piece, last_pieces),
        piped=True,
    )


def exchange_sum(keep, send, bit, *holds):
    got = flip_ctx(send, bit)
    if holds:
        got = after(got, *holds)
    return keep + got.astype(WIDE)


def sum_rest(total):
    lines = lax.axis_size("ctx") // lax.axis_size("fsdp")
    for bit in powers(lax.axis_size("ctx")):
        if bit not in (1, lines):
            low = total.astype(LOW)
            total = low.astype(WIDE) + flip_ctx(low, bit).astype(WIDE)
    return total.astype(LOW)


def trade_columns(low):
    part = low.shape[1]
    local = 4 * part
    far = flip_model(low[2:], 2)
    near = flip_model(jnp.stack([low[1], far[1]]), 1)
    columns = jnp.stack([low[0], near[0], far[0], near[1]])
    return jnp.concatenate([columns[..., : 3 * local], low[..., 3 * local :]], axis=-1)


def gather_pieces(piece, bits):
    first = flip_ctx(piece, bits[0])
    return piece, first, flip_ctx(jnp.stack([piece, first]), bits[1])


def move_columns(mate, cross, *holds):
    line = flip_ctx(after(cross, *holds), 1)
    return flip_model(mate, 1), cross, line, flip_model(cross, 1), flip_model(line, 1)


def core_sum(keep, send):
    mine = keep + flip_model(send, 1).astype(WIDE)
    return mine, flip_model(mine.astype(LOW), 2)


def sum_lines(low, lines):
    value = low.reshape(lines, -1, low.shape[1])
    for bit in reversed(line_bits()):
        value = value[:bit].astype(WIDE) + flip_ctx(value[bit:], bit).astype(WIDE)
        value = value.astype(LOW)
    return value[0]


def body(
    hidden,
    encoded,
    cotangent,
    dec_seg,
    enc_seg,
    self_qkv,
    self_out,
    cross_q,
    cross_kv,
    cross_out,
    ffn_in,
    ffn_out,
    biases,
    gains,
    ffn_bias,
):
    tokens = hidden.shape[1]
    width = hidden.shape[2]
    sources = encoded.shape[1]
    model = lax.axis_size("fsdp")
    lines = lax.axis_size("ctx") // model
    own = lax.axis_index("fsdp")
    ctx_index = lax.axis_index("ctx")
    local = width // model
    spot = jnp.stack([own, (ctx_index // lines) % 2, ctx_index % 2, ctx_index % lines])
    spot = spot.astype(jnp.int32)

    marks = jnp.concatenate([dec_seg[0], enc_seg[0]]).astype(LOW)
    marks = jnp.pad(marks, (0, width - tokens - sources))[None]
    block = jnp.concatenate([hidden[0], encoded[0], jnp.pad(marks, ((0, 15), (0, 0)))], axis=0)
    self_qkv = after(self_qkv, block)
    block = swap_places(block)
    small = jnp.concatenate([biases, gains, jnp.zeros((3, local), WIDE)], axis=0)
    qkv_own, qkv_mate, qkv_away = prepare_qkv(spot, self_qkv, small)
    qkv_cross = flip_model(qkv_away, 2)
    block = after(block, qkv_cross)
    block_far = flip_model(block, 2)
    qkv_blocks = (qkv_own,) + move_columns(qkv_mate, qkv_cross, block)
    near_rows = jnp.stack([block, block_far])[None]
    rest_own, rest_mate, rest_away, w_so, w_co, w_fo = prepare_rest(
        spot, cross_q, cross_kv, ffn_in, self_out, cross_out, ffn_out
    )
    near_rows = after(near_rows, rest_away, qkv_blocks[3])
    rest_cross = flip_model(after(rest_away, block_far), 2)
    other = swap_places(after(cotangent[0], block_far))
    for bit in line_bits():
        near_rows = jnp.concatenate([near_rows, flip_ctx(near_rows, bit)], axis=0)
    near_rows = after(near_rows, rest_cross)
    far_rows = flip_model(near_rows, 1)
    rest_blocks = (rest_own,) + move_columns(rest_mate, rest_cross, near_rows)

    inputs, source_rows, queries, keys, values, w_q, w_kv, table, marks, emarks = project(
        spot, near_rows, far_rows, qkv_blocks, tokens, sources
    )
    queries = after(queries, other)
    other_far = flip_model(other, 2)
    plain = keys.shape[0] > 2048
    line_ids = (ctx_index % lines) ^ jnp.arange(lines, dtype=jnp.int32)[:, None]
    model_ids = own ^ jnp.array([0, 2, 1, 3], jnp.int32)[None, :]
    starts = (model_ids * lines + line_ids) * tokens
    places = (starts[:, :, None] + jnp.arange(tokens, dtype=jnp.int32)).reshape(-1)
    if plain:
        attended, keep, send = plain_forward(marks, places, queries, keys, values, w_so)
    else:
        attended, keep, send = self_forward(spot, marks, queries, keys, values, w_so, tokens)
    keep, send = after(keep, other_far), after(send, other_far)
    mine, away = core_sum(keep, send)
    w_cq, w_ckv, w_fi, source_keys, source_values = arrange_rest(
        spot, rest_blocks, source_rows, table
    )
    away = after(away, w_cq)
    first, first_low, first_normal, first_rate = residual_norm(inputs, mine, away, table, 5, 0)
    first_other = flip_model(first_low, 1)
    small_low = small.astype(LOW).astype(WIDE)
    cross_queries, crossed, keep, send = cross_forward(
        spot, marks, emarks, first_low, first_other, w_cq, source_keys, source_values, w_co, small_low, tokens
    )
    mine, away = core_sum(keep, send)
    second, second_low, second_normal, second_rate = residual_norm(first, mine, away, table, 8, 1)
    second_other = flip_model(second_low, 1)
    inner_bias = ffn_bias.astype(LOW).astype(WIDE)[None]
    activated, slope, keep, send = ffn_forward(second_low, second_other, w_fi, w_fo, inner_bias)
    mine, away = core_sum(keep, send)
    result, third_grad, ffn_low, third_sums = turn_around(
        second, mine, away, table, other, other_far, tokens
    )
    result = swap_places(result)
    output = result[None]

    ffn_other = flip_model(ffn_low, 1)
    inner_grad, keep, send, inner_sum = ffn_back(ffn_low, ffn_other, w_fo, w_fi, slope)
    mine, away = core_sum(keep, send)
    out_keep, out_send, in_keep, in_send = produce_ffn(
        spot, activated, ffn_low, ffn_other, second_low, second_other, inner_grad
    )
    away = after(away, in_keep, result)
    out_got = flip_ctx(out_send, 1)
    in_got = flip_ctx(in_send, lines)
    second_grad, cross_low, second_sums = residual_back(
        third_grad, mine, away, second_normal, second_rate, table, 1, tokens
    )
    cross_other = flip_model(cross_low, 1)
    cross_query_pre, source_grad, keep, send, cross_sums = cross_back(
        spot, marks, emarks, cross_low, cross_other, w_co, cross_queries, source_keys, source_values, w_cq, tokens
    )
    mine, away = core_sum(keep, send)
    cross_keep, cross_send = produce_mixed(
        spot, (first_low, first_other), cross_query_pre, source_rows, source_grad, crossed, cross_low, cross_other
    )
    away = after(away, cross_keep)
    cross_got = flip_ctx(cross_send, 1)
    first_grad, self_low, first_sums = residual_back(
        second_grad, mine, away, first_normal, first_rate, table, 0, tokens
    )
    self_other = flip_model(self_low, 1)
    out_half = out_keep + after(out_got, self_low).astype(WIDE)
    in_half = in_keep + after(in_got, self_low).astype(WIDE)
    out_got = flip_ctx(out_half[1].astype(LOW), lines)
    in_got = flip_ctx(in_half[1].astype(LOW), 1)
    if plain:
        self_query_pre, pair_grad, self_sums = plain_back(
            marks, places, self_low, self_other, w_so, queries, keys, values
        )
    else:
        self_query_pre, pair_grad, self_sums = self_back(
            spot, marks, self_low, self_other, w_so, queries, keys, values, tokens
        )
    self_keep, self_send = produce_mixed(
        spot, (inputs,), self_query_pre, inputs, pair_grad, attended, self_low, self_other
    )
    self_total = exchange_sum(self_keep, self_send, 1)
    ffn_total = jnp.stack(
        [
            out_half[0] + after(out_got, self_keep).astype(WIDE),
            in_half[0] + after(in_got, self_keep).astype(WIDE),
        ]
    )
    ffn_total = sum_rest(ffn_total)
    cross_total = cross_keep + after(cross_got, self_keep).astype(WIDE)
    cross_total = exchange_sum(cross_total[0], cross_total[1].astype(LOW), lines, self_total)
    cross_piece = sum_rest(after(cross_total, ffn_total))
    pair_own = sum_lines(after(pair_grad, self_total), lines)
    source_own = sum_lines(after(source_grad, self_total), lines)
    encoded_part = mm_nt(source_own, w_ckv)
    encoded_part = encoded_part[: 2 * sources] + flip_model(
        encoded_part[2 * sources :].astype(LOW), 1
    ).astype(WIDE)
    encoded_part = encoded_part[:sources] + flip_model(
        encoded_part[sources:].astype(LOW), 2
    ).astype(WIDE)

    keep, send = input_back(self_query_pre, pair_own, w_q, w_kv)
    input_part = keep + flip_model(send, 1).astype(WIDE)
    input_part = input_part[:tokens] + flip_model(input_part[tokens:].astype(LOW), 2).astype(WIDE)
    input_grad = first_grad[:tokens] + input_part
    both = jnp.concatenate([input_grad, encoded_part], axis=0).astype(LOW)
    both = swap_places(both).astype(WIDE)[None]
    hidden_grad = both[:, :tokens]
    encoded_grad = both[:, tokens:]

    self_total = exchange_sum(self_total[0], self_total[1].astype(LOW), lines)
    self_piece = sum_rest(self_total)
    cross_pieces = gather_pieces(trade_columns(cross_piece), (1, lines))
    self_pieces = gather_pieces(trade_columns(self_piece), (lines, 1))
    ffn_far = flip_model(ffn_total[1, 2:], 2)
    ffn_near = flip_model(jnp.stack([ffn_total[1, 1], ffn_far[1]]), 1)
    ffn_piece = jnp.stack([ffn_total[1, 0], ffn_near[0], ffn_far[0], ffn_near[1]])
    out_pieces = gather_pieces(ffn_total[0], (lines, 1))
    in_pieces = gather_pieces(ffn_piece, (1, lines))
    g_cq, g_ckv, g_co = finish_mixed(spot, *cross_pieces, False)
    g_fo, g_fi = finish_ffn(spot, out_pieces, in_pieces)
    g_qkv, g_so = finish_mixed(spot, *self_pieces, True)

    wide_rows = jnp.concatenate([first_sums, second_sums, third_sums], axis=0)
    wide_rows = after(wide_rows, self_keep)
    for bit in (1, 2):
        wide_rows = wide_rows + flip_model(wide_rows, bit)
    wide_rows = lax.dynamic_slice_in_dim(wide_rows, own * local, local, axis=1)
    vectors = jnp.concatenate(
        [wide_rows, self_sums, cross_sums, inner_sum.reshape(-1, local)], axis=0
    )
    vectors = after(vectors, pair_own)
    holds = {1: input_grad, lines: self_piece}
    for bit in powers(lax.axis_size("ctx")):
        vectors = vectors + after(flip_ctx(vectors, bit), holds.get(bit, self_piece))
    d_bias = jnp.stack([vectors[i] for i in (0, 3, 6, 9, 10, 2, 11, 12, 5, 8)])
    d_gain = jnp.stack([vectors[i] for i in (1, 4, 7)])
    d_inner = vectors[13:].reshape(-1)
    return (
        output,
        hidden_grad,
        encoded_grad,
        g_qkv,
        g_so,
        g_cq,
        g_ckv,
        g_co,
        g_fi,
        g_fo,
        d_bias,
        d_gain,
        d_inner,
    )


def solution(mesh):
    whole = P("fsdp", "ctx", None)
    matrix = P("fsdp", None)
    ids = P("fsdp", "ctx")
    table = P(None, "fsdp")
    return jax.shard_map(
        body,
        mesh=mesh,
        in_specs=(whole, whole, whole, ids, ids) + (matrix,) * 7 + (table, table, P("fsdp")),
        out_specs=(whole,) * 3 + (matrix,) * 7 + (table, table, P("fsdp")),
        check_vma=False,
    )
```

```python
import jax
import jax.numpy as jnp
from jax import lax
from jax.experimental import pallas as pl
from jax.experimental.pallas import tpu as pltpu
from jax.sharding import PartitionSpec as P

H = 12
HD = 64
EPSILON = 1e-05
FLOOR_SCORE = -1e30
SCALE = float(HD) ** (-0.5)
LOW = jnp.bfloat16
WIDE = jnp.float32


def mm(left, right):
    return jnp.dot(left, right, preferred_element_type=WIDE)


def mm_tn(left, right):
    return lax.dot_general(left, right, (((0,), (0,)), ((), ())), preferred_element_type=WIDE)


def mm_nt(left, right):
    return lax.dot_general(left, right, (((1,), (1,)), ((), ())), preferred_element_type=WIDE)


def flip_model(value, bit):
    count = lax.axis_size("fsdp")
    return lax.ppermute(value, "fsdp", [(i, i ^ bit) for i in range(count)])


def flip_ctx(value, bit):
    count = lax.axis_size("ctx")
    return lax.ppermute(value, "ctx", [(i, i ^ bit) for i in range(count)])


def swap_places(value):
    model = lax.axis_size("fsdp")
    ctx = lax.axis_size("ctx")
    lines = ctx // model
    route = []
    for f in range(model):
        for z in range(model):
            for r in range(lines):
                route.append((f * ctx + z * lines + r, z * ctx + f * lines + r))
    return lax.ppermute(value, ("fsdp", "ctx"), route)


def powers(limit):
    bits = []
    bit = 1
    while bit < limit:
        bits.append(bit)
        bit *= 2
    return bits


def line_bits():
    return powers(lax.axis_size("ctx") // lax.axis_size("fsdp"))


def after(value, *others):
    return lax.optimization_barrier((value,) + others)[0]


def shape(dims, kind):
    return jax.ShapeDtypeStruct(tuple(dims), kind)


COST = 2.5


def cost(flops, *arrays):
    count = 0
    for array in arrays:
        count += array.size * array.dtype.itemsize
    return pl.CostEstimate(
        flops=int(flops * COST), transcendentals=0, bytes_accessed=int(count * COST)
    )


def call(kernel, outs, spot, operands, flops=0, scratch=(), limit=12, piped=False, cold=(), parked=(), saved=()):
    many = isinstance(outs, tuple)
    listed = list(outs) if many else [outs]
    count = len(operands)
    if saved:
        first = operands[saved[0]]
        height = sum(operands[at].shape[0] for at in saved)
        listed.append(shape((height,) + first.shape[1:], first.dtype))
        many = True
    body = kernel
    if cold or parked or saved:
        place = pl.BlockSpec(memory_space=pltpu.VMEM)
        far = pl.BlockSpec(memory_space=pltpu.HBM)
        own = count + len(listed) + len(scratch)

        def body(spot_ref, *all_refs):
            refs, buffers, done = list(all_refs[:own]), list(all_refs[own:-1]), all_refs[-1]
            used = 0
            ending = []

            def copy(source, target):
                nonlocal used
                moving = pltpu.make_async_copy(source, target, done.at[used])
                used += 1
                return moving

            incoming = []
            for at in cold:
                buffer = buffers.pop(0)
                incoming.append(copy(refs[at], buffer))
                incoming[-1].start()
                refs[at] = buffer
            row = 0
            for at in saved:
                target = refs[count + len(listed) - 1].at[pl.ds(row, operands[at].shape[0])]
                row += operands[at].shape[0]
                ending.append(copy(refs[at], target))
                ending[-1].start()
            for moving in incoming:
                moving.wait()
            outgoing = []
            for at in parked:
                buffer = buffers.pop(0)
                outgoing.append(copy(buffer, refs[count + at]))
                refs[count + at] = buffer
            if saved:
                refs.pop(count + len(listed) - 1)
            kernel(spot_ref, *refs)
            for moving in outgoing:
                moving.start()
            for moving in outgoing + ending:
                moving.wait()

        buffers = [pltpu.VMEM(operands[at].shape, operands[at].dtype) for at in cold]
        buffers += [pltpu.VMEM(listed[at].shape, listed[at].dtype) for at in parked]
        held = set(parked) | ({len(listed) - 1} if saved else set())
        out_specs = [far if at in held else place for at in range(len(listed))]
        moves = len(cold) + len(parked) + len(saved)
        spec = dict(
            in_specs=[pl.BlockSpec(memory_space=pltpu.SMEM)]
            + [far if at in cold else place for at in range(count)],
            out_specs=tuple(out_specs) if many else out_specs[0],
            scratch_shapes=list(scratch) + buffers + [pltpu.SemaphoreType.DMA((moves,))],
        )
        limit = limit + 8
    elif piped:
        place = lambda value: pl.BlockSpec(value.shape, lambda i, spot: (0,) * len(value.shape))
        spec = dict(
            grid_spec=pltpu.PrefetchScalarGridSpec(
                num_scalar_prefetch=1,
                grid=(1,),
                in_specs=[place(value) for value in operands],
                out_specs=tuple(place(value) for value in listed) if many else place(outs),
                scratch_shapes=list(scratch),
            )
        )
        limit = limit + 12
    else:
        place = pl.BlockSpec(memory_space=pltpu.VMEM)
        spec = dict(
            in_specs=[pl.BlockSpec(memory_space=pltpu.SMEM)] + [place] * count,
            out_specs=tuple(place for _ in listed) if many else place,
            scratch_shapes=list(scratch),
        )
    return pl.pallas_call(
        body,
        out_shape=tuple(listed) if many else outs,
        cost_estimate=cost(flops, *operands, *listed),
        compiler_params=pltpu.CompilerParams(vmem_limit_bytes=limit << 20),
        **spec,
    )(spot, *operands)


def prepare_qkv(spot, weight, small):
    rows = weight.shape[0]

    def kernel(spot_ref, w_ref, small_ref, own_ref, near_ref, far_ref, all_ref):
        me = spot_ref[0]
        side = spot_ref[2]
        small = small_ref[...].astype(LOW)
        tail = jnp.zeros((16, 2 * rows), LOW)
        for d in range(4):
            for p in range(3):
                piece = w_ref[:, p * 4 * rows + d * rows : p * 4 * rows + (d + 1) * rows]
                all_ref[me ^ d, :, p * rows : (p + 1) * rows] = piece.astype(LOW)
        own_ref[:rows] = all_ref[0]
        near_ref[:rows] = all_ref[1]
        far_ref[:rows] = all_ref[2 + side]
        for ref in (own_ref, near_ref, far_ref):
            ref[rows:, :rows] = small
            ref[rows:, rows:] = tail

    piece = (rows + 16, 3 * rows)
    return call(
        kernel,
        (shape(piece, LOW),) * 3,
        spot,
        (weight, small),
        scratch=[pltpu.VMEM((4, rows, 3 * rows), LOW)],
    )


def prepare_rest(spot, cross_q, cross_kv, ffn_in, self_out, cross_out, ffn_out):
    rows = cross_q.shape[0]
    wide = ffn_in.shape[1] // 4
    piece = (rows, 3 * rows + wide)

    def kernel(spot_ref, q_ref, kv_ref, fi_ref, so_ref, co_ref, fo_ref, *outs):
        own_ref, near_ref, far_ref, so_out, co_out, fo_out, all_ref = outs
        me = spot_ref[0]
        side = spot_ref[2]
        for d in range(4):
            all_ref[me ^ d, :, :rows] = q_ref[:, d * rows : (d + 1) * rows].astype(LOW)
            for p in range(2):
                part = kv_ref[:, (p * 4 + d) * rows : (p * 4 + d + 1) * rows]
                all_ref[me ^ d, :, (1 + p) * rows : (2 + p) * rows] = part.astype(LOW)
            all_ref[me ^ d, :, 3 * rows :] = fi_ref[:, d * wide : (d + 1) * wide].astype(LOW)
        own_ref[...] = all_ref[0]
        near_ref[...] = all_ref[1]
        far_ref[...] = all_ref[2 + side]
        so_out[...] = so_ref[...].astype(LOW)
        co_out[...] = co_ref[...].astype(LOW)
        fo_out[...] = fo_ref[...].astype(LOW)

    return call(
        kernel,
        (shape(piece, LOW),) * 3
        + (shape(self_out.shape, LOW), shape(cross_out.shape, LOW), shape(ffn_out.shape, LOW)),
        spot,
        (cross_q, cross_kv, ffn_in, self_out, cross_out, ffn_out),
        scratch=[pltpu.VMEM((4,) + piece, LOW)],
        limit=16,
        piped=True,
    )


def ordered_blocks(spot_ref, refs, pair_ref):
    side = spot_ref[2]
    pair_ref[0, side] = refs[2][...]
    pair_ref[0, 1 - side] = refs[3][...]
    pair_ref[1, side] = refs[4][...]
    pair_ref[1, 1 - side] = refs[5][...]
    return refs[0][...], refs[1][...], pair_ref[0, 0], pair_ref[1, 1]


def arrange_rest(spot, blocks, near_rows, far_rows, table):
    rows = blocks[0].shape[0]
    wide = blocks[0].shape[1] - 3 * rows
    lines, _, sources, width = near_rows.shape
    count = lines * 4 * sources

    def kernel(spot_ref, *refs):
        a_ref, b_ref, table_ref, q_ref, kv_ref, fi_ref, x_ref, *outs = refs[6:]
        keys_ref, values_ref, rel_ref, pair_ref = outs
        me = spot_ref[0]
        parts = ordered_blocks(spot_ref, refs[:6], pair_ref)
        for k in range(4):
            start = pl.multiple_of((me ^ k) * rows, 64)
            q_ref[pl.ds(start, rows), :] = parts[k][:, :rows]
            kv_ref[pl.ds(start, rows), :] = parts[k][:, rows : 3 * rows]
            fi_ref[pl.ds(start, rows), :] = parts[k][:, 3 * rows :]
        for r in range(lines):
            for kc, ref in enumerate((a_ref, b_ref)):
                for kx in range(2):
                    start = (4 * r + 2 * kc + kx) * sources
                    x_ref[start : start + sources, :] = ref[r, kx]
        for j in range(4):
            rel_ref[j] = table_ref[:, j * rows : (j + 1) * rows]
        shift = rel_ref[me][7:8]
        out = mm(x_ref[...], kv_ref[...])
        keys_ref[...] = out[:, :rows].astype(LOW)
        values_ref[...] = (out[:, rows:] + shift).astype(LOW)

    return call(
        kernel,
        (
            shape((4 * rows, rows), LOW),
            shape((4 * rows, 2 * rows), LOW),
            shape((4 * rows, wide), LOW),
            shape((count, width), LOW),
            shape((count, rows), LOW),
            shape((count, rows), LOW),
        ),
        spot,
        tuple(blocks) + (near_rows, far_rows, table),
        flops=4 * count * width * rows,
        scratch=[pltpu.VMEM((4, 16, rows), WIDE), pltpu.VMEM((2, 2) + blocks[0].shape, LOW)],
        limit=16,
        parked=(3,),
    )


def project(spot, near_rows, far_rows, blocks, tokens, sources):
    lines = near_rows.shape[0]
    width = near_rows.shape[-1]
    local = width // 4
    span = near_rows.shape[2]
    rows = 4 * tokens

    def kernel(spot_ref, a_ref, b_ref, *refs):
        x_ref, q_ref, k_ref, v_ref, wq_ref, wkv_ref, table_ref, *outs = refs[6:]
        marks_ref, emarks_ref, rel_ref, w_ref, pair_ref = outs
        me = spot_ref[0]

        @pl.when(pl.program_id(0) == 0)
        def _():
            parts = ordered_blocks(spot_ref, refs[:6], pair_ref)
            for k in range(4):
                start = pl.multiple_of((me ^ k) * local, 64)
                w_ref[pl.ds(start, local), :] = parts[k][:local]
                rel_ref[k] = parts[k][local:, :local].astype(WIDE)
            for j in range(4):
                table_ref[:, j * local : (j + 1) * local] = rel_ref[me ^ j]
            wq_ref[...] = w_ref[:, :local]
            wkv_ref[...] = w_ref[:, local:]

        lane = lax.broadcasted_iota(jnp.int32, (1, 128), 1)
        emarks = jnp.zeros((1, 128), WIDE)
        for kc, ref in enumerate((a_ref, b_ref)):
            for kx in range(2):
                at = 2 * kc + kx
                start = at * tokens
                x_ref[start : start + tokens, :] = ref[0, kx, :tokens, :]
                marks = ref[0, kx, tokens : tokens + 16, :256].astype(WIDE)
                marks_ref[:, start : start + tokens] = marks[0:1, :tokens]
                moved = pltpu.roll(marks[:8, 128:], at * sources, 1)[0:1]
                emarks = emarks + jnp.where((lane // sources) == at, moved, 0.0)
        emarks_ref[...] = emarks
        own_small = rel_ref[0]
        out = mm(x_ref[...], w_ref[...])
        k_ref[...] = out[:, local : 2 * local].astype(LOW)
        v_ref[...] = (out[:, 2 * local :] + own_small[4:5]).astype(LOW)

        @pl.when(pl.program_id(0) == 0)
        def _():
            q_ref[...] = ((out[:, :local] + own_small[3:4]) * SCALE).astype(LOW)

    full = lambda *dims: pl.BlockSpec(dims, lambda i, spot: (0,) * len(dims))
    band = lambda w: pl.BlockSpec((rows, w), lambda i, spot: (i, 0))
    part = pl.BlockSpec((1, 2, span, width), lambda i, spot: (i, 0, 0, 0))
    piece = (local + 16, 3 * local)
    outs = (
        shape((lines * rows, width), LOW),
        shape((rows, local), LOW),
        shape((lines * rows, local), LOW),
        shape((lines * rows, local), LOW),
        shape((width, local), LOW),
        shape((width, 2 * local), LOW),
        shape((16, width), WIDE),
        shape((1, lines * rows), WIDE),
        shape((1, lines * 4 * sources), WIDE),
    )
    operands = (near_rows, far_rows) + tuple(blocks)
    return pl.pallas_call(
        kernel,
        out_shape=outs,
        grid_spec=pltpu.PrefetchScalarGridSpec(
            num_scalar_prefetch=1,
            grid=(lines,),
            in_specs=[part, part] + [full(*piece)] * 6,
            out_specs=(
                band(width),
                full(rows, local),
                band(local),
                band(local),
                full(width, local),
                full(width, 2 * local),
                full(16, width),
                pl.BlockSpec((1, rows), lambda i, spot: (0, i)),
                pl.BlockSpec((1, 4 * sources), lambda i, spot: (0, i)),
            ),
            scratch_shapes=[
                pltpu.VMEM((4, 16, local), WIDE),
                pltpu.VMEM((width, 3 * local), LOW),
                pltpu.VMEM((2, 2) + piece, LOW),
            ],
        ),
        cost_estimate=cost(6 * lines * rows * width * local, *operands, *outs),
        compiler_params=pltpu.CompilerParams(vmem_limit_bytes=20 << 20),
    )(spot, *operands)


def block_start(spot_ref, index, tokens, lines):
    me = spot_ref[0]
    line = spot_ref[3]
    kr, kc, kx = index // 4, (index // 2) % 2, index % 2
    return ((me ^ (kc + 2 * kx)) * lines + (line ^ kr)) * tokens


def upright(row):
    return jnp.transpose(jnp.broadcast_to(row, (128, row.shape[1])))


def self_floor(spot_ref, marks_ref, query_blocks, tokens, turned):
    blocks = marks_ref.shape[1] // tokens
    lines = blocks // 4
    down = lax.broadcasted_iota(jnp.int32, (tokens, tokens), 0)
    right = lax.broadcasted_iota(jnp.int32, (tokens, tokens), 1)
    outer, inner = (range(blocks), query_blocks) if turned else (query_blocks, range(blocks))
    table = []
    for i in outer:
        tall = upright(marks_ref[:, i * tokens : (i + 1) * tokens])
        line = []
        for j in inner:
            flat = marks_ref[:, j * tokens : (j + 1) * tokens]
            gap = block_start(spot_ref, j, tokens, lines) - block_start(spot_ref, i, tokens, lines)
            ahead = (right + gap) - down
            near = (ahead >= 0) if turned else (ahead <= 0)
            line.append(jnp.where((tall == flat) & near, 0.0, FLOOR_SCORE))
        table.append(jnp.concatenate(line, axis=1))
    return jnp.concatenate(table, axis=0)


def head_lanes(value, head):
    lane = lax.broadcasted_iota(jnp.int32, (1, value.shape[1]), 1) // HD
    return jnp.where(lane == head, value, jnp.zeros_like(value))


def attend_rows(queries, keys, values, floor):
    heads = queries.shape[1] // HD
    total = None
    for h in range(heads):
        scores = mm_nt(head_lanes(queries, h), keys) + floor
        top = jnp.max(scores, axis=1, keepdims=True)
        weights = jnp.exp(scores - top)
        prob = weights / jnp.sum(weights, axis=1, keepdims=True)
        part = head_lanes(mm(prob.astype(LOW), values), h)
        total = part if total is None else total + part
    return total.astype(LOW)


def attend_rows_back(queries, keys, values, grads, floor):
    heads = queries.shape[1] // HD
    query_grad = key_grad = value_grad = None
    for h in range(heads):
        own_queries = head_lanes(queries, h)
        own_grads = head_lanes(grads, h)
        scores = mm_nt(keys, own_queries) + floor
        top = jnp.max(scores, axis=0, keepdims=True)
        weights = jnp.exp(scores - top)
        prob = weights / jnp.sum(weights, axis=0, keepdims=True)
        prob_grad = mm_nt(values, own_grads)
        inner = jnp.sum(prob * prob_grad, axis=0, keepdims=True)
        score_grad = (prob * (prob_grad - inner)).astype(LOW)
        part_q = head_lanes(mm_tn(score_grad, keys), h)
        part_k = mm(score_grad, own_queries)
        part_v = mm(prob.astype(LOW), own_grads)
        query_grad = part_q if query_grad is None else query_grad + part_q
        key_grad = part_k if key_grad is None else key_grad + part_k
        value_grad = part_v if value_grad is None else value_grad + part_v
    return query_grad, key_grad, value_grad


def block_rows(keys):
    return 256 if keys <= 1024 else 128


def self_forward(spot, marks, queries, keys, values, weight, tokens):
    rows, local = queries.shape
    width = weight.shape[1]
    size = block_rows(keys.shape[0])

    def kernel(spot_ref, marks_ref, q_ref, k_ref, v_ref, w_ref, o_ref, keep_ref, send_ref):
        for begin in range(0, rows, size):
            blocks = range(begin // tokens, (begin + size) // tokens)
            floor = self_floor(spot_ref, marks_ref, blocks, tokens, False)
            low = attend_rows(q_ref[begin : begin + size], k_ref[...], v_ref[...], floor)
            o_ref[begin : begin + size] = low
            part = mm(low, w_ref[...])
            if begin < rows // 2:
                keep_ref[begin : begin + size] = part
            else:
                send_ref[begin - rows // 2 : begin - rows // 2 + size] = part.astype(LOW)

    return call(
        kernel,
        (shape((rows, local), LOW), shape((rows // 2, width), WIDE), shape((rows // 2, width), LOW)),
        spot,
        (marks, queries, keys, values, weight),
        flops=4 * rows * keys.size + 2 * rows * weight.size,
        limit=20,
    )


def plain_floor(marks, places, rows):
    same = marks.reshape(-1)[:rows, None] == marks
    return jnp.where(same & (places[None, :] <= places[:rows, None]), 0.0, FLOOR_SCORE)


def plain_forward(marks, places, queries, keys, values, weight):
    rows = queries.shape[0]
    low = attend_rows(queries, keys, values, plain_floor(marks, places, rows))
    part = mm(low, weight)
    return low, part[: rows // 2], part[rows // 2 :].astype(LOW)


def plain_back(marks, places, low, other, w_so, queries, keys, values):
    grads = mm_nt(jnp.concatenate([low, other], axis=0), w_so).astype(LOW)
    floor = plain_floor(marks, places, queries.shape[0])
    dq, dk, dv = attend_rows_back(queries, keys, values, grads, floor.T)
    pre = (dq.astype(LOW).astype(WIDE) * SCALE).astype(LOW)
    sums = jnp.concatenate(column_rows(pre, dv), axis=0)
    return pre, jnp.concatenate([dk, dv], axis=1).astype(LOW), sums


def norm_rows(values):
    center = values - jnp.mean(values, axis=-1, keepdims=True)
    spread = jnp.mean(center * center, axis=-1, keepdims=True)
    rate = lax.rsqrt(spread + EPSILON)
    return center * rate, rate


def turned_halves(ref):
    half = ref.shape[0] // 2
    return jnp.concatenate([ref[half:], ref[:half]], axis=0).astype(WIDE)


def residual_norm(residual, mine, other, table, bias_row, norm_row):
    rows, width = mine.shape

    def kernel(spot_ref, r_ref, mine_ref, other_ref, table_ref, h_ref, low_ref, n_ref, rate_ref):
        total = r_ref[:rows].astype(WIDE) + mine_ref[...] + turned_halves(other_ref)
        normal, rate = norm_rows(total + table_ref[bias_row : bias_row + 1])
        gain = table_ref[10 + norm_row : 11 + norm_row]
        result = normal * gain + table_ref[norm_row : norm_row + 1]
        h_ref[...] = result
        low_ref[...] = result.astype(LOW)
        n_ref[...] = normal
        rate_ref[...] = rate

    return call(
        kernel,
        (
            shape((rows, width), WIDE),
            shape((rows, width), LOW),
            shape((rows, width), WIDE),
            shape((rows, 1), WIDE),
        ),
        jnp.zeros((1,), jnp.int32),
        (residual, mine, other, table),
    )


def cross_forward(spot, marks, emarks, low, other, w_cq, keys, values, w_co, small, tokens):
    half, width = low.shape
    local = w_cq.shape[1]

    def kernel(spot_ref, marks_ref, emarks_ref, a_ref, b_ref, w_ref, k_ref, v_ref, o_ref, small_ref, *outs):
        q_out, c_out, keep_ref, send_ref = outs
        for place, ref in enumerate((a_ref, b_ref)):
            at = slice(place * half, (place + 1) * half)
            low = ((mm(ref[...], w_ref[...]) + small_ref[6:7]) * SCALE).astype(LOW)
            q_out[at] = low
            tall = []
            for i in range(place * half // tokens, (place + 1) * half // tokens):
                tall.append(upright(marks_ref[:, i * tokens : (i + 1) * tokens])[:, :1])
            tall = jnp.concatenate(tall, axis=0)
            floor = jnp.where(tall == emarks_ref[...], 0.0, FLOOR_SCORE)
            crossed = attend_rows(low, k_ref[...], v_ref[...], floor)
            c_out[at] = crossed
            part = mm(crossed, o_ref[...])
            if place == 0:
                keep_ref[...] = part
            else:
                send_ref[...] = part.astype(LOW)

    return call(
        kernel,
        (
            shape((2 * half, local), LOW),
            shape((2 * half, local), LOW),
            shape((half, width), WIDE),
            shape((half, width), LOW),
        ),
        spot,
        (marks, emarks, low, other, w_cq, keys, values, w_co, small),
        flops=8 * half * width * local,
        limit=16,
        parked=(1,),
        saved=(2, 3),
    )


def ffn_forward(low, other, w_fi, w_fo, shift):
    half, width = low.shape
    wide = w_fi.shape[1]

    def kernel(spot_ref, a_ref, b_ref, w_ref, o_ref, shift_ref, g_ref, slope_ref, keep_ref, send_ref):
        for place, ref in enumerate((a_ref, b_ref)):
            at = slice(place * half, (place + 1) * half)
            pre = mm(ref[...], w_ref[...]) + shift_ref[...]
            bell = 0.5 * (1.0 + lax.erf(pre * (0.5**0.5)))
            act = (pre * bell).astype(LOW)
            g_ref[at] = act
            slope_ref[at] = bell + pre * jnp.exp(-0.5 * pre * pre) * 0.3989422804014327
            part = mm(act, o_ref[...])
            if place == 0:
                keep_ref[...] = part
            else:
                send_ref[...] = part.astype(LOW)

    return call(
        kernel,
        (
            shape((2 * half, wide), LOW),
            shape((2 * half, wide), WIDE),
            shape((half, width), WIDE),
            shape((half, width), LOW),
        ),
        jnp.zeros((1,), jnp.int32),
        (low, other, w_fi, w_fo, shift),
        flops=8 * half * width * wide,
    )


def norm_back(grad, normal, rate, gain):
    up = grad * gain
    mean_up = jnp.mean(up, axis=-1, keepdims=True)
    mean_both = jnp.mean(up * normal, axis=-1, keepdims=True)
    return rate * (up - mean_up - normal * mean_both)


def column_rows(*values):
    rows = [jnp.sum(value.astype(WIDE), axis=0, keepdims=True) for value in values]
    return rows


def turn_around(residual, mine, other, table, own_grad, other_grad, tokens):
    rows, width = mine.shape

    def kernel(spot_ref, r_ref, mine_ref, other_ref, table_ref, a_ref, b_ref, out_ref, d_ref, low_ref, sum_ref):
        total = r_ref[...] + mine_ref[...] + turned_halves(other_ref) + table_ref[9:10]
        normal, rate = norm_rows(total)
        gain = table_ref[12:13]
        out_ref[...] = (normal[:tokens] * gain + table_ref[2:3]).astype(LOW)
        grad = jnp.concatenate([a_ref[:tokens], b_ref[:tokens]], axis=0).astype(WIDE)
        back = norm_back(grad, normal, rate, gain)
        low = back.astype(LOW)
        d_ref[...] = back
        low_ref[...] = low
        rows = column_rows(grad, grad * normal, low)
        for i in range(3):
            sum_ref[i : i + 1] = rows[i]

    return call(
        kernel,
        (
            shape((tokens, width), LOW),
            shape((rows, width), WIDE),
            shape((rows, width), LOW),
            shape((3, width), WIDE),
        ),
        jnp.zeros((1,), jnp.int32),
        (residual, mine, other, table, own_grad, other_grad),
        piped=True,
    )


def residual_back(previous, mine, other, normal, rate, table, norm_row, tokens):
    rows, width = mine.shape

    def kernel(spot_ref, p_ref, mine_ref, other_ref, n_ref, rate_ref, table_ref, d_ref, low_ref, sum_ref):
        grad = p_ref[...] + mine_ref[...] + turned_halves(other_ref)
        normal = n_ref[...]
        back = norm_back(grad, normal, rate_ref[...], table_ref[10 + norm_row : 11 + norm_row])
        low = back.astype(LOW)
        d_ref[...] = back
        low_ref[...] = low
        rows = column_rows(grad, grad * normal, low)
        for i in range(3):
            sum_ref[i : i + 1] = rows[i]

    return call(
        kernel,
        (shape((rows, width), WIDE), shape((rows, width), LOW), shape((3, width), WIDE)),
        jnp.zeros((1,), jnp.int32),
        (previous, mine, other, normal, rate, table),
        cold=(3, 4),
    )


def ffn_back(low, other, w_fo, w_fi, slope):
    half, width = low.shape
    wide = w_fi.shape[1]

    def kernel(spot_ref, a_ref, b_ref, o_ref, w_ref, slope_ref, u_ref, keep_ref, send_ref, sum_ref):
        total = None
        for place, ref in enumerate((a_ref, b_ref)):
            at = slice(place * half, (place + 1) * half)
            inner = (mm_nt(ref[...], o_ref[...]) * slope_ref[at]).astype(LOW)
            u_ref[at] = inner
            row = column_rows(inner)[0]
            total = row if total is None else total + row
            part = mm_nt(inner, w_ref[...])
            if place == 0:
                keep_ref[...] = part
            else:
                send_ref[...] = part.astype(LOW)
        sum_ref[...] = total

    return call(
        kernel,
        (
            shape((2 * half, wide), LOW),
            shape((half, width), WIDE),
            shape((half, width), LOW),
            shape((1, wide), WIDE),
        ),
        jnp.zeros((1,), jnp.int32),
        (low, other, w_fo, w_fi, slope),
        flops=8 * half * width * wide,
        piped=True,
    )


def cross_back(spot, marks, emarks, low, other, w_co, queries, keys, values, w_cq, tokens):
    half, width = low.shape
    count, local = keys.shape

    def kernel(spot_ref, marks_ref, emarks_ref, a_ref, b_ref, co_ref, q_ref, k_ref, v_ref, cq_ref, *outs):
        dq_ref, dkv_ref, keep_ref, send_ref, sum_ref = outs
        key_grad = value_grad = None
        tall = []
        for i in range(count // 128):
            tall.append(upright(emarks_ref[:, i * 128 : (i + 1) * 128])[:, :1])
        tall = jnp.concatenate(tall, axis=0)
        totals = None
        for place, ref in enumerate((a_ref, b_ref)):
            at = slice(place * half, (place + 1) * half)
            grads = mm_nt(ref[...], co_ref[...]).astype(LOW)
            floor = jnp.where(tall == marks_ref[:, at], 0.0, FLOOR_SCORE)
            dq, dk, dv = attend_rows_back(q_ref[at], k_ref[...], v_ref[...], grads, floor)
            pre = (dq.astype(LOW).astype(WIDE) * SCALE).astype(LOW)
            dq_ref[at] = pre
            key_grad = dk if key_grad is None else key_grad + dk
            value_grad = dv if value_grad is None else value_grad + dv
            row = column_rows(pre)[0]
            totals = row if totals is None else totals + row
            part = mm_nt(pre, cq_ref[...])
            if place == 0:
                keep_ref[...] = part
            else:
                send_ref[...] = part.astype(LOW)
        dkv_ref[:, :local] = key_grad.astype(LOW)
        dkv_ref[:, local:] = value_grad.astype(LOW)
        sum_ref[0:1] = totals
        sum_ref[1:2] = column_rows(value_grad)[0]

    return call(
        kernel,
        (
            shape((2 * half, local), LOW),
            shape((count, 2 * local), LOW),
            shape((half, width), WIDE),
            shape((half, width), LOW),
            shape((2, local), WIDE),
        ),
        spot,
        (marks, emarks, low, other, w_co, queries, keys, values, w_cq),
        flops=8 * half * width * local,
        limit=16,
        cold=(4, 5, 6, 7, 8),
        saved=(2, 3),
    )


def self_back(spot, marks, low, other, w_so, queries, keys, values, tokens):
    half, width = low.shape
    count, local = keys.shape
    rows = 2 * half
    size = block_rows(count)

    def kernel(spot_ref, marks_ref, a_ref, b_ref, so_ref, q_ref, k_ref, v_ref, dq_ref, dkv_ref, sum_ref, dk_ref, dv_ref):
        totals = None
        for begin in range(0, rows, size):
            source = a_ref if begin < half else b_ref
            local_at = begin % half
            grads = mm_nt(source[local_at : local_at + size], so_ref[...]).astype(LOW)
            blocks = range(begin // tokens, (begin + size) // tokens)
            floor = self_floor(spot_ref, marks_ref, blocks, tokens, True)
            at = slice(begin, begin + size)
            dq, dk, dv = attend_rows_back(q_ref[at], k_ref[...], v_ref[...], grads, floor)
            pre = (dq.astype(LOW).astype(WIDE) * SCALE).astype(LOW)
            dq_ref[at] = pre
            row = column_rows(pre)[0]
            totals = row if totals is None else totals + row
            if begin == 0:
                dk_ref[...] = dk
                dv_ref[...] = dv
            else:
                dk_ref[...] += dk
                dv_ref[...] += dv
        dkv_ref[:, :local] = dk_ref[...].astype(LOW)
        dkv_ref[:, local:] = dv_ref[...].astype(LOW)
        sum_ref[0:1] = totals
        sum_ref[1:2] = column_rows(dv_ref[...])[0]

    return call(
        kernel,
        (shape((rows, local), LOW), shape((count, 2 * local), LOW), shape((2, local), WIDE)),
        spot,
        (marks, low, other, w_so, queries, keys, values),
        flops=10 * rows * keys.size,
        scratch=[pltpu.VMEM((count, local), WIDE), pltpu.VMEM((count, local), WIDE)],
        limit=24,
        cold=(3, 4, 5, 6),
    )


def input_back(query_grad, pair_grad, source_grad, w_q, w_kv, w_ckv, tokens, sources):
    width = w_q.shape[0]
    span = tokens + sources

    def kernel(spot_ref, q_ref, kv_ref, s_ref, wq_ref, wkv_ref, ws_ref, keep_ref, send_ref):
        part = mm_nt(q_ref[...], wq_ref[...]) + mm_nt(kv_ref[...], wkv_ref[...])
        more = mm_nt(s_ref[...], ws_ref[...])
        for kc, ref in enumerate((keep_ref, send_ref)):
            for kx in range(2):
                at = 2 * kc + kx
                start = kx * span
                piece = part[at * tokens : (at + 1) * tokens]
                ref[start : start + tokens] = piece.astype(ref.dtype)
                piece = more[at * sources : (at + 1) * sources]
                ref[start + tokens : start + span] = piece.astype(ref.dtype)

    return call(
        kernel,
        (shape((2 * span, width), WIDE), shape((2 * span, width), LOW)),
        jnp.zeros((1,), jnp.int32),
        (query_grad, pair_grad, source_grad, w_q, w_kv, w_ckv),
        flops=2 * query_grad.shape[0] * (w_q.size + w_kv.size),
        piped=True,
    )


def produce_ffn(spot, activated, grad_low, grad_other, low, other, inner_grad):
    wide = activated.shape[1]
    half, width = grad_low.shape
    part = width // 16

    def kernel(spot_ref, a_ref, g0_ref, g1_ref, x0_ref, x1_ref, u_ref, *refs):
        outs, all_ref = refs[:4], refs[4]
        me = spot_ref[0]
        high = spot_ref[1]
        low = spot_ref[2]
        for place in range(2):
            if place == 0:
                result = mm_tn(a_ref[:half], g0_ref[...]) + mm_tn(a_ref[half:], g1_ref[...])
            else:
                result = mm_tn(x0_ref[...], u_ref[:half]) + mm_tn(x1_ref[...], u_ref[half:])
            for d in range(4):
                for z in range(2):
                    for y in range(2):
                        at = (4 * d + 2 * z + y) * part
                        piece = result[at : at + part]
                        if place == 0:
                            all_ref[low ^ y, high ^ z, d] = piece
                        else:
                            all_ref[high ^ z, low ^ y, me ^ d] = piece
            outs[2 * place][...] = all_ref[0]
            outs[2 * place + 1][...] = all_ref[1].astype(LOW)

    piece = (2, 4, part, width)
    return call(
        kernel,
        (shape(piece, WIDE), shape(piece, LOW)) * 2,
        spot,
        (activated, grad_low, grad_other, low, other, inner_grad),
        flops=8 * half * width * wide,
        scratch=[pltpu.VMEM((2,) + piece, WIDE)],
        limit=16,
        piped=True,
    )


def join_ffn(out_half, out_got, in_half, in_got):
    def kernel(spot_ref, a_ref, b_ref, c_ref, d_ref, out_ref):
        out_ref[0] = (a_ref[0] + b_ref[...].astype(WIDE)).astype(LOW)
        out_ref[1] = (c_ref[0] + d_ref[...].astype(WIDE)).astype(LOW)

    return call(
        kernel,
        shape((2,) + out_got.shape, LOW),
        jnp.zeros((1,), jnp.int32),
        (out_half, out_got, in_half, in_got),
    )


def finish_ffn(spot, out_pieces, in_pieces):
    part, width = out_pieces[0].shape[1:]
    rows = 4 * part

    def kernel(spot_ref, oa_ref, ob_ref, oc_ref, ia_ref, ib_ref, ic_ref, fo_ref, fi_ref):
        me = spot_ref[0]
        high = spot_ref[1]
        low = spot_ref[2]
        for kz in range(2):
            for ky in range(2):
                quarter = ((kz ^ high) * 2 + (ky ^ low)) * part
                source = oc_ref.at[kz] if ky else (ob_ref if kz else oa_ref)
                for d in range(4):
                    row = pl.multiple_of(d * rows + quarter, 16)
                    fo_ref[pl.ds(row, part), :] = source[d].astype(WIDE)
                source = ic_ref.at[ky] if kz else (ib_ref if ky else ia_ref)
                row = pl.multiple_of(quarter, 16)
                for j in range(4):
                    fi_ref[pl.ds(row, part), j * width : (j + 1) * width] = source[me ^ j].astype(WIDE)

    return call(
        kernel,
        (shape((4 * rows, width), WIDE), shape((rows, 4 * width), WIDE)),
        spot,
        tuple(out_pieces) + tuple(in_pieces),
        limit=16,
        piped=True,
    )


def produce_mixed(spot, one_in, one_grad, two_in, two_grad, heads, heads_grads):
    rows, local = one_grad.shape
    width = one_in.shape[1]
    part = local // 4
    pieces = len(heads_grads)
    half = rows // pieces

    def kernel(spot_ref, a_ref, ag_ref, b_ref, bg_ref, o_ref, *refs):
        g_refs, (keep_ref, send_ref, all_ref) = refs[:pieces], refs[pieces:]
        me = spot_ref[0]
        high = spot_ref[1]
        low = spot_ref[2]
        one = mm_tn(a_ref[:rows], ag_ref[...])
        two = mm_tn(b_ref[...], bg_ref[...])
        three = mm_tn(o_ref[:half], g_refs[0][...])
        if pieces == 2:
            three = three + mm_tn(o_ref[half:], g_refs[1][...])
        for z in range(2):
            for y in range(2):
                quarter = (2 * z + y) * part
                for d in range(4):
                    at = d * local + quarter
                    all_ref[low ^ y, high ^ z, me ^ d, :, :local] = one[at : at + part]
                    all_ref[low ^ y, high ^ z, me ^ d, :, local : 3 * local] = two[at : at + part]
                    piece = three[quarter : quarter + part, d * local : (d + 1) * local]
                    all_ref[low ^ y, high ^ z, d, :, 3 * local :] = piece
        keep_ref[...] = all_ref[0]
        send_ref[...] = all_ref[1].astype(LOW)

    operands = (one_in, one_grad, two_in, two_grad, heads) + tuple(heads_grads)
    wide = two_in.shape[0] > 2048
    return call(
        kernel,
        (shape((2, 4, part, width), WIDE), shape((2, 4, part, width), LOW)),
        spot,
        operands,
        flops=2 * width * (one_grad.size + two_grad.size + heads.size),
        scratch=[pltpu.VMEM((2, 2, 4, part, width), WIDE)],
        cold=() if wide else (0, 2, 4) + ((5,) if pieces == 1 else ()),
        piped=wide,
    )


def finish_mixed(spot, own_piece, first_piece, last_pieces, fused):
    part, width = own_piece.shape[1:]
    local = 4 * part

    def kernel(spot_ref, a_ref, b_ref, c_ref, *outs):
        me = spot_ref[0]
        high = spot_ref[1]
        low = spot_ref[2]
        for kz in range(2):
            for ky in range(2):
                row = pl.multiple_of(((kz ^ high) * 2 + (ky ^ low)) * part, 16)
                early, late = (kz, ky) if fused else (ky, kz)
                ref = c_ref.at[early] if late else (b_ref if early else a_ref)
                for j in range(4):
                    block = ref[me ^ j].astype(WIDE)
                    for p in range(3):
                        piece = block[:, p * local : (p + 1) * local]
                        if fused:
                            out, at = outs[0], p * width + j * local
                        elif p == 0:
                            out, at = outs[0], j * local
                        else:
                            out, at = outs[1], (p - 1) * width + j * local
                        out[pl.ds(row, part), at : at + local] = piece
                    flat = ref[j, :, 3 * local :].astype(WIDE)
                    outs[-1][pl.ds(row, part), j * local : (j + 1) * local] = flat

    widths = (3 * width, width) if fused else (width, 2 * width, width)
    return call(
        kernel,
        tuple(shape((local, w), WIDE) for w in widths),
        spot,
        (own_piece, first_piece, last_pieces),
        piped=True,
    )


def widen_rows(value, tokens):
    rows, width = value.shape

    def kernel(spot_ref, x_ref, top_ref, rest_ref):
        top_ref[...] = x_ref[:tokens].astype(WIDE)
        rest_ref[...] = x_ref[tokens:].astype(WIDE)

    return call(
        kernel,
        (shape((tokens, width), WIDE), shape((rows - tokens, width), WIDE)),
        jnp.zeros((1,), jnp.int32),
        (value,),
    )


def sort_vectors(value, got):
    rows, width = value.shape
    order = (0, 3, 6, 9, 10, 2, 11, 12, 5, 8)

    def kernel(spot_ref, a_ref, b_ref, bias_ref, gain_ref, inner_ref):
        total = a_ref[...] + b_ref[...]
        for at, source in enumerate(order):
            bias_ref[at : at + 1] = total[source : source + 1]
        for at, source in enumerate((1, 4, 7)):
            gain_ref[at : at + 1] = total[source : source + 1]
        for at in range(4):
            inner_ref[at : at + 1] = total[13 + at : 14 + at]

    return call(
        kernel,
        (shape((10, width), WIDE), shape((3, width), WIDE), shape((4, width), WIDE)),
        jnp.zeros((1,), jnp.int32),
        (value, got),
    )


def exchange_sum(keep, send, bit, *holds):
    got = flip_ctx(send, bit)
    if holds:
        got = after(got, *holds)
    return keep + got.astype(WIDE)


def sum_rest(total, *holds):
    lines = lax.axis_size("ctx") // lax.axis_size("fsdp")
    for bit in powers(lax.axis_size("ctx")):
        if bit not in (1, lines):
            low = total.astype(LOW)
            total = low.astype(WIDE) + after(flip_ctx(low, bit), *holds).astype(WIDE)
    return total.astype(LOW)


def trade_columns(low):
    part = low.shape[1]
    local = 4 * part
    far = flip_model(low[2:], 2)
    near = flip_model(jnp.stack([low[1], far[1]]), 1)
    columns = jnp.stack([low[0], near[0], far[0], near[1]])
    return jnp.concatenate([columns[..., : 3 * local], low[..., 3 * local :]], axis=-1)


def gather_pieces(piece, bits, *holds):
    first = after(flip_ctx(piece, bits[0]), *holds)
    return piece, first, flip_ctx(jnp.stack([piece, first]), bits[1])


def move_columns(mate, cross, *holds):
    line = flip_ctx(after(cross, *holds), 1)
    return flip_model(mate, 1), cross, line, flip_model(cross, 1), flip_model(line, 1)


def core_sum(keep, send):
    mine = keep + flip_model(send, 1).astype(WIDE)
    return mine, flip_model(mine.astype(LOW), 2)


def sum_lines(value):
    for bit in reversed(line_bits()):
        value = value[:bit].astype(WIDE) + flip_ctx(value[bit:], bit).astype(WIDE)
        value = value.astype(LOW)
    return value[0]


def body(
    hidden,
    encoded,
    cotangent,
    dec_seg,
    enc_seg,
    self_qkv,
    self_out,
    cross_q,
    cross_kv,
    cross_out,
    ffn_in,
    ffn_out,
    biases,
    gains,
    ffn_bias,
):
    tokens = hidden.shape[1]
    rows = 4 * tokens
    width = hidden.shape[2]
    sources = encoded.shape[1]
    model = lax.axis_size("fsdp")
    lines = lax.axis_size("ctx") // model
    own = lax.axis_index("fsdp")
    ctx_index = lax.axis_index("ctx")
    local = width // model
    spot = jnp.stack([own, (ctx_index // lines) % 2, ctx_index % 2, ctx_index % lines])
    spot = spot.astype(jnp.int32)

    marks = jnp.concatenate([dec_seg[0], enc_seg[0]]).astype(LOW)
    marks = jnp.pad(marks, (0, width - tokens - sources))[None]
    block = jnp.concatenate([hidden[0], jnp.pad(marks, ((0, 15), (0, 0)))], axis=0)
    self_qkv = after(self_qkv, block)
    block = swap_places(block)
    small = jnp.concatenate([biases, gains, jnp.zeros((3, local), WIDE)], axis=0)
    qkv_own, qkv_mate, qkv_away = prepare_qkv(spot, self_qkv, small)
    qkv_cross = flip_model(qkv_away, 2)
    rest_own, rest_mate, rest_away, w_so, w_co, w_fo = prepare_rest(
        spot, cross_q, cross_kv, ffn_in, self_out, cross_out, ffn_out
    )
    block = after(block, rest_away)
    block_far = flip_model(block, 2)
    qkv_blocks = (qkv_own,) + move_columns(qkv_mate, qkv_cross, block)
    near_rows = jnp.stack([block, block_far])[None]
    near_rows = after(near_rows, qkv_blocks[3])
    rest_cross = flip_model(after(rest_away, block_far), 2)
    other = jnp.concatenate([cotangent[0], encoded[0]], axis=0)
    other = swap_places(after(other, block_far))
    for bit in line_bits():
        near_rows = jnp.concatenate([near_rows, flip_ctx(near_rows, bit)], axis=0)
    near_rows = after(near_rows, rest_cross, other)
    far_rows = flip_model(near_rows, 1)
    rest_blocks = (rest_own,) + move_columns(rest_mate, rest_cross, near_rows)

    inputs, queries, keys, values, w_q, w_kv, table, marks, emarks = project(
        spot, near_rows, far_rows, qkv_blocks, tokens, sources
    )
    other_far = flip_model(after(other, queries), 2)
    near_sources = jnp.stack([other[tokens:], other_far[tokens:]])[None]
    for bit in line_bits():
        near_sources = jnp.concatenate([near_sources, flip_ctx(near_sources, bit)], axis=0)
    far_sources = flip_model(near_sources, 1)
    plain = keys.shape[0] > 2048
    line_ids = (ctx_index % lines) ^ jnp.arange(lines, dtype=jnp.int32)[:, None]
    model_ids = own ^ jnp.array([0, 2, 1, 3], jnp.int32)[None, :]
    starts = (model_ids * lines + line_ids) * tokens
    places = (starts[:, :, None] + jnp.arange(tokens, dtype=jnp.int32)).reshape(-1)
    if plain:
        attended, keep, send = plain_forward(marks, places, queries, keys, values, w_so)
    else:
        attended, keep, send = self_forward(spot, marks, queries, keys, values, w_so, tokens)
    keep, send = after(keep, other_far), after(send, other_far)
    mine, away = core_sum(keep, send)
    w_cq, w_ckv, w_fi, source_rows, source_keys, source_values = arrange_rest(
        spot, rest_blocks, near_sources, far_sources, table
    )
    away = after(away, w_cq)
    first, first_low, first_normal, first_rate = residual_norm(inputs, mine, away, table, 5, 0)
    first_other = flip_model(first_low, 1)
    small_low = small.astype(LOW).astype(WIDE)
    cross_queries, crossed, keep, send, first_all = cross_forward(
        spot, marks, emarks, first_low, first_other, w_cq, source_keys, source_values, w_co, small_low, tokens
    )
    mine, away = core_sum(keep, send)
    second, second_low, second_normal, second_rate = residual_norm(first, mine, away, table, 8, 1)
    second_other = flip_model(second_low, 1)
    inner_bias = ffn_bias.astype(LOW).astype(WIDE)[None]
    activated, slope, keep, send = ffn_forward(second_low, second_other, w_fi, w_fo, inner_bias)
    mine, away = core_sum(keep, send)
    result, third_grad, ffn_low, third_sums = turn_around(
        second, mine, away, table, other, other_far, tokens
    )
    result = swap_places(result)
    output = result[None]

    ffn_other = flip_model(ffn_low, 1)
    inner_grad, keep, send, inner_sum = ffn_back(ffn_low, ffn_other, w_fo, w_fi, slope)
    mine, away = core_sum(keep, send)
    out_keep, out_send, in_keep, in_send = produce_ffn(
        spot, activated, ffn_low, ffn_other, second_low, second_other, inner_grad
    )
    away = after(away, in_keep, result)
    out_got = flip_ctx(out_send, 1)
    in_got = flip_ctx(in_send, lines)
    second_grad, cross_low, second_sums = residual_back(
        third_grad, mine, away, second_normal, second_rate, table, 1, tokens
    )
    cross_other = flip_model(cross_low, 1)
    cross_query_pre, source_grad, keep, send, cross_sums, cross_all = cross_back(
        spot, marks, emarks, cross_low, cross_other, w_co, cross_queries, source_keys, source_values, w_cq, tokens
    )
    keep, send = after(keep, out_got, in_got), after(send, out_got, in_got)
    mine, away = core_sum(keep, send)
    out_half = out_keep + after(out_got, mine).astype(WIDE)
    in_half = in_keep + after(in_got, mine).astype(WIDE)
    out_got = flip_ctx(out_half[1].astype(LOW), lines)
    in_got = flip_ctx(in_half[1].astype(LOW), 1)
    cross_keep, cross_send = produce_mixed(
        spot, first_all, cross_query_pre, source_rows, source_grad, crossed, (cross_all,)
    )
    away = after(away, cross_keep, out_got, in_got)
    first_grad, self_low, first_sums = residual_back(
        second_grad, mine, away, first_normal, first_rate, table, 0, tokens
    )
    self_other = flip_model(self_low, 1)
    cross_got = flip_ctx(cross_send, 1)
    ffn_total = join_ffn(out_half, after(out_got, self_low), in_half, after(in_got, self_low))
    self_low = after(self_low, ffn_total)
    if plain:
        self_query_pre, pair_grad, self_sums = plain_back(
            marks, places, self_low, self_other, w_so, queries, keys, values
        )
    else:
        self_query_pre, pair_grad, self_sums = self_back(
            spot, marks, self_low, self_other, w_so, queries, keys, values, tokens
        )
    self_keep, self_send = produce_mixed(
        spot, inputs, self_query_pre, inputs, pair_grad, attended, (self_low, self_other)
    )
    wide_rows = jnp.concatenate([first_sums, second_sums, third_sums], axis=0)
    wide_rows = wide_rows + after(flip_model(wide_rows, 1), self_keep)
    wide_rows = lax.dynamic_slice_in_dim(wide_rows, own * local, local, axis=1)
    vectors = jnp.concatenate(
        [wide_rows, self_sums, after(cross_sums, self_keep), after(inner_sum, self_keep).reshape(-1, local)], axis=0
    )
    vectors = jnp.pad(vectors, ((0, 32 - vectors.shape[0]), (0, 0))).reshape(16, 2 * local)
    self_half = exchange_sum(self_keep, self_send, 1)
    cross_half = cross_keep + after(cross_got, self_keep).astype(WIDE)
    cross_total = exchange_sum(cross_half[0], cross_half[1].astype(LOW), lines, self_half)
    ffn_total = sum_rest(ffn_total, self_half)
    lined = jnp.concatenate(
        [
            pair_grad.reshape(lines, rows, 2 * local),
            source_grad.reshape(lines, 4 * sources, 2 * local),
            jnp.broadcast_to(vectors.astype(LOW)[None], (lines,) + vectors.shape),
        ],
        axis=1,
    )
    lined = sum_lines(after(lined, self_half))
    pair_own = lined[:rows]
    source_own = lined[rows : rows + 4 * sources]
    vectors = lined[rows + 4 * sources :].astype(WIDE)
    keep, send = input_back(
        self_query_pre, pair_own, source_own, w_q, w_kv, w_ckv, tokens, sources
    )
    both_half = keep + flip_model(send, 1).astype(WIDE)
    span = tokens + sources
    both = both_half[:span] + flip_model(both_half[span:].astype(LOW), 2).astype(WIDE)
    both = jnp.concatenate([both[:tokens] + first_grad[:tokens], both[tokens:]], axis=0)
    both = both.astype(LOW)
    hidden_grad, encoded_grad = widen_rows(swap_places(both), tokens)
    hidden_grad = hidden_grad[None]
    encoded_grad = encoded_grad[None]

    cross_total = after(cross_total, ffn_total)
    self_total = exchange_sum(self_half[0], self_half[1].astype(LOW), lines, lined, cross_total)
    ffn_far = flip_model(ffn_total[1, 2:], 2)
    ffn_near = flip_model(jnp.stack([ffn_total[1, 1], ffn_far[1]]), 1)
    ffn_piece = jnp.stack([ffn_total[1, 0], ffn_near[0], ffn_far[0], ffn_near[1]])
    out_pieces = gather_pieces(ffn_total[0], (lines, 1))
    in_pieces = gather_pieces(ffn_piece, (1, lines))
    cross_piece = sum_rest(cross_total, self_total)
    self_piece = sum_rest(self_total, out_pieces[1], in_pieces[1])
    self_traded = trade_columns(self_piece)
    self_pieces = gather_pieces(self_traded, (lines, 1))
    cross_pieces = gather_pieces(trade_columns(cross_piece), (1, lines), self_traded)
    vectors = vectors.reshape(-1, local)
    bits = powers(lax.axis_size("ctx"))[len(line_bits()) :]
    for bit in bits[:-1]:
        vectors = vectors + after(flip_ctx(vectors, bit), self_piece)
    d_bias, d_gain, d_inner = sort_vectors(vectors, after(flip_ctx(vectors, bits[-1]), self_pieces[1]))
    d_inner = d_inner.reshape(-1)
    g_cq, g_ckv, g_co = finish_mixed(spot, *cross_pieces, False)
    g_fo, g_fi = finish_ffn(spot, out_pieces, in_pieces)
    last = after(self_pieces[2], g_fi, g_cq, d_bias, hidden_grad)
    g_qkv, g_so = finish_mixed(spot, self_pieces[0], self_pieces[1], last, True)
    return (
        output,
        hidden_grad,
        encoded_grad,
        g_qkv,
        g_so,
        g_cq,
        g_ckv,
        g_co,
        g_fi,
        g_fo,
        d_bias,
        d_gain,
        d_inner,
    )


def solution(mesh):
    whole = P("fsdp", "ctx", None)
    matrix = P("fsdp", None)
    ids = P("fsdp", "ctx")
    table = P(None, "fsdp")
    return jax.shard_map(
        body,
        mesh=mesh,
        in_specs=(whole, whole, whole, ids, ids) + (matrix,) * 7 + (table, table, P("fsdp")),
        out_specs=(whole,) * 3 + (matrix,) * 7 + (table, table, P("fsdp")),
        check_vma=False,
    )
```

```python
import jax
import jax.numpy as jnp
from jax import lax
from jax.experimental import pallas as pl
from jax.experimental.pallas import tpu as pltpu
from jax.sharding import PartitionSpec as P

H = 12
HD = 64
EPSILON = 1e-05
FLOOR_SCORE = -1e30
SCALE = float(HD) ** (-0.5)
LOW = jnp.bfloat16
WIDE = jnp.float32


def mm(left, right):
    return jnp.dot(left, right, preferred_element_type=WIDE)


def mm_tn(left, right):
    return lax.dot_general(left, right, (((0,), (0,)), ((), ())), preferred_element_type=WIDE)


def mm_nt(left, right):
    return lax.dot_general(left, right, (((1,), (1,)), ((), ())), preferred_element_type=WIDE)


def flip_model(value, bit):
    count = lax.axis_size("fsdp")
    return lax.ppermute(value, "fsdp", [(i, i ^ bit) for i in range(count)])


def flip_ctx(value, bit):
    count = lax.axis_size("ctx")
    return lax.ppermute(value, "ctx", [(i, i ^ bit) for i in range(count)])


def swap_places(value):
    model = lax.axis_size("fsdp")
    ctx = lax.axis_size("ctx")
    lines = ctx // model
    route = []
    for f in range(model):
        for z in range(model):
            for r in range(lines):
                route.append((f * ctx + z * lines + r, z * ctx + f * lines + r))
    return lax.ppermute(value, ("fsdp", "ctx"), route)


def powers(limit):
    bits = []
    bit = 1
    while bit < limit:
        bits.append(bit)
        bit *= 2
    return bits


def line_bits():
    return powers(lax.axis_size("ctx") // lax.axis_size("fsdp"))


def after(value, *others):
    return lax.optimization_barrier((value,) + others)[0]


def shape(dims, kind):
    return jax.ShapeDtypeStruct(tuple(dims), kind)


COST = 5.0


def cost(flops, *arrays):
    count = 0
    for array in arrays:
        count += array.size * array.dtype.itemsize
    return pl.CostEstimate(
        flops=int(flops * COST), transcendentals=0, bytes_accessed=int(count * COST)
    )


def call(kernel, outs, spot, operands, flops=0, scratch=(), limit=12, piped=False, cold=(), parked=(), saved=()):
    many = isinstance(outs, tuple)
    listed = list(outs) if many else [outs]
    count = len(operands)
    if saved:
        first = operands[saved[0]]
        height = sum(operands[at].shape[0] for at in saved)
        listed.append(shape((height,) + first.shape[1:], first.dtype))
        many = True
    body = kernel
    if cold or parked or saved:
        place = pl.BlockSpec(memory_space=pltpu.VMEM)
        far = pl.BlockSpec(memory_space=pltpu.HBM)
        own = count + len(listed) + len(scratch)

        def body(spot_ref, *all_refs):
            refs, buffers, done = list(all_refs[:own]), list(all_refs[own:-1]), all_refs[-1]
            used = 0
            ending = []

            def copy(source, target):
                nonlocal used
                moving = pltpu.make_async_copy(source, target, done.at[used])
                used += 1
                return moving

            incoming = []
            for at in cold:
                buffer = buffers.pop(0)
                incoming.append(copy(refs[at], buffer))
                incoming[-1].start()
                refs[at] = buffer
            row = 0
            for at in saved:
                target = refs[count + len(listed) - 1].at[pl.ds(row, operands[at].shape[0])]
                row += operands[at].shape[0]
                ending.append(copy(refs[at], target))
                ending[-1].start()
            for moving in incoming:
                moving.wait()
            outgoing = []
            for at in parked:
                buffer = buffers.pop(0)
                outgoing.append(copy(buffer, refs[count + at]))
                refs[count + at] = buffer
            if saved:
                refs.pop(count + len(listed) - 1)
            kernel(spot_ref, *refs)
            for moving in outgoing:
                moving.start()
            for moving in outgoing + ending:
                moving.wait()

        buffers = [pltpu.VMEM(operands[at].shape, operands[at].dtype) for at in cold]
        buffers += [pltpu.VMEM(listed[at].shape, listed[at].dtype) for at in parked]
        held = set(parked) | ({len(listed) - 1} if saved else set())
        out_specs = [far if at in held else place for at in range(len(listed))]
        moves = len(cold) + len(parked) + len(saved)
        spec = dict(
            in_specs=[pl.BlockSpec(memory_space=pltpu.SMEM)]
            + [far if at in cold else place for at in range(count)],
            out_specs=tuple(out_specs) if many else out_specs[0],
            scratch_shapes=list(scratch) + buffers + [pltpu.SemaphoreType.DMA((moves,))],
        )
        limit = limit + 8
    elif piped:
        place = lambda value: pl.BlockSpec(value.shape, lambda i, spot: (0,) * len(value.shape))
        spec = dict(
            grid_spec=pltpu.PrefetchScalarGridSpec(
                num_scalar_prefetch=1,
                grid=(1,),
                in_specs=[place(value) for value in operands],
                out_specs=tuple(place(value) for value in listed) if many else place(outs),
                scratch_shapes=list(scratch),
            )
        )
        limit = limit + 12
    else:
        place = pl.BlockSpec(memory_space=pltpu.VMEM)
        spec = dict(
            in_specs=[pl.BlockSpec(memory_space=pltpu.SMEM)] + [place] * count,
            out_specs=tuple(place for _ in listed) if many else place,
            scratch_shapes=list(scratch),
        )
    return pl.pallas_call(
        body,
        out_shape=tuple(listed) if many else outs,
        cost_estimate=cost(flops, *operands, *listed),
        compiler_params=pltpu.CompilerParams(vmem_limit_bytes=limit << 20),
        **spec,
    )(spot, *operands)


def pack_rows(tokens, sources, token_marks, source_marks):
    count, width = tokens.shape
    more = sources.shape[0]

    def kernel(spot_ref, x_ref, e_ref, m_ref, s_ref, out_ref):
        out_ref[:count] = x_ref[...]
        out_ref[count : count + more] = e_ref[...]
        out_ref[count + more :] = jnp.zeros((16, width), LOW)
        first = jnp.broadcast_to(m_ref[...], (16, count)).astype(WIDE).astype(LOW)
        second = jnp.broadcast_to(s_ref[...], (16, more)).astype(WIDE).astype(LOW)
        out_ref[count + more :, :count] = first
        out_ref[count + more :, count : count + more] = second

    return call(
        kernel,
        shape((count + more + 16, width), LOW),
        jnp.zeros((1,), jnp.int32),
        (tokens, sources, token_marks, source_marks),
        piped=True,
    )


def prepare_qkv(spot, weight, small):
    rows = weight.shape[0]

    def kernel(spot_ref, w_ref, small_ref, own_ref, near_ref, far_ref, all_ref):
        me = spot_ref[0]
        side = spot_ref[2]
        small = small_ref[...].astype(LOW)
        tail = jnp.zeros((16, 2 * rows), LOW)
        for d in range(4):
            for p in range(3):
                piece = w_ref[:, p * 4 * rows + d * rows : p * 4 * rows + (d + 1) * rows]
                all_ref[me ^ d, :, p * rows : (p + 1) * rows] = piece.astype(LOW)
        own_ref[:rows] = all_ref[0]
        near_ref[:rows] = all_ref[1]
        far_ref[:rows] = all_ref[2 + side]
        for ref in (own_ref, near_ref, far_ref):
            ref[rows:, :rows] = small
            ref[rows:, rows:] = tail

    piece = (rows + 16, 3 * rows)
    return call(
        kernel,
        (shape(piece, LOW),) * 3,
        spot,
        (weight, small),
        scratch=[pltpu.VMEM((4, rows, 3 * rows), LOW)],
    )


def prepare_rest(spot, cross_q, cross_kv, ffn_in, self_out, cross_out, ffn_out):
    rows = cross_q.shape[0]
    wide = ffn_in.shape[1] // 4
    piece = (rows, 3 * rows + wide)

    def kernel(spot_ref, q_ref, kv_ref, fi_ref, so_ref, co_ref, fo_ref, *outs):
        own_ref, near_ref, far_ref, so_out, co_out, fo_out, all_ref = outs
        me = spot_ref[0]
        side = spot_ref[2]
        for d in range(4):
            all_ref[me ^ d, :, :rows] = q_ref[:, d * rows : (d + 1) * rows].astype(LOW)
            for p in range(2):
                part = kv_ref[:, (p * 4 + d) * rows : (p * 4 + d + 1) * rows]
                all_ref[me ^ d, :, (1 + p) * rows : (2 + p) * rows] = part.astype(LOW)
            all_ref[me ^ d, :, 3 * rows :] = fi_ref[:, d * wide : (d + 1) * wide].astype(LOW)
        own_ref[...] = all_ref[0]
        near_ref[...] = all_ref[1]
        far_ref[...] = all_ref[2 + side]
        so_out[...] = so_ref[...].astype(LOW)
        co_out[...] = co_ref[...].astype(LOW)
        fo_out[...] = fo_ref[...].astype(LOW)

    return call(
        kernel,
        (shape(piece, LOW),) * 3
        + (shape(self_out.shape, LOW), shape(cross_out.shape, LOW), shape(ffn_out.shape, LOW)),
        spot,
        (cross_q, cross_kv, ffn_in, self_out, cross_out, ffn_out),
        scratch=[pltpu.VMEM((4,) + piece, LOW)],
        limit=16,
        piped=True,
    )


def ordered_blocks(spot_ref, refs, pair_ref):
    side = spot_ref[2]
    pair_ref[0, side] = refs[2][...]
    pair_ref[0, 1 - side] = refs[3][...]
    pair_ref[1, side] = refs[4][...]
    pair_ref[1, 1 - side] = refs[5][...]
    return refs[0][...], refs[1][...], pair_ref[0, 0], pair_ref[1, 1]


def arrange_rest(spot, blocks, source_rows, table):
    rows = blocks[0].shape[0]
    wide = blocks[0].shape[1] - 3 * rows
    count, width = source_rows.shape

    def kernel(spot_ref, *refs):
        x_ref, table_ref, q_ref, kv_ref, fi_ref, *outs = refs[6:]
        keys_ref, values_ref, rel_ref, pair_ref = outs
        me = spot_ref[0]
        parts = ordered_blocks(spot_ref, refs[:6], pair_ref)
        for k in range(4):
            start = pl.multiple_of((me ^ k) * rows, 64)
            q_ref[pl.ds(start, rows), :] = parts[k][:, :rows]
            kv_ref[pl.ds(start, rows), :] = parts[k][:, rows : 3 * rows]
            fi_ref[pl.ds(start, rows), :] = parts[k][:, 3 * rows :]
        for j in range(4):
            rel_ref[j] = table_ref[:, j * rows : (j + 1) * rows]
        shift = rel_ref[me][7:8]
        out = mm(x_ref[...], kv_ref[...])
        keys_ref[...] = out[:, :rows].astype(LOW)
        values_ref[...] = (out[:, rows:] + shift).astype(LOW)

    return call(
        kernel,
        (
            shape((4 * rows, rows), LOW),
            shape((4 * rows, 2 * rows), LOW),
            shape((4 * rows, wide), LOW),
            shape((count, rows), LOW),
            shape((count, rows), LOW),
        ),
        spot,
        tuple(blocks) + (source_rows, table),
        flops=4 * count * width * rows,
        scratch=[pltpu.VMEM((4, 16, rows), WIDE), pltpu.VMEM((2, 2) + blocks[0].shape, LOW)],
        limit=16,
    )


def project(spot, near_rows, far_rows, blocks, tokens, sources):
    lines = near_rows.shape[0]
    width = near_rows.shape[-1]
    local = width // 4
    span = near_rows.shape[2]
    rows = 4 * tokens

    def kernel(spot_ref, a_ref, b_ref, *refs):
        x_ref, e_ref, q_ref, k_ref, v_ref, wq_ref, wkv_ref, table_ref, *outs = refs[6:]
        marks_ref, emarks_ref, rel_ref, w_ref, pair_ref = outs
        me = spot_ref[0]

        @pl.when(pl.program_id(0) == 0)
        def _():
            parts = ordered_blocks(spot_ref, refs[:6], pair_ref)
            for k in range(4):
                start = pl.multiple_of((me ^ k) * local, 64)
                w_ref[pl.ds(start, local), :] = parts[k][:local]
                rel_ref[k] = parts[k][local:, :local].astype(WIDE)
            for j in range(4):
                table_ref[:, j * local : (j + 1) * local] = rel_ref[me ^ j]
            wq_ref[...] = w_ref[:, :local]
            wkv_ref[...] = w_ref[:, local:]

        lane = lax.broadcasted_iota(jnp.int32, (1, 128), 1)
        emarks = jnp.zeros((1, 128), WIDE)
        for kc, ref in enumerate((a_ref, b_ref)):
            for kx in range(2):
                at = 2 * kc + kx
                start = at * tokens
                x_ref[start : start + tokens, :] = ref[0, kx, :tokens, :]
                e_ref[at * sources : (at + 1) * sources, :] = ref[0, kx, tokens : tokens + sources, :]
                marks = ref[0, kx, tokens + sources : tokens + sources + 16, :256].astype(WIDE)
                marks_ref[:, start : start + tokens] = marks[0:1, :tokens]
                moved = pltpu.roll(marks[:8, 128:], at * sources, 1)[0:1]
                emarks = emarks + jnp.where((lane // sources) == at, moved, 0.0)
        emarks_ref[...] = emarks
        own_small = rel_ref[0]
        out = mm(x_ref[...], w_ref[...])
        k_ref[...] = out[:, local : 2 * local].astype(LOW)
        v_ref[...] = (out[:, 2 * local :] + own_small[4:5]).astype(LOW)

        @pl.when(pl.program_id(0) == 0)
        def _():
            q_ref[...] = ((out[:, :local] + own_small[3:4]) * SCALE).astype(LOW)

    full = lambda *dims: pl.BlockSpec(dims, lambda i, spot: (0,) * len(dims))
    band = lambda w: pl.BlockSpec((rows, w), lambda i, spot: (i, 0))
    part = pl.BlockSpec((1, 2, span, width), lambda i, spot: (i, 0, 0, 0))
    piece = (local + 16, 3 * local)
    outs = (
        shape((lines * rows, width), LOW),
        shape((lines * 4 * sources, width), LOW),
        shape((rows, local), LOW),
        shape((lines * rows, local), LOW),
        shape((lines * rows, local), LOW),
        shape((width, local), LOW),
        shape((width, 2 * local), LOW),
        shape((16, width), WIDE),
        shape((1, lines * rows), WIDE),
        shape((1, lines * 4 * sources), WIDE),
    )
    operands = (near_rows, far_rows) + tuple(blocks)
    return pl.pallas_call(
        kernel,
        out_shape=outs,
        grid_spec=pltpu.PrefetchScalarGridSpec(
            num_scalar_prefetch=1,
            grid=(lines,),
            in_specs=[part, part] + [full(*piece)] * 6,
            out_specs=(
                band(width),
                pl.BlockSpec((4 * sources, width), lambda i, spot: (i, 0)),
                full(rows, local),
                band(local),
                band(local),
                full(width, local),
                full(width, 2 * local),
                full(16, width),
                pl.BlockSpec((1, rows), lambda i, spot: (0, i)),
                pl.BlockSpec((1, 4 * sources), lambda i, spot: (0, i)),
            ),
            scratch_shapes=[
                pltpu.VMEM((4, 16, local), WIDE),
                pltpu.VMEM((width, 3 * local), LOW),
                pltpu.VMEM((2, 2) + piece, LOW),
            ],
        ),
        cost_estimate=cost(6 * lines * rows * width * local, *operands, *outs),
        compiler_params=pltpu.CompilerParams(vmem_limit_bytes=20 << 20),
    )(spot, *operands)


def block_start(spot_ref, index, tokens, lines):
    me = spot_ref[0]
    line = spot_ref[3]
    kr, kc, kx = index // 4, (index // 2) % 2, index % 2
    return ((me ^ (kc + 2 * kx)) * lines + (line ^ kr)) * tokens


def upright(row):
    return jnp.transpose(jnp.broadcast_to(row, (128, row.shape[1])))


def self_floor(spot_ref, marks_ref, query_blocks, tokens, turned):
    blocks = marks_ref.shape[1] // tokens
    lines = blocks // 4
    down = lax.broadcasted_iota(jnp.int32, (tokens, tokens), 0)
    right = lax.broadcasted_iota(jnp.int32, (tokens, tokens), 1)
    outer, inner = (range(blocks), query_blocks) if turned else (query_blocks, range(blocks))
    table = []
    for i in outer:
        tall = upright(marks_ref[:, i * tokens : (i + 1) * tokens])
        line = []
        for j in inner:
            flat = marks_ref[:, j * tokens : (j + 1) * tokens]
            gap = block_start(spot_ref, j, tokens, lines) - block_start(spot_ref, i, tokens, lines)
            ahead = (right + gap) - down
            near = (ahead >= 0) if turned else (ahead <= 0)
            line.append(jnp.where((tall == flat) & near, 0.0, FLOOR_SCORE))
        table.append(jnp.concatenate(line, axis=1))
    return jnp.concatenate(table, axis=0)


def head_lanes(value, head):
    lane = lax.broadcasted_iota(jnp.int32, (1, value.shape[1]), 1) // HD
    return jnp.where(lane == head, value, jnp.zeros_like(value))


def attend_rows(queries, keys, values, floor):
    heads = queries.shape[1] // HD
    total = None
    for h in range(heads):
        scores = mm_nt(head_lanes(queries, h), keys) + floor
        top = jnp.max(scores, axis=1, keepdims=True)
        weights = jnp.exp(scores - top)
        prob = weights / jnp.sum(weights, axis=1, keepdims=True)
        part = head_lanes(mm(prob.astype(LOW), values), h)
        total = part if total is None else total + part
    return total.astype(LOW)


def attend_rows_back(queries, keys, values, grads, floor):
    heads = queries.shape[1] // HD
    query_grad = key_grad = value_grad = None
    for h in range(heads):
        own_queries = head_lanes(queries, h)
        own_grads = head_lanes(grads, h)
        scores = mm_nt(keys, own_queries) + floor
        top = jnp.max(scores, axis=0, keepdims=True)
        weights = jnp.exp(scores - top)
        prob = weights / jnp.sum(weights, axis=0, keepdims=True)
        prob_grad = mm_nt(values, own_grads)
        inner = jnp.sum(prob * prob_grad, axis=0, keepdims=True)
        score_grad = (prob * (prob_grad - inner)).astype(LOW)
        part_q = head_lanes(mm_tn(score_grad, keys), h)
        part_k = mm(score_grad, own_queries)
        part_v = mm(prob.astype(LOW), own_grads)
        query_grad = part_q if query_grad is None else query_grad + part_q
        key_grad = part_k if key_grad is None else key_grad + part_k
        value_grad = part_v if value_grad is None else value_grad + part_v
    return query_grad, key_grad, value_grad


def block_rows(keys):
    return 256 if keys <= 1024 else 128


def self_forward(spot, marks, queries, keys, values, weight, tokens):
    rows, local = queries.shape
    width = weight.shape[1]
    size = block_rows(keys.shape[0])

    def kernel(spot_ref, marks_ref, q_ref, k_ref, v_ref, w_ref, o_ref, keep_ref, send_ref):
        for begin in range(0, rows, size):
            blocks = range(begin // tokens, (begin + size) // tokens)
            floor = self_floor(spot_ref, marks_ref, blocks, tokens, False)
            low = attend_rows(q_ref[begin : begin + size], k_ref[...], v_ref[...], floor)
            o_ref[begin : begin + size] = low
            part = mm(low, w_ref[...])
            if begin < rows // 2:
                keep_ref[begin : begin + size] = part
            else:
                send_ref[begin - rows // 2 : begin - rows // 2 + size] = part.astype(LOW)

    return call(
        kernel,
        (shape((rows, local), LOW), shape((rows // 2, width), WIDE), shape((rows // 2, width), LOW)),
        spot,
        (marks, queries, keys, values, weight),
        flops=4 * rows * keys.size + 2 * rows * weight.size,
        limit=20,
    )


def plain_floor(marks, places, rows):
    same = marks.reshape(-1)[:rows, None] == marks
    return jnp.where(same & (places[None, :] <= places[:rows, None]), 0.0, FLOOR_SCORE)


def plain_forward(marks, places, queries, keys, values, weight):
    rows = queries.shape[0]
    low = attend_rows(queries, keys, values, plain_floor(marks, places, rows))
    part = mm(low, weight)
    return low, part[: rows // 2], part[rows // 2 :].astype(LOW)


def plain_back(marks, places, low, other, w_so, queries, keys, values):
    grads = mm_nt(jnp.concatenate([low, other], axis=0), w_so).astype(LOW)
    floor = plain_floor(marks, places, queries.shape[0])
    dq, dk, dv = attend_rows_back(queries, keys, values, grads, floor.T)
    pre = (dq.astype(LOW).astype(WIDE) * SCALE).astype(LOW)
    sums = jnp.concatenate(column_rows(pre, dv), axis=0)
    return pre, jnp.concatenate([dk, dv], axis=1).astype(LOW), sums


def norm_rows(values):
    center = values - jnp.mean(values, axis=-1, keepdims=True)
    spread = jnp.mean(center * center, axis=-1, keepdims=True)
    rate = lax.rsqrt(spread + EPSILON)
    return center * rate, rate


def turned_halves(ref):
    half = ref.shape[0] // 2
    return jnp.concatenate([ref[half:], ref[:half]], axis=0).astype(WIDE)


def residual_norm(residual, mine, other, table, bias_row, norm_row):
    rows, width = mine.shape

    def kernel(spot_ref, r_ref, mine_ref, other_ref, table_ref, h_ref, low_ref, n_ref, rate_ref):
        total = r_ref[:rows].astype(WIDE) + mine_ref[...] + turned_halves(other_ref)
        normal, rate = norm_rows(total + table_ref[bias_row : bias_row + 1])
        gain = table_ref[10 + norm_row : 11 + norm_row]
        result = normal * gain + table_ref[norm_row : norm_row + 1]
        h_ref[...] = result
        low_ref[...] = result.astype(LOW)
        n_ref[...] = normal
        rate_ref[...] = rate

    return call(
        kernel,
        (
            shape((rows, width), WIDE),
            shape((rows, width), LOW),
            shape((rows, width), WIDE),
            shape((rows, 1), WIDE),
        ),
        jnp.zeros((1,), jnp.int32),
        (residual, mine, other, table),
    )


def cross_forward(spot, marks, emarks, low, other, w_cq, keys, values, w_co, small, tokens):
    half, width = low.shape
    local = w_cq.shape[1]

    def kernel(spot_ref, marks_ref, emarks_ref, a_ref, b_ref, w_ref, k_ref, v_ref, o_ref, small_ref, *outs):
        q_out, c_out, keep_ref, send_ref = outs
        for place, ref in enumerate((a_ref, b_ref)):
            at = slice(place * half, (place + 1) * half)
            low = ((mm(ref[...], w_ref[...]) + small_ref[6:7]) * SCALE).astype(LOW)
            q_out[at] = low
            tall = []
            for i in range(place * half // tokens, (place + 1) * half // tokens):
                tall.append(upright(marks_ref[:, i * tokens : (i + 1) * tokens])[:, :1])
            tall = jnp.concatenate(tall, axis=0)
            floor = jnp.where(tall == emarks_ref[...], 0.0, FLOOR_SCORE)
            crossed = attend_rows(low, k_ref[...], v_ref[...], floor)
            c_out[at] = crossed
            part = mm(crossed, o_ref[...])
            if place == 0:
                keep_ref[...] = part
            else:
                send_ref[...] = part.astype(LOW)

    return call(
        kernel,
        (
            shape((2 * half, local), LOW),
            shape((2 * half, local), LOW),
            shape((half, width), WIDE),
            shape((half, width), LOW),
        ),
        spot,
        (marks, emarks, low, other, w_cq, keys, values, w_co, small),
        flops=8 * half * width * local,
        limit=16,
        parked=(1,),
        saved=(2, 3),
    )


def ffn_forward(low, other, w_fi, w_fo, shift):
    half, width = low.shape
    wide = w_fi.shape[1]

    def kernel(spot_ref, a_ref, b_ref, w_ref, o_ref, shift_ref, g_ref, slope_ref, keep_ref, send_ref):
        for place, ref in enumerate((a_ref, b_ref)):
            at = slice(place * half, (place + 1) * half)
            pre = mm(ref[...], w_ref[...]) + shift_ref[...]
            bell = 0.5 * (1.0 + lax.erf(pre * (0.5**0.5)))
            act = (pre * bell).astype(LOW)
            g_ref[at] = act
            slope_ref[at] = bell + pre * jnp.exp(-0.5 * pre * pre) * 0.3989422804014327
            part = mm(act, o_ref[...])
            if place == 0:
                keep_ref[...] = part
            else:
                send_ref[...] = part.astype(LOW)

    return call(
        kernel,
        (
            shape((2 * half, wide), LOW),
            shape((2 * half, wide), WIDE),
            shape((half, width), WIDE),
            shape((half, width), LOW),
        ),
        jnp.zeros((1,), jnp.int32),
        (low, other, w_fi, w_fo, shift),
        flops=8 * half * width * wide,
    )


def norm_back(grad, normal, rate, gain):
    up = grad * gain
    mean_up = jnp.mean(up, axis=-1, keepdims=True)
    mean_both = jnp.mean(up * normal, axis=-1, keepdims=True)
    return rate * (up - mean_up - normal * mean_both)


def column_rows(*values):
    rows = [jnp.sum(value.astype(WIDE), axis=0, keepdims=True) for value in values]
    return rows


def turn_around(residual, mine, other, table, own_grad, other_grad, tokens):
    rows, width = mine.shape

    def kernel(spot_ref, r_ref, mine_ref, other_ref, table_ref, a_ref, b_ref, out_ref, d_ref, low_ref, sum_ref):
        total = r_ref[...] + mine_ref[...] + turned_halves(other_ref) + table_ref[9:10]
        normal, rate = norm_rows(total)
        gain = table_ref[12:13]
        out_ref[...] = (normal[:tokens] * gain + table_ref[2:3]).astype(LOW)
        grad = jnp.concatenate([a_ref[:tokens], b_ref[:tokens]], axis=0).astype(WIDE)
        back = norm_back(grad, normal, rate, gain)
        low = back.astype(LOW)
        d_ref[...] = back
        low_ref[...] = low
        rows = column_rows(grad, grad * normal, low)
        for i in range(3):
            sum_ref[i : i + 1] = rows[i]

    return call(
        kernel,
        (
            shape((tokens, width), LOW),
            shape((rows, width), WIDE),
            shape((rows, width), LOW),
            shape((3, width), WIDE),
        ),
        jnp.zeros((1,), jnp.int32),
        (residual, mine, other, table, own_grad, other_grad),
        piped=True,
    )


def residual_back(previous, mine, other, normal, rate, table, norm_row, tokens):
    rows, width = mine.shape

    def kernel(spot_ref, p_ref, mine_ref, other_ref, n_ref, rate_ref, table_ref, d_ref, low_ref, sum_ref):
        grad = p_ref[...] + mine_ref[...] + turned_halves(other_ref)
        normal = n_ref[...]
        back = norm_back(grad, normal, rate_ref[...], table_ref[10 + norm_row : 11 + norm_row])
        low = back.astype(LOW)
        d_ref[...] = back
        low_ref[...] = low
        rows = column_rows(grad, grad * normal, low)
        for i in range(3):
            sum_ref[i : i + 1] = rows[i]

    return call(
        kernel,
        (shape((rows, width), WIDE), shape((rows, width), LOW), shape((3, width), WIDE)),
        jnp.zeros((1,), jnp.int32),
        (previous, mine, other, normal, rate, table),
    )


def ffn_back(low, other, w_fo, w_fi, slope):
    half, width = low.shape
    wide = w_fi.shape[1]

    def kernel(spot_ref, a_ref, b_ref, o_ref, w_ref, slope_ref, u_ref, keep_ref, send_ref, sum_ref):
        total = None
        for place, ref in enumerate((a_ref, b_ref)):
            at = slice(place * half, (place + 1) * half)
            inner = (mm_nt(ref[...], o_ref[...]) * slope_ref[at]).astype(LOW)
            u_ref[at] = inner
            row = column_rows(inner)[0]
            total = row if total is None else total + row
            part = mm_nt(inner, w_ref[...])
            if place == 0:
                keep_ref[...] = part
            else:
                send_ref[...] = part.astype(LOW)
        sum_ref[...] = total

    return call(
        kernel,
        (
            shape((2 * half, wide), LOW),
            shape((half, width), WIDE),
            shape((half, width), LOW),
            shape((1, wide), WIDE),
        ),
        jnp.zeros((1,), jnp.int32),
        (low, other, w_fo, w_fi, slope),
        flops=8 * half * width * wide,
        piped=True,
    )


def cross_back(spot, marks, emarks, low, other, w_co, queries, keys, values, w_cq, tokens):
    half, width = low.shape
    count, local = keys.shape

    def kernel(spot_ref, marks_ref, emarks_ref, a_ref, b_ref, co_ref, q_ref, k_ref, v_ref, cq_ref, *outs):
        dq_ref, dkv_ref, keep_ref, send_ref, sum_ref = outs
        key_grad = value_grad = None
        tall = []
        for i in range(count // 128):
            tall.append(upright(emarks_ref[:, i * 128 : (i + 1) * 128])[:, :1])
        tall = jnp.concatenate(tall, axis=0)
        totals = None
        for place, ref in enumerate((a_ref, b_ref)):
            at = slice(place * half, (place + 1) * half)
            grads = mm_nt(ref[...], co_ref[...]).astype(LOW)
            floor = jnp.where(tall == marks_ref[:, at], 0.0, FLOOR_SCORE)
            dq, dk, dv = attend_rows_back(q_ref[at], k_ref[...], v_ref[...], grads, floor)
            pre = (dq.astype(LOW).astype(WIDE) * SCALE).astype(LOW)
            dq_ref[at] = pre
            key_grad = dk if key_grad is None else key_grad + dk
            value_grad = dv if value_grad is None else value_grad + dv
            row = column_rows(pre)[0]
            totals = row if totals is None else totals + row
            part = mm_nt(pre, cq_ref[...])
            if place == 0:
                keep_ref[...] = part
            else:
                send_ref[...] = part.astype(LOW)
        dkv_ref[:, :local] = key_grad.astype(LOW)
        dkv_ref[:, local:] = value_grad.astype(LOW)
        sum_ref[0:1] = totals
        sum_ref[1:2] = column_rows(value_grad)[0]

    return call(
        kernel,
        (
            shape((2 * half, local), LOW),
            shape((count, 2 * local), LOW),
            shape((half, width), WIDE),
            shape((half, width), LOW),
            shape((2, local), WIDE),
        ),
        spot,
        (marks, emarks, low, other, w_co, queries, keys, values, w_cq),
        flops=8 * half * width * local,
        limit=16,
        cold=(4, 5, 6, 7, 8),
        saved=(2, 3),
    )


def self_back(spot, marks, low, other, w_so, queries, keys, values, tokens):
    half, width = low.shape
    count, local = keys.shape
    rows = 2 * half
    size = block_rows(count)

    def kernel(spot_ref, marks_ref, a_ref, b_ref, so_ref, q_ref, k_ref, v_ref, dq_ref, dkv_ref, sum_ref, dk_ref, dv_ref):
        totals = None
        for begin in range(0, rows, size):
            source = a_ref if begin < half else b_ref
            local_at = begin % half
            grads = mm_nt(source[local_at : local_at + size], so_ref[...]).astype(LOW)
            blocks = range(begin // tokens, (begin + size) // tokens)
            floor = self_floor(spot_ref, marks_ref, blocks, tokens, True)
            at = slice(begin, begin + size)
            dq, dk, dv = attend_rows_back(q_ref[at], k_ref[...], v_ref[...], grads, floor)
            pre = (dq.astype(LOW).astype(WIDE) * SCALE).astype(LOW)
            dq_ref[at] = pre
            row = column_rows(pre)[0]
            totals = row if totals is None else totals + row
            if begin == 0:
                dk_ref[...] = dk
                dv_ref[...] = dv
            else:
                dk_ref[...] += dk
                dv_ref[...] += dv
        dkv_ref[:, :local] = dk_ref[...].astype(LOW)
        dkv_ref[:, local:] = dv_ref[...].astype(LOW)
        sum_ref[0:1] = totals
        sum_ref[1:2] = column_rows(dv_ref[...])[0]

    return call(
        kernel,
        (shape((rows, local), LOW), shape((count, 2 * local), LOW), shape((2, local), WIDE)),
        spot,
        (marks, low, other, w_so, queries, keys, values),
        flops=10 * rows * keys.size,
        scratch=[pltpu.VMEM((count, local), WIDE), pltpu.VMEM((count, local), WIDE)],
        limit=24,
        cold=(3, 4, 5, 6),
    )


def input_back(query_grad, pair_grad, source_grad, w_q, w_kv, w_ckv, tokens, sources):
    width = w_q.shape[0]
    span = tokens + sources

    def kernel(spot_ref, q_ref, kv_ref, s_ref, wq_ref, wkv_ref, ws_ref, keep_ref, send_ref):
        part = mm_nt(q_ref[...], wq_ref[...]) + mm_nt(kv_ref[...], wkv_ref[...])
        more = mm_nt(s_ref[...], ws_ref[...])
        for kc, ref in enumerate((keep_ref, send_ref)):
            for kx in range(2):
                at = 2 * kc + kx
                start = kx * span
                piece = part[at * tokens : (at + 1) * tokens]
                ref[start : start + tokens] = piece.astype(ref.dtype)
                piece = more[at * sources : (at + 1) * sources]
                ref[start + tokens : start + span] = piece.astype(ref.dtype)

    return call(
        kernel,
        (shape((2 * span, width), WIDE), shape((2 * span, width), LOW)),
        jnp.zeros((1,), jnp.int32),
        (query_grad, pair_grad, source_grad, w_q, w_kv, w_ckv),
        flops=2 * query_grad.shape[0] * (w_q.size + w_kv.size),
        piped=True,
    )


def produce_ffn(spot, activated, grad_low, grad_other, low, other, inner_grad):
    wide = activated.shape[1]
    half, width = grad_low.shape
    part = width // 16

    def kernel(spot_ref, a_ref, g0_ref, g1_ref, x0_ref, x1_ref, u_ref, *refs):
        outs, all_ref = refs[:4], refs[4]
        me = spot_ref[0]
        high = spot_ref[1]
        low = spot_ref[2]
        for place in range(2):
            if place == 0:
                result = mm_tn(a_ref[:half], g0_ref[...]) + mm_tn(a_ref[half:], g1_ref[...])
            else:
                result = mm_tn(x0_ref[...], u_ref[:half]) + mm_tn(x1_ref[...], u_ref[half:])
            for d in range(4):
                for z in range(2):
                    for y in range(2):
                        at = (4 * d + 2 * z + y) * part
                        piece = result[at : at + part]
                        if place == 0:
                            all_ref[low ^ y, high ^ z, d] = piece
                        else:
                            all_ref[high ^ z, low ^ y, me ^ d] = piece
            outs[2 * place][...] = all_ref[0]
            outs[2 * place + 1][...] = all_ref[1].astype(LOW)

    piece = (2, 4, part, width)
    return call(
        kernel,
        (shape(piece, WIDE), shape(piece, LOW)) * 2,
        spot,
        (activated, grad_low, grad_other, low, other, inner_grad),
        flops=8 * half * width * wide,
        scratch=[pltpu.VMEM((2,) + piece, WIDE)],
        limit=16,
        piped=True,
    )


def join_ffn(out_half, out_got, in_half, in_got):
    def kernel(spot_ref, a_ref, b_ref, c_ref, d_ref, out_ref):
        out_ref[0] = (a_ref[0] + b_ref[...].astype(WIDE)).astype(LOW)
        out_ref[1] = (c_ref[0] + d_ref[...].astype(WIDE)).astype(LOW)

    return call(
        kernel,
        shape((2,) + out_got.shape, LOW),
        jnp.zeros((1,), jnp.int32),
        (out_half, out_got, in_half, in_got),
    )


def finish_ffn(spot, out_pieces, in_pieces):
    part, width = out_pieces[0].shape[1:]
    rows = 4 * part

    def kernel(spot_ref, oa_ref, ob_ref, oc_ref, ia_ref, ib_ref, ic_ref, fo_ref, fi_ref):
        me = spot_ref[0]
        high = spot_ref[1]
        low = spot_ref[2]
        for kz in range(2):
            for ky in range(2):
                quarter = ((kz ^ high) * 2 + (ky ^ low)) * part
                source = oc_ref.at[ky] if kz else (ob_ref if ky else oa_ref)
                for d in range(4):
                    row = pl.multiple_of(d * rows + quarter, 16)
                    fo_ref[pl.ds(row, part), :] = source[d].astype(WIDE)
                source = ic_ref.at[kz] if ky else (ib_ref if kz else ia_ref)
                row = pl.multiple_of(quarter, 16)
                for j in range(4):
                    fi_ref[pl.ds(row, part), j * width : (j + 1) * width] = source[me ^ j].astype(WIDE)

    return call(
        kernel,
        (shape((4 * rows, width), WIDE), shape((rows, 4 * width), WIDE)),
        spot,
        tuple(out_pieces) + tuple(in_pieces),
        limit=16,
        piped=True,
    )


def produce_mixed(spot, one_in, one_grad, two_in, two_grad, heads, heads_grads):
    rows, local = one_grad.shape
    width = one_in.shape[1]
    part = local // 4
    pieces = len(heads_grads)
    half = rows // pieces

    def kernel(spot_ref, a_ref, ag_ref, b_ref, bg_ref, o_ref, *refs):
        g_refs, (keep_ref, send_ref, all_ref) = refs[:pieces], refs[pieces:]
        me = spot_ref[0]
        high = spot_ref[1]
        low = spot_ref[2]
        one = mm_tn(a_ref[:rows], ag_ref[...])
        two = mm_tn(b_ref[...], bg_ref[...])
        three = mm_tn(o_ref[:half], g_refs[0][...])
        if pieces == 2:
            three = three + mm_tn(o_ref[half:], g_refs[1][...])
        for z in range(2):
            for y in range(2):
                quarter = (2 * z + y) * part
                for d in range(4):
                    at = d * local + quarter
                    all_ref[low ^ y, high ^ z, me ^ d, :, :local] = one[at : at + part]
                    all_ref[low ^ y, high ^ z, me ^ d, :, local : 3 * local] = two[at : at + part]
                    piece = three[quarter : quarter + part, d * local : (d + 1) * local]
                    all_ref[low ^ y, high ^ z, d, :, 3 * local :] = piece
        keep_ref[...] = all_ref[0]
        send_ref[...] = all_ref[1].astype(LOW)

    operands = (one_in, one_grad, two_in, two_grad, heads) + tuple(heads_grads)
    wide = two_in.shape[0] > 2048
    return call(
        kernel,
        (shape((2, 4, part, width), WIDE), shape((2, 4, part, width), LOW)),
        spot,
        operands,
        flops=2 * width * (one_grad.size + two_grad.size + heads.size),
        scratch=[pltpu.VMEM((2, 2, 4, part, width), WIDE)],
        cold=() if wide else (0, 2, 4) + ((5,) if pieces == 1 else ()),
        piped=wide,
    )


def place_mixed(spot, pieces, late, far_first, fused, earlier=()):
    part, width = pieces.shape[2:]
    local = 4 * part

    def kernel(spot_ref, piece_ref, *refs):
        outs = refs[len(earlier) :]
        me = spot_ref[0]
        for j in range(4):
            block = piece_ref[0, me ^ j].astype(WIDE)
            for p in range(3):
                piece = block[:, p * local : (p + 1) * local]
                if fused:
                    out, at = outs[0], p * width + j * local
                elif p == 0:
                    out, at = outs[0], j * local
                else:
                    out, at = outs[1], (p - 1) * width + j * local
                out[:, at : at + local] = piece
            outs[-1][:, j * local : (j + 1) * local] = piece_ref[0, j, :, 3 * local :].astype(WIDE)

    def source(i, spot):
        return (i ^ spot[1] if far_first else i ^ spot[2], 0, 0, 0)

    def target(i, spot):
        return (2 * i + (spot[2] ^ late) if far_first else 2 * (spot[1] ^ late) + i, 0)

    widths = (3 * width, width) if fused else (width, 2 * width, width)
    outs = tuple(shape((local, w), WIDE) for w in widths)
    return pl.pallas_call(
        kernel,
        out_shape=outs,
        grid_spec=pltpu.PrefetchScalarGridSpec(
            num_scalar_prefetch=1,
            grid=(2,),
            in_specs=[pl.BlockSpec((1, 4, part, width), source)]
            + [pl.BlockSpec(memory_space=pl.ANY) for _ in earlier],
            out_specs=tuple(pl.BlockSpec((part, w), target) for w in widths),
        ),
        input_output_aliases={2 + at: at for at in range(len(earlier))},
        cost_estimate=cost(0, pieces, *outs),
        compiler_params=pltpu.CompilerParams(vmem_limit_bytes=12 << 20),
    )(spot, pieces, *earlier)


def widen_rows(value, tokens):
    rows, width = value.shape

    def kernel(spot_ref, x_ref, top_ref, rest_ref):
        top_ref[...] = x_ref[:tokens].astype(WIDE)
        rest_ref[...] = x_ref[tokens:].astype(WIDE)

    return call(
        kernel,
        (shape((tokens, width), WIDE), shape((rows - tokens, width), WIDE)),
        jnp.zeros((1,), jnp.int32),
        (value,),
    )


def settle(value, *holds):
    def kernel(spot_ref, x_ref, out_ref):
        out_ref[...] = x_ref[...]

    return call(kernel, shape(value.shape, value.dtype), jnp.zeros((1,), jnp.int32), (after(value, *holds),))


def sort_vectors(value, got):
    rows, width = value.shape
    order = (0, 3, 6, 9, 10, 2, 11, 12, 5, 8)

    def kernel(spot_ref, a_ref, b_ref, bias_ref, gain_ref, inner_ref):
        total = a_ref[...] + b_ref[...]
        for at, source in enumerate(order):
            bias_ref[at : at + 1] = total[source : source + 1]
        for at, source in enumerate((1, 4, 7)):
            gain_ref[at : at + 1] = total[source : source + 1]
        for at in range(4):
            inner_ref[at : at + 1] = total[13 + at : 14 + at]

    return call(
        kernel,
        (shape((10, width), WIDE), shape((3, width), WIDE), shape((4, width), WIDE)),
        jnp.zeros((1,), jnp.int32),
        (value, got),
    )


def exchange_sum(keep, send, bit, *holds):
    got = flip_ctx(send, bit)
    if holds:
        got = after(got, *holds)
    return keep + got.astype(WIDE)


def sum_rest(total, *holds):
    lines = lax.axis_size("ctx") // lax.axis_size("fsdp")
    for bit in powers(lax.axis_size("ctx")):
        if bit not in (1, lines):
            low = total.astype(LOW)
            total = low.astype(WIDE) + after(flip_ctx(low, bit), *holds).astype(WIDE)
    return total.astype(LOW)


def trade_columns(low):
    part = low.shape[1]
    local = 4 * part
    far = flip_model(low[2:], 2)
    near = flip_model(jnp.stack([low[1], far[1]]), 1)
    columns = jnp.stack([low[0], near[0], far[0], near[1]])
    return jnp.concatenate([columns[..., : 3 * local], low[..., 3 * local :]], axis=-1)


def gather_pieces(piece, bits, *holds):
    first = after(flip_ctx(piece, bits[0]), *holds)
    both = jnp.stack([piece, first])
    return piece, first, flip_ctx(both, bits[1]), both


def move_columns(mate, cross, *holds):
    line = flip_ctx(after(cross, *holds), 1)
    return flip_model(mate, 1), cross, line, flip_model(cross, 1), flip_model(line, 1)


def core_sum(keep, send):
    mine = keep + flip_model(send, 1).astype(WIDE)
    return mine, flip_model(mine.astype(LOW), 2)


def sum_lines(value):
    for bit in reversed(line_bits()):
        value = value[:bit].astype(WIDE) + flip_ctx(value[bit:], bit).astype(WIDE)
        value = value.astype(LOW)
    return value[0]


def body(
    hidden,
    encoded,
    cotangent,
    dec_seg,
    enc_seg,
    self_qkv,
    self_out,
    cross_q,
    cross_kv,
    cross_out,
    ffn_in,
    ffn_out,
    biases,
    gains,
    ffn_bias,
):
    tokens = hidden.shape[1]
    rows = 4 * tokens
    width = hidden.shape[2]
    sources = encoded.shape[1]
    model = lax.axis_size("fsdp")
    lines = lax.axis_size("ctx") // model
    own = lax.axis_index("fsdp")
    ctx_index = lax.axis_index("ctx")
    local = width // model
    spot = jnp.stack([own, (ctx_index // lines) % 2, ctx_index % 2, ctx_index % lines])
    spot = spot.astype(jnp.int32)

    block = pack_rows(hidden[0], encoded[0], dec_seg, enc_seg)
    self_qkv = after(self_qkv, block)
    block = swap_places(block)
    small = jnp.concatenate([biases, gains, jnp.zeros((3, local), WIDE)], axis=0)
    qkv_own, qkv_mate, qkv_away = prepare_qkv(spot, self_qkv, small)
    qkv_cross = flip_model(qkv_away, 2)
    rest_own, rest_mate, rest_away, w_so, w_co, w_fo = prepare_rest(
        spot, cross_q, cross_kv, ffn_in, self_out, cross_out, ffn_out
    )
    block = after(block, rest_away)
    block_far = flip_model(block, 2)
    qkv_blocks = (qkv_own,) + move_columns(qkv_mate, qkv_cross, block)
    near_rows = jnp.stack([block, block_far])[None]
    near_rows = after(near_rows, qkv_blocks[3])
    rest_cross = flip_model(after(rest_away, block_far), 2)
    for bit in line_bits():
        near_rows = jnp.concatenate([near_rows, flip_ctx(near_rows, bit)], axis=0)
    near_rows = after(near_rows, rest_cross, *qkv_blocks[1:])
    far_rows = flip_model(near_rows, 1)
    rest_blocks = (rest_own,) + move_columns(rest_mate, rest_cross, near_rows)

    inputs, source_rows, queries, keys, values, w_q, w_kv, table, marks, emarks = project(
        spot, near_rows, far_rows, qkv_blocks, tokens, sources
    )
    other = swap_places(after(cotangent[0], rest_cross))
    plain = keys.shape[0] > 2048
    line_ids = (ctx_index % lines) ^ jnp.arange(lines, dtype=jnp.int32)[:, None]
    model_ids = own ^ jnp.array([0, 2, 1, 3], jnp.int32)[None, :]
    starts = (model_ids * lines + line_ids) * tokens
    places = (starts[:, :, None] + jnp.arange(tokens, dtype=jnp.int32)).reshape(-1)
    if plain:
        attended, keep, send = plain_forward(marks, places, queries, keys, values, w_so)
    else:
        attended, keep, send = self_forward(spot, marks, queries, keys, values, w_so, tokens)
    keep, send = after(keep, other), after(send, other)
    mine, away = core_sum(keep, send)
    w_cq, w_ckv, w_fi, source_keys, source_values = arrange_rest(
        spot, rest_blocks, source_rows, table
    )
    away = after(away, w_cq)
    first, first_low, first_normal, first_rate = residual_norm(inputs, mine, away, table, 5, 0)
    first_other = flip_model(first_low, 1)
    other_far = flip_model(after(other, away), 2)
    small_low = small.astype(LOW).astype(WIDE)
    cross_queries, crossed, keep, send, first_all = cross_forward(
        spot, marks, emarks, first_low, first_other, w_cq, source_keys, source_values, w_co, small_low, tokens
    )
    keep, send = after(keep, other_far), after(send, other_far)
    mine, away = core_sum(keep, send)
    second, second_low, second_normal, second_rate = residual_norm(first, mine, away, table, 8, 1)
    second_other = flip_model(second_low, 1)
    inner_bias = ffn_bias.astype(LOW).astype(WIDE)[None]
    activated, slope, keep, send = ffn_forward(second_low, second_other, w_fi, w_fo, inner_bias)
    mine, away = core_sum(keep, send)
    result, third_grad, ffn_low, third_sums = turn_around(
        second, mine, away, table, other, other_far, tokens
    )

    ffn_other = flip_model(ffn_low, 1)
    inner_grad, keep, send, inner_sum = ffn_back(ffn_low, ffn_other, w_fo, w_fi, slope)
    mine, away = core_sum(keep, send)
    out_keep, out_send, in_keep, in_send = produce_ffn(
        spot, activated, ffn_low, ffn_other, second_low, second_other, inner_grad
    )
    away = after(away, in_keep)
    out_got = flip_ctx(out_send, 1)
    in_got = flip_ctx(in_send, lines)
    second_grad, cross_low, second_sums = residual_back(
        third_grad, mine, away, second_normal, second_rate, table, 1, tokens
    )
    cross_other = flip_model(cross_low, 1)
    result = swap_places(after(result, cross_low))
    cross_query_pre, source_grad, keep, send, cross_sums, cross_all = cross_back(
        spot, marks, emarks, cross_low, cross_other, w_co, cross_queries, source_keys, source_values, w_cq, tokens
    )
    keep, send = after(keep, out_got, in_got), after(send, out_got, in_got)
    mine, away = core_sum(keep, send)
    out_half = out_keep + after(out_got, mine).astype(WIDE)
    in_half = in_keep + after(in_got, mine).astype(WIDE)
    out_got = flip_ctx(out_half[1].astype(LOW), lines)
    in_got = flip_ctx(in_half[1].astype(LOW), 1)
    cross_keep, cross_send = produce_mixed(
        spot, after(first_all, result), cross_query_pre, source_rows, source_grad, crossed, (cross_all,)
    )
    away = after(away, cross_keep, out_got, in_got)
    first_grad, self_low, first_sums = residual_back(
        second_grad, mine, away, first_normal, first_rate, table, 0, tokens
    )
    self_other = flip_model(self_low, 1)
    cross_got = flip_ctx(cross_send, 1)
    ffn_total = join_ffn(out_half, after(out_got, self_low), in_half, after(in_got, self_low))
    self_low = after(self_low, ffn_total)
    if plain:
        self_query_pre, pair_grad, self_sums = plain_back(
            marks, places, self_low, self_other, w_so, queries, keys, values
        )
    else:
        self_query_pre, pair_grad, self_sums = self_back(
            spot, marks, self_low, self_other, w_so, queries, keys, values, tokens
        )
    self_keep, self_send = produce_mixed(
        spot, inputs, self_query_pre, inputs, pair_grad, attended, (self_low, self_other)
    )
    self_half = exchange_sum(self_keep, self_send, 1)
    cross_half = cross_keep + after(cross_got, self_keep).astype(WIDE)
    wide_rows = jnp.concatenate([first_sums, second_sums, third_sums], axis=0)
    wide_rows = wide_rows + after(flip_model(wide_rows, 1), cross_half)
    wide_rows = lax.dynamic_slice_in_dim(wide_rows, own * local, local, axis=1)
    vectors = jnp.concatenate(
        [wide_rows, after(self_sums, cross_half), after(cross_sums, cross_half), after(inner_sum, cross_half).reshape(-1, local)], axis=0
    )
    vectors = jnp.pad(vectors, ((0, 32 - vectors.shape[0]), (0, 0))).reshape(16, 2 * local)
    cross_total = exchange_sum(cross_half[0], cross_half[1].astype(LOW), lines, self_half)
    ffn_total = sum_rest(ffn_total, self_half)
    lined = jnp.concatenate(
        [
            pair_grad.reshape(lines, rows, 2 * local),
            source_grad.reshape(lines, 4 * sources, 2 * local),
            jnp.broadcast_to(vectors.astype(LOW)[None], (lines,) + vectors.shape),
        ],
        axis=1,
    )
    lined = sum_lines(after(lined, self_half))
    pair_own = lined[:rows]
    source_own = lined[rows : rows + 4 * sources]
    vectors = lined[rows + 4 * sources :].astype(WIDE)
    keep, send = input_back(
        self_query_pre, pair_own, source_own, w_q, w_kv, w_ckv, tokens, sources
    )
    both_half = keep + flip_model(send, 1).astype(WIDE)
    span = tokens + sources
    both = both_half[:span] + flip_model(both_half[span:].astype(LOW), 2).astype(WIDE)
    both = jnp.concatenate([both[:tokens] + first_grad[:tokens], both[tokens:]], axis=0)
    both = both.astype(LOW)
    hidden_grad, encoded_grad = widen_rows(swap_places(both), tokens)
    hidden_grad = hidden_grad[None]
    encoded_grad = encoded_grad[None]

    cross_total = after(cross_total, ffn_total)
    self_total = exchange_sum(self_half[0], self_half[1].astype(LOW), lines, lined, cross_total)
    ffn_far = flip_model(ffn_total[1, 2:], 2)
    ffn_near = flip_model(jnp.stack([ffn_total[1, 1], ffn_far[1]]), 1)
    ffn_piece = jnp.stack([ffn_total[1, 0], ffn_near[0], ffn_far[0], ffn_near[1]])
    out_pieces = gather_pieces(ffn_total[0], (1, lines))
    in_pieces = gather_pieces(ffn_piece, (lines, 1))
    cross_piece = sum_rest(cross_total, self_total)
    self_piece = sum_rest(self_total, out_pieces[1])
    self_traded = trade_columns(self_piece)
    self_pieces = gather_pieces(self_traded, (lines, 1))
    cross_pieces = gather_pieces(trade_columns(cross_piece), (1, lines), self_traded)
    vectors = vectors.reshape(-1, local)
    bits = powers(lax.axis_size("ctx"))[len(line_bits()) :]
    for bit in bits[:-1]:
        vectors = vectors + after(flip_ctx(vectors, bit), self_traded)
    d_bias, d_gain, d_inner = sort_vectors(vectors, after(flip_ctx(vectors, bits[-1]), self_pieces[1]))
    d_inner = d_inner.reshape(-1)
    output = settle(result, self_piece)[None]
    cross_early = place_mixed(spot, cross_pieces[3], 0, False, False)
    self_early = place_mixed(spot, self_pieces[3], 0, True, True)
    g_cq, g_ckv, g_co = place_mixed(spot, cross_pieces[2], 1, False, False, cross_early)
    g_fo, g_fi = finish_ffn(spot, out_pieces[:3], in_pieces[:3])
    last = after(self_pieces[2], g_fi, d_bias, output, cross_early[0], self_early[0])
    g_qkv, g_so = place_mixed(spot, last, 1, True, True, self_early)
    return (
        output,
        hidden_grad,
        encoded_grad,
        g_qkv,
        g_so,
        g_cq,
        g_ckv,
        g_co,
        g_fi,
        g_fo,
        d_bias,
        d_gain,
        d_inner,
    )


def solution(mesh):
    whole = P("fsdp", "ctx", None)
    matrix = P("fsdp", None)
    ids = P("fsdp", "ctx")
    table = P(None, "fsdp")
    return jax.shard_map(
        body,
        mesh=mesh,
        in_specs=(whole, whole, whole, ids, ids) + (matrix,) * 7 + (table, table, P("fsdp")),
        out_specs=(whole,) * 3 + (matrix,) * 7 + (table, table, P("fsdp")),
        check_vma=False,
    )
```

```python
import jax
import jax.numpy as jnp
from jax import lax
from jax.experimental import pallas as pl
from jax.experimental.pallas import tpu as pltpu
from jax.sharding import PartitionSpec as P

H = 12
HD = 64
EPSILON = 1e-05
FLOOR_SCORE = -1e30
SCALE = float(HD) ** (-0.5)
LOW = jnp.bfloat16
WIDE = jnp.float32


def mm(left, right):
    return jnp.dot(left, right, preferred_element_type=WIDE)


def mm_tn(left, right):
    return lax.dot_general(left, right, (((0,), (0,)), ((), ())), preferred_element_type=WIDE)


def mm_nt(left, right):
    return lax.dot_general(left, right, (((1,), (1,)), ((), ())), preferred_element_type=WIDE)


def flip_model(value, bit):
    count = lax.axis_size("fsdp")
    return lax.ppermute(value, "fsdp", [(i, i ^ bit) for i in range(count)])


def flip_ctx(value, bit):
    count = lax.axis_size("ctx")
    return lax.ppermute(value, "ctx", [(i, i ^ bit) for i in range(count)])


def swap_places(value):
    model = lax.axis_size("fsdp")
    ctx = lax.axis_size("ctx")
    lines = ctx // model
    route = []
    for f in range(model):
        for z in range(model):
            for r in range(lines):
                route.append((f * ctx + z * lines + r, z * ctx + f * lines + r))
    return lax.ppermute(value, ("fsdp", "ctx"), route)


def powers(limit):
    bits = []
    bit = 1
    while bit < limit:
        bits.append(bit)
        bit *= 2
    return bits


def line_bits():
    return powers(lax.axis_size("ctx") // lax.axis_size("fsdp"))


def after(value, *others):
    return lax.optimization_barrier((value,) + others)[0]


def shape(dims, kind):
    return jax.ShapeDtypeStruct(tuple(dims), kind)


COST = 5.0


def cost(flops, *arrays):
    count = 0
    for array in arrays:
        count += array.size * array.dtype.itemsize
    return pl.CostEstimate(
        flops=int(flops * COST), transcendentals=0, bytes_accessed=int(count * COST)
    )


def call(kernel, outs, spot, operands, flops=0, scratch=(), limit=12, piped=False, cold=(), parked=(), saved=()):
    many = isinstance(outs, tuple)
    listed = list(outs) if many else [outs]
    count = len(operands)
    if saved:
        first = operands[saved[0]]
        height = sum(operands[at].shape[0] for at in saved)
        listed.append(shape((height,) + first.shape[1:], first.dtype))
        many = True
    body = kernel
    if cold or parked or saved:
        place = pl.BlockSpec(memory_space=pltpu.VMEM)
        far = pl.BlockSpec(memory_space=pltpu.HBM)
        own = count + len(listed) + len(scratch)

        def body(spot_ref, *all_refs):
            refs, buffers, done = list(all_refs[:own]), list(all_refs[own:-1]), all_refs[-1]
            used = 0
            ending = []

            def copy(source, target):
                nonlocal used
                moving = pltpu.make_async_copy(source, target, done.at[used])
                used += 1
                return moving

            incoming = []
            for at in cold:
                buffer = buffers.pop(0)
                incoming.append(copy(refs[at], buffer))
                incoming[-1].start()
                refs[at] = buffer
            row = 0
            for at in saved:
                target = refs[count + len(listed) - 1].at[pl.ds(row, operands[at].shape[0])]
                row += operands[at].shape[0]
                ending.append(copy(refs[at], target))
                ending[-1].start()
            for moving in incoming:
                moving.wait()
            outgoing = []
            for at in parked:
                buffer = buffers.pop(0)
                outgoing.append(copy(buffer, refs[count + at]))
                refs[count + at] = buffer
            if saved:
                refs.pop(count + len(listed) - 1)
            kernel(spot_ref, *refs)
            for moving in outgoing:
                moving.start()
            for moving in outgoing + ending:
                moving.wait()

        buffers = [pltpu.VMEM(operands[at].shape, operands[at].dtype) for at in cold]
        buffers += [pltpu.VMEM(listed[at].shape, listed[at].dtype) for at in parked]
        held = set(parked) | ({len(listed) - 1} if saved else set())
        out_specs = [far if at in held else place for at in range(len(listed))]
        moves = len(cold) + len(parked) + len(saved)
        spec = dict(
            in_specs=[pl.BlockSpec(memory_space=pltpu.SMEM)]
            + [far if at in cold else place for at in range(count)],
            out_specs=tuple(out_specs) if many else out_specs[0],
            scratch_shapes=list(scratch) + buffers + [pltpu.SemaphoreType.DMA((moves,))],
        )
        limit = limit + 8
    elif piped:
        place = lambda value: pl.BlockSpec(value.shape, lambda i, spot: (0,) * len(value.shape))
        spec = dict(
            grid_spec=pltpu.PrefetchScalarGridSpec(
                num_scalar_prefetch=1,
                grid=(1,),
                in_specs=[place(value) for value in operands],
                out_specs=tuple(place(value) for value in listed) if many else place(outs),
                scratch_shapes=list(scratch),
            )
        )
        limit = limit + 12
    else:
        place = pl.BlockSpec(memory_space=pltpu.VMEM)
        spec = dict(
            in_specs=[pl.BlockSpec(memory_space=pltpu.SMEM)] + [place] * count,
            out_specs=tuple(place for _ in listed) if many else place,
            scratch_shapes=list(scratch),
        )
    return pl.pallas_call(
        body,
        out_shape=tuple(listed) if many else outs,
        cost_estimate=cost(flops, *operands, *listed),
        compiler_params=pltpu.CompilerParams(vmem_limit_bytes=limit << 20),
        **spec,
    )(spot, *operands)


def pack_rows(tokens, sources, token_marks, source_marks):
    count, width = tokens.shape
    more = sources.shape[0]

    def kernel(spot_ref, x_ref, e_ref, m_ref, s_ref, out_ref):
        out_ref[:count] = x_ref[...]
        out_ref[count : count + more] = e_ref[...]
        out_ref[count + more :] = jnp.zeros((16, width), LOW)
        first = jnp.broadcast_to(m_ref[...], (16, count)).astype(WIDE).astype(LOW)
        second = jnp.broadcast_to(s_ref[...], (16, more)).astype(WIDE).astype(LOW)
        out_ref[count + more :, :count] = first
        out_ref[count + more :, count : count + more] = second

    return call(
        kernel,
        shape((count + more + 16, width), LOW),
        jnp.zeros((1,), jnp.int32),
        (tokens, sources, token_marks, source_marks),
        piped=True,
    )


def prepare_qkv(spot, weight, small):
    rows = weight.shape[0]

    def kernel(spot_ref, w_ref, small_ref, own_ref, near_ref, far_ref, all_ref):
        me = spot_ref[0]
        side = spot_ref[2]
        small = small_ref[...].astype(LOW)
        tail = jnp.zeros((16, 2 * rows), LOW)
        for d in range(4):
            for p in range(3):
                piece = w_ref[:, p * 4 * rows + d * rows : p * 4 * rows + (d + 1) * rows]
                all_ref[me ^ d, :, p * rows : (p + 1) * rows] = piece.astype(LOW)
        own_ref[:rows] = all_ref[0]
        near_ref[:rows] = all_ref[1]
        far_ref[:rows] = all_ref[2 + side]
        for ref in (own_ref, near_ref, far_ref):
            ref[rows:, :rows] = small
            ref[rows:, rows:] = tail

    piece = (rows + 16, 3 * rows)
    return call(
        kernel,
        (shape(piece, LOW),) * 3,
        spot,
        (weight, small),
        scratch=[pltpu.VMEM((4, rows, 3 * rows), LOW)],
    )


def prepare_rest(spot, cross_q, cross_kv, ffn_in, self_out, cross_out, ffn_out):
    rows = cross_q.shape[0]
    wide = ffn_in.shape[1] // 4
    piece = (rows, 3 * rows + wide)

    def kernel(spot_ref, q_ref, kv_ref, fi_ref, so_ref, co_ref, fo_ref, *outs):
        own_ref, near_ref, far_ref, so_out, co_out, fo_out, all_ref = outs
        me = spot_ref[0]
        side = spot_ref[2]
        for d in range(4):
            all_ref[me ^ d, :, :rows] = q_ref[:, d * rows : (d + 1) * rows].astype(LOW)
            for p in range(2):
                part = kv_ref[:, (p * 4 + d) * rows : (p * 4 + d + 1) * rows]
                all_ref[me ^ d, :, (1 + p) * rows : (2 + p) * rows] = part.astype(LOW)
            all_ref[me ^ d, :, 3 * rows :] = fi_ref[:, d * wide : (d + 1) * wide].astype(LOW)
        own_ref[...] = all_ref[0]
        near_ref[...] = all_ref[1]
        far_ref[...] = all_ref[2 + side]
        so_out[...] = so_ref[...].astype(LOW)
        co_out[...] = co_ref[...].astype(LOW)
        fo_out[...] = fo_ref[...].astype(LOW)

    return call(
        kernel,
        (shape(piece, LOW),) * 3
        + (shape(self_out.shape, LOW), shape(cross_out.shape, LOW), shape(ffn_out.shape, LOW)),
        spot,
        (cross_q, cross_kv, ffn_in, self_out, cross_out, ffn_out),
        scratch=[pltpu.VMEM((4,) + piece, LOW)],
        limit=16,
        piped=True,
    )


def ordered_blocks(spot_ref, refs, pair_ref):
    side = spot_ref[2]
    pair_ref[0, side] = refs[2][...]
    pair_ref[0, 1 - side] = refs[3][...]
    pair_ref[1, side] = refs[4][...]
    pair_ref[1, 1 - side] = refs[5][...]
    return refs[0][...], refs[1][...], pair_ref[0, 0], pair_ref[1, 1]


def arrange_rest(spot, blocks, source_rows, table):
    rows = blocks[0].shape[0]
    wide = blocks[0].shape[1] - 3 * rows
    count, width = source_rows.shape

    def kernel(spot_ref, *refs):
        x_ref, table_ref, q_ref, kv_ref, fi_ref, *outs = refs[6:]
        keys_ref, values_ref, rel_ref, pair_ref = outs
        me = spot_ref[0]
        parts = ordered_blocks(spot_ref, refs[:6], pair_ref)
        for k in range(4):
            start = pl.multiple_of((me ^ k) * rows, 64)
            q_ref[pl.ds(start, rows), :] = parts[k][:, :rows]
            kv_ref[pl.ds(start, rows), :] = parts[k][:, rows : 3 * rows]
            fi_ref[pl.ds(start, rows), :] = parts[k][:, 3 * rows :]
        for j in range(4):
            rel_ref[j] = table_ref[:, j * rows : (j + 1) * rows]
        shift = rel_ref[me][7:8]
        out = mm(x_ref[...], kv_ref[...])
        keys_ref[...] = out[:, :rows].astype(LOW)
        values_ref[...] = (out[:, rows:] + shift).astype(LOW)

    return call(
        kernel,
        (
            shape((4 * rows, rows), LOW),
            shape((4 * rows, 2 * rows), LOW),
            shape((4 * rows, wide), LOW),
            shape((count, rows), LOW),
            shape((count, rows), LOW),
        ),
        spot,
        tuple(blocks) + (source_rows, table),
        flops=4 * count * width * rows,
        scratch=[pltpu.VMEM((4, 16, rows), WIDE), pltpu.VMEM((2, 2) + blocks[0].shape, LOW)],
        limit=16,
    )


def project(spot, near_rows, far_rows, blocks, tokens, sources):
    lines = near_rows.shape[0]
    width = near_rows.shape[-1]
    local = width // 4
    span = near_rows.shape[2]
    rows = 4 * tokens

    def kernel(spot_ref, a_ref, b_ref, *refs):
        x_ref, e_ref, q_ref, k_ref, v_ref, wq_ref, wkv_ref, table_ref, *outs = refs[6:]
        marks_ref, emarks_ref, rel_ref, w_ref, pair_ref = outs
        me = spot_ref[0]

        @pl.when(pl.program_id(0) == 0)
        def _():
            parts = ordered_blocks(spot_ref, refs[:6], pair_ref)
            for k in range(4):
                start = pl.multiple_of((me ^ k) * local, 64)
                w_ref[pl.ds(start, local), :] = parts[k][:local]
                rel_ref[k] = parts[k][local:, :local].astype(WIDE)
            for j in range(4):
                table_ref[:, j * local : (j + 1) * local] = rel_ref[me ^ j]
            wq_ref[...] = w_ref[:, :local]
            wkv_ref[...] = w_ref[:, local:]

        lane = lax.broadcasted_iota(jnp.int32, (1, 128), 1)
        emarks = jnp.zeros((1, 128), WIDE)
        for kc, ref in enumerate((a_ref, b_ref)):
            for kx in range(2):
                at = 2 * kc + kx
                start = at * tokens
                x_ref[start : start + tokens, :] = ref[0, kx, :tokens, :]
                e_ref[at * sources : (at + 1) * sources, :] = ref[0, kx, tokens : tokens + sources, :]
                marks = ref[0, kx, tokens + sources : tokens + sources + 16, :256].astype(WIDE)
                marks_ref[:, start : start + tokens] = marks[0:1, :tokens]
                moved = pltpu.roll(marks[:8, 128:], at * sources, 1)[0:1]
                emarks = emarks + jnp.where((lane // sources) == at, moved, 0.0)
        emarks_ref[...] = emarks
        own_small = rel_ref[0]
        out = mm(x_ref[...], w_ref[...])
        k_ref[...] = out[:, local : 2 * local].astype(LOW)
        v_ref[...] = (out[:, 2 * local :] + own_small[4:5]).astype(LOW)

        @pl.when(pl.program_id(0) == 0)
        def _():
            q_ref[...] = ((out[:, :local] + own_small[3:4]) * SCALE).astype(LOW)

    full = lambda *dims: pl.BlockSpec(dims, lambda i, spot: (0,) * len(dims))
    band = lambda w: pl.BlockSpec((rows, w), lambda i, spot: (i, 0))
    part = pl.BlockSpec((1, 2, span, width), lambda i, spot: (i, 0, 0, 0))
    piece = (local + 16, 3 * local)
    outs = (
        shape((lines * rows, width), LOW),
        shape((lines * 4 * sources, width), LOW),
        shape((rows, local), LOW),
        shape((lines * rows, local), LOW),
        shape((lines * rows, local), LOW),
        shape((width, local), LOW),
        shape((width, 2 * local), LOW),
        shape((16, width), WIDE),
        shape((1, lines * rows), WIDE),
        shape((1, lines * 4 * sources), WIDE),
    )
    operands = (near_rows, far_rows) + tuple(blocks)
    return pl.pallas_call(
        kernel,
        out_shape=outs,
        grid_spec=pltpu.PrefetchScalarGridSpec(
            num_scalar_prefetch=1,
            grid=(lines,),
            in_specs=[part, part] + [full(*piece)] * 6,
            out_specs=(
                band(width),
                pl.BlockSpec((4 * sources, width), lambda i, spot: (i, 0)),
                full(rows, local),
                band(local),
                band(local),
                full(width, local),
                full(width, 2 * local),
                full(16, width),
                pl.BlockSpec((1, rows), lambda i, spot: (0, i)),
                pl.BlockSpec((1, 4 * sources), lambda i, spot: (0, i)),
            ),
            scratch_shapes=[
                pltpu.VMEM((4, 16, local), WIDE),
                pltpu.VMEM((width, 3 * local), LOW),
                pltpu.VMEM((2, 2) + piece, LOW),
            ],
        ),
        cost_estimate=cost(6 * lines * rows * width * local, *operands, *outs),
        compiler_params=pltpu.CompilerParams(vmem_limit_bytes=20 << 20),
    )(spot, *operands)


def block_start(spot_ref, index, tokens, lines):
    me = spot_ref[0]
    line = spot_ref[3]
    kr, kc, kx = index // 4, (index // 2) % 2, index % 2
    return ((me ^ (kc + 2 * kx)) * lines + (line ^ kr)) * tokens


def upright(row):
    return jnp.transpose(jnp.broadcast_to(row, (128, row.shape[1])))


def self_floor(spot_ref, marks_ref, query_blocks, tokens, turned):
    blocks = marks_ref.shape[1] // tokens
    lines = blocks // 4
    down = lax.broadcasted_iota(jnp.int32, (tokens, tokens), 0)
    right = lax.broadcasted_iota(jnp.int32, (tokens, tokens), 1)
    outer, inner = (range(blocks), query_blocks) if turned else (query_blocks, range(blocks))
    table = []
    for i in outer:
        tall = upright(marks_ref[:, i * tokens : (i + 1) * tokens])
        line = []
        for j in inner:
            flat = marks_ref[:, j * tokens : (j + 1) * tokens]
            gap = block_start(spot_ref, j, tokens, lines) - block_start(spot_ref, i, tokens, lines)
            ahead = (right + gap) - down
            near = (ahead >= 0) if turned else (ahead <= 0)
            line.append(jnp.where((tall == flat) & near, 0.0, FLOOR_SCORE))
        table.append(jnp.concatenate(line, axis=1))
    return jnp.concatenate(table, axis=0)


def head_lanes(value, head):
    lane = lax.broadcasted_iota(jnp.int32, (1, value.shape[1]), 1) // HD
    return jnp.where(lane == head, value, jnp.zeros_like(value))


def attend_rows(queries, keys, values, floor):
    heads = queries.shape[1] // HD
    total = None
    for h in range(heads):
        scores = mm_nt(head_lanes(queries, h), keys) + floor
        top = jnp.max(scores, axis=1, keepdims=True)
        weights = jnp.exp(scores - top)
        prob = weights / jnp.sum(weights, axis=1, keepdims=True)
        part = head_lanes(mm(prob.astype(LOW), values), h)
        total = part if total is None else total + part
    return total.astype(LOW)


def attend_rows_back(queries, keys, values, grads, floor):
    heads = queries.shape[1] // HD
    query_grad = key_grad = value_grad = None
    for h in range(heads):
        own_queries = head_lanes(queries, h)
        own_grads = head_lanes(grads, h)
        scores = mm_nt(keys, own_queries) + floor
        top = jnp.max(scores, axis=0, keepdims=True)
        weights = jnp.exp(scores - top)
        prob = weights / jnp.sum(weights, axis=0, keepdims=True)
        prob_grad = mm_nt(values, own_grads)
        inner = jnp.sum(prob * prob_grad, axis=0, keepdims=True)
        score_grad = (prob * (prob_grad - inner)).astype(LOW)
        part_q = head_lanes(mm_tn(score_grad, keys), h)
        part_k = mm(score_grad, own_queries)
        part_v = mm(prob.astype(LOW), own_grads)
        query_grad = part_q if query_grad is None else query_grad + part_q
        key_grad = part_k if key_grad is None else key_grad + part_k
        value_grad = part_v if value_grad is None else value_grad + part_v
    return query_grad, key_grad, value_grad


def block_rows(keys):
    return 256 if keys <= 1024 else 128


def self_forward(spot, marks, queries, keys, values, weight, tokens):
    rows, local = queries.shape
    width = weight.shape[1]
    size = block_rows(keys.shape[0])

    def kernel(spot_ref, marks_ref, q_ref, k_ref, v_ref, w_ref, o_ref, keep_ref, send_ref):
        for begin in range(0, rows, size):
            blocks = range(begin // tokens, (begin + size) // tokens)
            floor = self_floor(spot_ref, marks_ref, blocks, tokens, False)
            low = attend_rows(q_ref[begin : begin + size], k_ref[...], v_ref[...], floor)
            o_ref[begin : begin + size] = low
            part = mm(low, w_ref[...])
            if begin < rows // 2:
                keep_ref[begin : begin + size] = part
            else:
                send_ref[begin - rows // 2 : begin - rows // 2 + size] = part.astype(LOW)

    return call(
        kernel,
        (shape((rows, local), LOW), shape((rows // 2, width), WIDE), shape((rows // 2, width), LOW)),
        spot,
        (marks, queries, keys, values, weight),
        flops=4 * rows * keys.size + 2 * rows * weight.size,
        limit=20,
    )


def plain_floor(marks, places, rows):
    same = marks.reshape(-1)[:rows, None] == marks
    return jnp.where(same & (places[None, :] <= places[:rows, None]), 0.0, FLOOR_SCORE)


def plain_forward(marks, places, queries, keys, values, weight):
    rows = queries.shape[0]
    low = attend_rows(queries, keys, values, plain_floor(marks, places, rows))
    part = mm(low, weight)
    return low, part[: rows // 2], part[rows // 2 :].astype(LOW)


def plain_back(marks, places, low, other, w_so, queries, keys, values):
    grads = mm_nt(jnp.concatenate([low, other], axis=0), w_so).astype(LOW)
    floor = plain_floor(marks, places, queries.shape[0])
    dq, dk, dv = attend_rows_back(queries, keys, values, grads, floor.T)
    pre = (dq.astype(LOW).astype(WIDE) * SCALE).astype(LOW)
    sums = jnp.concatenate(column_rows(pre, dv), axis=0)
    return pre, jnp.concatenate([dk, dv], axis=1).astype(LOW), sums


def norm_rows(values):
    center = values - jnp.mean(values, axis=-1, keepdims=True)
    spread = jnp.mean(center * center, axis=-1, keepdims=True)
    rate = lax.rsqrt(spread + EPSILON)
    return center * rate, rate


def turned_halves(ref):
    half = ref.shape[0] // 2
    return jnp.concatenate([ref[half:], ref[:half]], axis=0).astype(WIDE)


def residual_norm(residual, mine, other, table, bias_row, norm_row):
    rows, width = mine.shape

    def kernel(spot_ref, r_ref, mine_ref, other_ref, table_ref, h_ref, low_ref, n_ref, rate_ref):
        total = r_ref[:rows].astype(WIDE) + mine_ref[...] + turned_halves(other_ref)
        normal, rate = norm_rows(total + table_ref[bias_row : bias_row + 1])
        gain = table_ref[10 + norm_row : 11 + norm_row]
        result = normal * gain + table_ref[norm_row : norm_row + 1]
        h_ref[...] = result
        low_ref[...] = result.astype(LOW)
        n_ref[...] = normal
        rate_ref[...] = rate

    return call(
        kernel,
        (
            shape((rows, width), WIDE),
            shape((rows, width), LOW),
            shape((rows, width), WIDE),
            shape((rows, 1), WIDE),
        ),
        jnp.zeros((1,), jnp.int32),
        (residual, mine, other, table),
    )


def cross_forward(spot, marks, emarks, low, other, w_cq, keys, values, w_co, small, tokens):
    half, width = low.shape
    local = w_cq.shape[1]

    def kernel(spot_ref, marks_ref, emarks_ref, a_ref, b_ref, w_ref, k_ref, v_ref, o_ref, small_ref, *outs):
        q_out, c_out, keep_ref, send_ref = outs
        for place, ref in enumerate((a_ref, b_ref)):
            at = slice(place * half, (place + 1) * half)
            low = ((mm(ref[...], w_ref[...]) + small_ref[6:7]) * SCALE).astype(LOW)
            q_out[at] = low
            tall = []
            for i in range(place * half // tokens, (place + 1) * half // tokens):
                tall.append(upright(marks_ref[:, i * tokens : (i + 1) * tokens])[:, :1])
            tall = jnp.concatenate(tall, axis=0)
            floor = jnp.where(tall == emarks_ref[...], 0.0, FLOOR_SCORE)
            crossed = attend_rows(low, k_ref[...], v_ref[...], floor)
            c_out[at] = crossed
            part = mm(crossed, o_ref[...])
            if place == 0:
                keep_ref[...] = part
            else:
                send_ref[...] = part.astype(LOW)

    return call(
        kernel,
        (
            shape((2 * half, local), LOW),
            shape((2 * half, local), LOW),
            shape((half, width), WIDE),
            shape((half, width), LOW),
        ),
        spot,
        (marks, emarks, low, other, w_cq, keys, values, w_co, small),
        flops=8 * half * width * local,
        limit=16,
        parked=(1,),
        saved=(2, 3),
    )


def ffn_forward(low, other, w_fi, w_fo, shift):
    half, width = low.shape
    wide = w_fi.shape[1]

    def kernel(spot_ref, a_ref, b_ref, w_ref, o_ref, shift_ref, g_ref, slope_ref, keep_ref, send_ref):
        for place, ref in enumerate((a_ref, b_ref)):
            at = slice(place * half, (place + 1) * half)
            pre = mm(ref[...], w_ref[...]) + shift_ref[...]
            bell = 0.5 * (1.0 + lax.erf(pre * (0.5**0.5)))
            act = (pre * bell).astype(LOW)
            g_ref[at] = act
            slope_ref[at] = bell + pre * jnp.exp(-0.5 * pre * pre) * 0.3989422804014327
            part = mm(act, o_ref[...])
            if place == 0:
                keep_ref[...] = part
            else:
                send_ref[...] = part.astype(LOW)

    return call(
        kernel,
        (
            shape((2 * half, wide), LOW),
            shape((2 * half, wide), WIDE),
            shape((half, width), WIDE),
            shape((half, width), LOW),
        ),
        jnp.zeros((1,), jnp.int32),
        (low, other, w_fi, w_fo, shift),
        flops=8 * half * width * wide,
    )


def norm_back(grad, normal, rate, gain):
    up = grad * gain
    mean_up = jnp.mean(up, axis=-1, keepdims=True)
    mean_both = jnp.mean(up * normal, axis=-1, keepdims=True)
    return rate * (up - mean_up - normal * mean_both)


def column_rows(*values):
    rows = [jnp.sum(value.astype(WIDE), axis=0, keepdims=True) for value in values]
    return rows


def turn_around(residual, mine, other, table, own_grad, other_grad, tokens):
    rows, width = mine.shape

    def kernel(spot_ref, r_ref, mine_ref, other_ref, table_ref, a_ref, b_ref, out_ref, d_ref, low_ref, sum_ref):
        total = r_ref[...] + mine_ref[...] + turned_halves(other_ref) + table_ref[9:10]
        normal, rate = norm_rows(total)
        gain = table_ref[12:13]
        out_ref[...] = (normal[:tokens] * gain + table_ref[2:3]).astype(LOW)
        grad = jnp.concatenate([a_ref[:tokens], b_ref[:tokens]], axis=0).astype(WIDE)
        back = norm_back(grad, normal, rate, gain)
        low = back.astype(LOW)
        d_ref[...] = back
        low_ref[...] = low
        rows = column_rows(grad, grad * normal, low)
        for i in range(3):
            sum_ref[i : i + 1] = rows[i]

    return call(
        kernel,
        (
            shape((tokens, width), LOW),
            shape((rows, width), WIDE),
            shape((rows, width), LOW),
            shape((3, width), WIDE),
        ),
        jnp.zeros((1,), jnp.int32),
        (residual, mine, other, table, own_grad, other_grad),
        piped=True,
    )


def residual_back(previous, mine, other, normal, rate, table, norm_row, tokens):
    rows, width = mine.shape

    def kernel(spot_ref, p_ref, mine_ref, other_ref, n_ref, rate_ref, table_ref, d_ref, low_ref, sum_ref):
        grad = p_ref[...] + mine_ref[...] + turned_halves(other_ref)
        normal = n_ref[...]
        back = norm_back(grad, normal, rate_ref[...], table_ref[10 + norm_row : 11 + norm_row])
        low = back.astype(LOW)
        d_ref[...] = back
        low_ref[...] = low
        rows = column_rows(grad, grad * normal, low)
        for i in range(3):
            sum_ref[i : i + 1] = rows[i]

    return call(
        kernel,
        (shape((rows, width), WIDE), shape((rows, width), LOW), shape((3, width), WIDE)),
        jnp.zeros((1,), jnp.int32),
        (previous, mine, other, normal, rate, table),
    )


def ffn_back(low, other, w_fo, w_fi, slope):
    half, width = low.shape
    wide = w_fi.shape[1]

    def kernel(spot_ref, a_ref, b_ref, o_ref, w_ref, slope_ref, u_ref, keep_ref, send_ref, sum_ref):
        total = None
        for place, ref in enumerate((a_ref, b_ref)):
            at = slice(place * half, (place + 1) * half)
            inner = (mm_nt(ref[...], o_ref[...]) * slope_ref[at]).astype(LOW)
            u_ref[at] = inner
            row = column_rows(inner)[0]
            total = row if total is None else total + row
            part = mm_nt(inner, w_ref[...])
            if place == 0:
                keep_ref[...] = part
            else:
                send_ref[...] = part.astype(LOW)
        sum_ref[...] = total

    return call(
        kernel,
        (
            shape((2 * half, wide), LOW),
            shape((half, width), WIDE),
            shape((half, width), LOW),
            shape((1, wide), WIDE),
        ),
        jnp.zeros((1,), jnp.int32),
        (low, other, w_fo, w_fi, slope),
        flops=8 * half * width * wide,
        piped=True,
    )


def cross_back(spot, marks, emarks, low, other, w_co, queries, keys, values, w_cq, tokens):
    half, width = low.shape
    count, local = keys.shape

    def kernel(spot_ref, marks_ref, emarks_ref, a_ref, b_ref, co_ref, q_ref, k_ref, v_ref, cq_ref, *outs):
        dq_ref, dkv_ref, keep_ref, send_ref, sum_ref = outs
        key_grad = value_grad = None
        tall = []
        for i in range(count // 128):
            tall.append(upright(emarks_ref[:, i * 128 : (i + 1) * 128])[:, :1])
        tall = jnp.concatenate(tall, axis=0)
        totals = None
        for place, ref in enumerate((a_ref, b_ref)):
            at = slice(place * half, (place + 1) * half)
            grads = mm_nt(ref[...], co_ref[...]).astype(LOW)
            floor = jnp.where(tall == marks_ref[:, at], 0.0, FLOOR_SCORE)
            dq, dk, dv = attend_rows_back(q_ref[at], k_ref[...], v_ref[...], grads, floor)
            pre = (dq.astype(LOW).astype(WIDE) * SCALE).astype(LOW)
            dq_ref[at] = pre
            key_grad = dk if key_grad is None else key_grad + dk
            value_grad = dv if value_grad is None else value_grad + dv
            row = column_rows(pre)[0]
            totals = row if totals is None else totals + row
            part = mm_nt(pre, cq_ref[...])
            if place == 0:
                keep_ref[...] = part
            else:
                send_ref[...] = part.astype(LOW)
        dkv_ref[:, :local] = key_grad.astype(LOW)
        dkv_ref[:, local:] = value_grad.astype(LOW)
        sum_ref[0:1] = totals
        sum_ref[1:2] = column_rows(value_grad)[0]

    return call(
        kernel,
        (
            shape((2 * half, local), LOW),
            shape((count, 2 * local), LOW),
            shape((half, width), WIDE),
            shape((half, width), LOW),
            shape((2, local), WIDE),
        ),
        spot,
        (marks, emarks, low, other, w_co, queries, keys, values, w_cq),
        flops=8 * half * width * local,
        limit=16,
        cold=(4, 5, 6, 7, 8),
        saved=(2, 3),
    )


def self_back(spot, marks, low, other, w_so, queries, keys, values, tokens):
    half, width = low.shape
    count, local = keys.shape
    rows = 2 * half
    size = block_rows(count)

    def kernel(spot_ref, marks_ref, a_ref, b_ref, so_ref, q_ref, k_ref, v_ref, dq_ref, dkv_ref, sum_ref, dk_ref, dv_ref):
        totals = None
        for begin in range(0, rows, size):
            source = a_ref if begin < half else b_ref
            local_at = begin % half
            grads = mm_nt(source[local_at : local_at + size], so_ref[...]).astype(LOW)
            blocks = range(begin // tokens, (begin + size) // tokens)
            floor = self_floor(spot_ref, marks_ref, blocks, tokens, True)
            at = slice(begin, begin + size)
            dq, dk, dv = attend_rows_back(q_ref[at], k_ref[...], v_ref[...], grads, floor)
            pre = (dq.astype(LOW).astype(WIDE) * SCALE).astype(LOW)
            dq_ref[at] = pre
            row = column_rows(pre)[0]
            totals = row if totals is None else totals + row
            if begin == 0:
                dk_ref[...] = dk
                dv_ref[...] = dv
            else:
                dk_ref[...] += dk
                dv_ref[...] += dv
        dkv_ref[:, :local] = dk_ref[...].astype(LOW)
        dkv_ref[:, local:] = dv_ref[...].astype(LOW)
        sum_ref[0:1] = totals
        sum_ref[1:2] = column_rows(dv_ref[...])[0]

    return call(
        kernel,
        (shape((rows, local), LOW), shape((count, 2 * local), LOW), shape((2, local), WIDE)),
        spot,
        (marks, low, other, w_so, queries, keys, values),
        flops=10 * rows * keys.size,
        scratch=[pltpu.VMEM((count, local), WIDE), pltpu.VMEM((count, local), WIDE)],
        limit=24,
        cold=(3, 4, 5, 6),
    )


def input_back(query_grad, pair_grad, source_grad, w_q, w_kv, w_ckv, tokens, sources):
    width = w_q.shape[0]
    span = tokens + sources

    def kernel(spot_ref, q_ref, kv_ref, s_ref, wq_ref, wkv_ref, ws_ref, keep_ref, send_ref):
        part = mm_nt(q_ref[...], wq_ref[...]) + mm_nt(kv_ref[...], wkv_ref[...])
        more = mm_nt(s_ref[...], ws_ref[...])
        for kc, ref in enumerate((keep_ref, send_ref)):
            for kx in range(2):
                at = 2 * kc + kx
                start = kx * span
                piece = part[at * tokens : (at + 1) * tokens]
                ref[start : start + tokens] = piece.astype(ref.dtype)
                piece = more[at * sources : (at + 1) * sources]
                ref[start + tokens : start + span] = piece.astype(ref.dtype)

    return call(
        kernel,
        (shape((2 * span, width), WIDE), shape((2 * span, width), LOW)),
        jnp.zeros((1,), jnp.int32),
        (query_grad, pair_grad, source_grad, w_q, w_kv, w_ckv),
        flops=2 * query_grad.shape[0] * (w_q.size + w_kv.size),
        piped=True,
    )


def produce_ffn(spot, activated, grad_low, grad_other, low, other, inner_grad):
    wide = activated.shape[1]
    half, width = grad_low.shape
    part = width // 16

    def kernel(spot_ref, a_ref, g0_ref, g1_ref, x0_ref, x1_ref, u_ref, *refs):
        outs, all_ref = refs[:4], refs[4]
        me = spot_ref[0]
        high = spot_ref[1]
        low = spot_ref[2]
        for place in range(2):
            if place == 0:
                result = mm_tn(a_ref[:half], g0_ref[...]) + mm_tn(a_ref[half:], g1_ref[...])
            else:
                result = mm_tn(x0_ref[...], u_ref[:half]) + mm_tn(x1_ref[...], u_ref[half:])
            for d in range(4):
                for z in range(2):
                    for y in range(2):
                        at = (4 * d + 2 * z + y) * part
                        piece = result[at : at + part]
                        if place == 0:
                            all_ref[low ^ y, high ^ z, d] = piece
                        else:
                            all_ref[high ^ z, low ^ y, me ^ d] = piece
            outs[2 * place][...] = all_ref[0]
            outs[2 * place + 1][...] = all_ref[1].astype(LOW)

    piece = (2, 4, part, width)
    return call(
        kernel,
        (shape(piece, WIDE), shape(piece, LOW)) * 2,
        spot,
        (activated, grad_low, grad_other, low, other, inner_grad),
        flops=8 * half * width * wide,
        scratch=[pltpu.VMEM((2,) + piece, WIDE)],
        limit=16,
        piped=True,
    )


def join_ffn(out_half, out_got, in_half, in_got):
    def kernel(spot_ref, a_ref, b_ref, c_ref, d_ref, out_ref):
        out_ref[0] = (a_ref[0] + b_ref[...].astype(WIDE)).astype(LOW)
        out_ref[1] = (c_ref[0] + d_ref[...].astype(WIDE)).astype(LOW)

    return call(
        kernel,
        shape((2,) + out_got.shape, LOW),
        jnp.zeros((1,), jnp.int32),
        (out_half, out_got, in_half, in_got),
    )


def finish_ffn(spot, out_pieces, in_pieces):
    part, width = out_pieces[0].shape[1:]
    rows = 4 * part

    def kernel(spot_ref, oa_ref, ob_ref, oc_ref, ia_ref, ib_ref, ic_ref, fo_ref, fi_ref):
        me = spot_ref[0]
        high = spot_ref[1]
        low = spot_ref[2]
        for kz in range(2):
            for ky in range(2):
                quarter = ((kz ^ high) * 2 + (ky ^ low)) * part
                source = oc_ref.at[ky] if kz else (ob_ref if ky else oa_ref)
                for d in range(4):
                    row = pl.multiple_of(d * rows + quarter, 16)
                    fo_ref[pl.ds(row, part), :] = source[d].astype(WIDE)
                source = ic_ref.at[kz] if ky else (ib_ref if kz else ia_ref)
                row = pl.multiple_of(quarter, 16)
                for j in range(4):
                    fi_ref[pl.ds(row, part), j * width : (j + 1) * width] = source[me ^ j].astype(WIDE)

    return call(
        kernel,
        (shape((4 * rows, width), WIDE), shape((rows, 4 * width), WIDE)),
        spot,
        tuple(out_pieces) + tuple(in_pieces),
        limit=16,
        piped=True,
    )


def produce_mixed(spot, one_in, one_grad, two_in, two_grad, heads, heads_grads):
    rows, local = one_grad.shape
    width = one_in.shape[1]
    part = local // 4
    pieces = len(heads_grads)
    half = rows // pieces

    def kernel(spot_ref, a_ref, ag_ref, b_ref, bg_ref, o_ref, *refs):
        g_refs, (keep_ref, send_ref, all_ref) = refs[:pieces], refs[pieces:]
        me = spot_ref[0]
        high = spot_ref[1]
        low = spot_ref[2]
        one = mm_tn(a_ref[:rows], ag_ref[...])
        two = mm_tn(b_ref[...], bg_ref[...])
        three = mm_tn(o_ref[:half], g_refs[0][...])
        if pieces == 2:
            three = three + mm_tn(o_ref[half:], g_refs[1][...])
        for z in range(2):
            for y in range(2):
                quarter = (2 * z + y) * part
                for d in range(4):
                    at = d * local + quarter
                    all_ref[low ^ y, high ^ z, me ^ d, :, :local] = one[at : at + part]
                    all_ref[low ^ y, high ^ z, me ^ d, :, local : 3 * local] = two[at : at + part]
                    piece = three[quarter : quarter + part, d * local : (d + 1) * local]
                    all_ref[low ^ y, high ^ z, d, :, 3 * local :] = piece
        keep_ref[...] = all_ref[0]
        send_ref[...] = all_ref[1].astype(LOW)

    operands = (one_in, one_grad, two_in, two_grad, heads) + tuple(heads_grads)
    wide = two_in.shape[0] > 2048
    return call(
        kernel,
        (shape((2, 4, part, width), WIDE), shape((2, 4, part, width), LOW)),
        spot,
        operands,
        flops=2 * width * (one_grad.size + two_grad.size + heads.size),
        scratch=[pltpu.VMEM((2, 2, 4, part, width), WIDE)],
        cold=() if wide else (0, 2, 4) + ((5,) if pieces == 1 else ()),
        piped=wide,
    )


def place_mixed(spot, pieces, late, far_first, fused, earlier=()):
    part, width = pieces.shape[2:]
    local = 4 * part

    def kernel(spot_ref, piece_ref, *refs):
        outs = refs[len(earlier) :]
        me = spot_ref[0]
        for j in range(4):
            block = piece_ref[0, me ^ j].astype(WIDE)
            for p in range(3):
                piece = block[:, p * local : (p + 1) * local]
                if fused:
                    out, at = outs[0], p * width + j * local
                elif p == 0:
                    out, at = outs[0], j * local
                else:
                    out, at = outs[1], (p - 1) * width + j * local
                out[:, at : at + local] = piece
            outs[-1][:, j * local : (j + 1) * local] = piece_ref[0, j, :, 3 * local :].astype(WIDE)

    def source(i, spot):
        return (i ^ spot[1] if far_first else i ^ spot[2], 0, 0, 0)

    def target(i, spot):
        return (2 * i + (spot[2] ^ late) if far_first else 2 * (spot[1] ^ late) + i, 0)

    widths = (3 * width, width) if fused else (width, 2 * width, width)
    outs = tuple(shape((local, w), WIDE) for w in widths)
    return pl.pallas_call(
        kernel,
        out_shape=outs,
        grid_spec=pltpu.PrefetchScalarGridSpec(
            num_scalar_prefetch=1,
            grid=(2,),
            in_specs=[pl.BlockSpec((1, 4, part, width), source)]
            + [pl.BlockSpec(memory_space=pl.ANY) for _ in earlier],
            out_specs=tuple(pl.BlockSpec((part, w), target) for w in widths),
        ),
        input_output_aliases={2 + at: at for at in range(len(earlier))},
        cost_estimate=cost(0, pieces, *outs),
        compiler_params=pltpu.CompilerParams(vmem_limit_bytes=12 << 20),
    )(spot, pieces, *earlier)


def widen_rows(value, tokens):
    rows, width = value.shape

    def kernel(spot_ref, x_ref, top_ref, rest_ref):
        top_ref[...] = x_ref[:tokens].astype(WIDE)
        rest_ref[...] = x_ref[tokens:].astype(WIDE)

    return call(
        kernel,
        (shape((tokens, width), WIDE), shape((rows - tokens, width), WIDE)),
        jnp.zeros((1,), jnp.int32),
        (value,),
    )


def settle(value, *holds):
    def kernel(spot_ref, x_ref, out_ref):
        out_ref[...] = x_ref[...]

    return call(kernel, shape(value.shape, value.dtype), jnp.zeros((1,), jnp.int32), (after(value, *holds),))


def sort_vectors(value, got):
    rows, width = value.shape
    order = (0, 3, 6, 9, 10, 2, 11, 12, 5, 8)

    def kernel(spot_ref, a_ref, b_ref, bias_ref, gain_ref, inner_ref):
        total = a_ref[...] + b_ref[...]
        for at, source in enumerate(order):
            bias_ref[at : at + 1] = total[source : source + 1]
        for at, source in enumerate((1, 4, 7)):
            gain_ref[at : at + 1] = total[source : source + 1]
        for at in range(4):
            inner_ref[at : at + 1] = total[13 + at : 14 + at]

    return call(
        kernel,
        (shape((10, width), WIDE), shape((3, width), WIDE), shape((4, width), WIDE)),
        jnp.zeros((1,), jnp.int32),
        (value, got),
    )


def exchange_sum(keep, send, bit, *holds):
    got = flip_ctx(send, bit)
    if holds:
        got = after(got, *holds)
    return keep + got.astype(WIDE)


def sum_rest(total, *holds):
    lines = lax.axis_size("ctx") // lax.axis_size("fsdp")
    for bit in powers(lax.axis_size("ctx")):
        if bit not in (1, lines):
            low = total.astype(LOW)
            total = low.astype(WIDE) + after(flip_ctx(low, bit), *holds).astype(WIDE)
    return total.astype(LOW)


def trade_columns(low):
    part = low.shape[1]
    local = 4 * part
    far = flip_model(low[2:], 2)
    near = flip_model(jnp.stack([low[1], far[1]]), 1)
    columns = jnp.stack([low[0], near[0], far[0], near[1]])
    return jnp.concatenate([columns[..., : 3 * local], low[..., 3 * local :]], axis=-1)


def gather_pieces(piece, bits, *holds):
    first = after(flip_ctx(piece, bits[0]), *holds)
    both = jnp.stack([piece, first])
    return piece, first, flip_ctx(both, bits[1]), both


def move_columns(mate, cross, *holds):
    line = flip_ctx(after(cross, *holds), 1)
    return flip_model(mate, 1), cross, line, flip_model(cross, 1), flip_model(line, 1)


def core_sum(keep, send):
    mine = keep + flip_model(send, 1).astype(WIDE)
    return mine, flip_model(mine.astype(LOW), 2)


def sum_lines(value):
    for bit in reversed(line_bits()):
        value = value[:bit].astype(WIDE) + flip_ctx(value[bit:], bit).astype(WIDE)
        value = value.astype(LOW)
    return value[0]


def body(
    hidden,
    encoded,
    cotangent,
    dec_seg,
    enc_seg,
    self_qkv,
    self_out,
    cross_q,
    cross_kv,
    cross_out,
    ffn_in,
    ffn_out,
    biases,
    gains,
    ffn_bias,
):
    tokens = hidden.shape[1]
    rows = 4 * tokens
    width = hidden.shape[2]
    sources = encoded.shape[1]
    model = lax.axis_size("fsdp")
    lines = lax.axis_size("ctx") // model
    own = lax.axis_index("fsdp")
    ctx_index = lax.axis_index("ctx")
    local = width // model
    spot = jnp.stack([own, (ctx_index // lines) % 2, ctx_index % 2, ctx_index % lines])
    spot = spot.astype(jnp.int32)

    block = pack_rows(hidden[0], encoded[0], dec_seg, enc_seg)
    self_qkv = after(self_qkv, block)
    block = swap_places(block)
    small = jnp.concatenate([biases, gains, jnp.zeros((3, local), WIDE)], axis=0)
    qkv_own, qkv_mate, qkv_away = prepare_qkv(spot, self_qkv, small)
    qkv_cross = flip_model(qkv_away, 2)
    rest_own, rest_mate, rest_away, w_so, w_co, w_fo = prepare_rest(
        spot, cross_q, cross_kv, ffn_in, self_out, cross_out, ffn_out
    )
    block = after(block, rest_away)
    block_far = flip_model(block, 2)
    qkv_blocks = (qkv_own,) + move_columns(qkv_mate, qkv_cross, block)
    near_rows = jnp.stack([block, block_far])[None]
    near_rows = after(near_rows, qkv_blocks[3])
    rest_cross = flip_model(after(rest_away, block_far), 2)
    for bit in line_bits():
        near_rows = jnp.concatenate([near_rows, flip_ctx(near_rows, bit)], axis=0)
    near_rows = after(near_rows, rest_cross, *qkv_blocks[1:])
    far_rows = flip_model(near_rows, 1)
    rest_blocks = (rest_own,) + move_columns(rest_mate, rest_cross, near_rows)

    inputs, source_rows, queries, keys, values, w_q, w_kv, table, marks, emarks = project(
        spot, near_rows, far_rows, qkv_blocks, tokens, sources
    )
    other = swap_places(after(cotangent[0], rest_cross))
    plain = keys.shape[0] > 2048
    line_ids = (ctx_index % lines) ^ jnp.arange(lines, dtype=jnp.int32)[:, None]
    model_ids = own ^ jnp.array([0, 2, 1, 3], jnp.int32)[None, :]
    starts = (model_ids * lines + line_ids) * tokens
    places = (starts[:, :, None] + jnp.arange(tokens, dtype=jnp.int32)).reshape(-1)
    if plain:
        attended, keep, send = plain_forward(marks, places, queries, keys, values, w_so)
    else:
        attended, keep, send = self_forward(spot, marks, queries, keys, values, w_so, tokens)
    keep, send = after(keep, other), after(send, other)
    mine, away = core_sum(keep, send)
    w_cq, w_ckv, w_fi, source_keys, source_values = arrange_rest(
        spot, rest_blocks, source_rows, table
    )
    away = after(away, w_cq)
    first, first_low, first_normal, first_rate = residual_norm(inputs, mine, away, table, 5, 0)
    first_other = flip_model(first_low, 1)
    other_far = flip_model(after(other, away), 2)
    small_low = small.astype(LOW).astype(WIDE)
    cross_queries, crossed, keep, send, first_all = cross_forward(
        spot, marks, emarks, first_low, first_other, w_cq, source_keys, source_values, w_co, small_low, tokens
    )
    keep, send = after(keep, other_far), after(send, other_far)
    mine, away = core_sum(keep, send)
    second, second_low, second_normal, second_rate = residual_norm(first, mine, away, table, 8, 1)
    second_other = flip_model(second_low, 1)
    inner_bias = ffn_bias.astype(LOW).astype(WIDE)[None]
    activated, slope, keep, send = ffn_forward(second_low, second_other, w_fi, w_fo, inner_bias)
    mine, away = core_sum(keep, send)
    result, third_grad, ffn_low, third_sums = turn_around(
        second, mine, away, table, other, other_far, tokens
    )

    ffn_other = flip_model(ffn_low, 1)
    inner_grad, keep, send, inner_sum = ffn_back(ffn_low, ffn_other, w_fo, w_fi, slope)
    mine, away = core_sum(keep, send)
    out_keep, out_send, in_keep, in_send = produce_ffn(
        spot, activated, ffn_low, ffn_other, second_low, second_other, inner_grad
    )
    away = after(away, in_keep)
    out_got = flip_ctx(out_send, 1)
    in_got = flip_ctx(in_send, lines)
    second_grad, cross_low, second_sums = residual_back(
        third_grad, mine, away, second_normal, second_rate, table, 1, tokens
    )
    cross_other = flip_model(cross_low, 1)
    result = swap_places(after(result, cross_low))
    cross_query_pre, source_grad, keep, send, cross_sums, cross_all = cross_back(
        spot, marks, emarks, cross_low, cross_other, w_co, cross_queries, source_keys, source_values, w_cq, tokens
    )
    keep, send = after(keep, out_got, in_got), after(send, out_got, in_got)
    mine, away = core_sum(keep, send)
    out_half = out_keep + after(out_got, mine).astype(WIDE)
    in_half = in_keep + after(in_got, mine).astype(WIDE)
    out_got = flip_ctx(out_half[1].astype(LOW), lines)
    in_got = flip_ctx(in_half[1].astype(LOW), 1)
    cross_keep, cross_send = produce_mixed(
        spot, after(first_all, result), cross_query_pre, source_rows, source_grad, crossed, (cross_all,)
    )
    away = after(away, cross_keep, out_got, in_got)
    first_grad, self_low, first_sums = residual_back(
        second_grad, mine, away, first_normal, first_rate, table, 0, tokens
    )
    self_other = flip_model(self_low, 1)
    cross_got = flip_ctx(cross_send, 1)
    ffn_total = join_ffn(out_half, after(out_got, self_low), in_half, after(in_got, self_low))
    self_low = after(self_low, ffn_total)
    if plain:
        self_query_pre, pair_grad, self_sums = plain_back(
            marks, places, self_low, self_other, w_so, queries, keys, values
        )
    else:
        self_query_pre, pair_grad, self_sums = self_back(
            spot, marks, self_low, self_other, w_so, queries, keys, values, tokens
        )
    self_keep, self_send = produce_mixed(
        spot, inputs, self_query_pre, inputs, pair_grad, attended, (self_low, self_other)
    )
    self_half = exchange_sum(self_keep, self_send, 1)
    cross_half = cross_keep + after(cross_got, self_keep).astype(WIDE)
    wide_rows = jnp.concatenate([first_sums, second_sums, third_sums], axis=0)
    wide_rows = wide_rows + after(flip_model(wide_rows, 1), cross_half)
    wide_rows = lax.dynamic_slice_in_dim(wide_rows, own * local, local, axis=1)
    vectors = jnp.concatenate(
        [wide_rows, after(self_sums, cross_half), after(cross_sums, cross_half), after(inner_sum, cross_half).reshape(-1, local)], axis=0
    )
    vectors = jnp.pad(vectors, ((0, 32 - vectors.shape[0]), (0, 0))).reshape(16, 2 * local)
    cross_total = exchange_sum(cross_half[0], cross_half[1].astype(LOW), lines, self_half)
    ffn_total = sum_rest(ffn_total, self_half)
    lined = jnp.concatenate(
        [
            pair_grad.reshape(lines, rows, 2 * local),
            source_grad.reshape(lines, 4 * sources, 2 * local),
            jnp.broadcast_to(vectors.astype(LOW)[None], (lines,) + vectors.shape),
        ],
        axis=1,
    )
    lined = sum_lines(after(lined, self_half))
    pair_own = lined[:rows]
    source_own = lined[rows : rows + 4 * sources]
    vectors = lined[rows + 4 * sources :].astype(WIDE)
    keep, send = input_back(
        self_query_pre, pair_own, source_own, w_q, w_kv, w_ckv, tokens, sources
    )
    both_half = keep + flip_model(send, 1).astype(WIDE)
    span = tokens + sources
    both = both_half[:span] + flip_model(both_half[span:].astype(LOW), 2).astype(WIDE)
    both = jnp.concatenate([both[:tokens] + first_grad[:tokens], both[tokens:]], axis=0)
    both = both.astype(LOW)
    hidden_grad, encoded_grad = widen_rows(swap_places(both), tokens)
    hidden_grad = hidden_grad[None]
    encoded_grad = encoded_grad[None]

    cross_total = after(cross_total, ffn_total)
    self_total = exchange_sum(self_half[0], self_half[1].astype(LOW), lines, lined, cross_total)
    ffn_far = flip_model(ffn_total[1, 2:], 2)
    ffn_near = flip_model(jnp.stack([ffn_total[1, 1], ffn_far[1]]), 1)
    ffn_piece = jnp.stack([ffn_total[1, 0], ffn_near[0], ffn_far[0], ffn_near[1]])
    out_pieces = gather_pieces(ffn_total[0], (1, lines))
    in_pieces = gather_pieces(ffn_piece, (lines, 1))
    cross_piece = sum_rest(cross_total, self_total)
    self_piece = sum_rest(self_total, out_pieces[1])
    self_traded = trade_columns(self_piece)
    cross_pieces = gather_pieces(trade_columns(cross_piece), (1, lines), self_traded)
    cross_early = place_mixed(spot, cross_pieces[3], 0, False, False)
    vectors = vectors.reshape(-1, local)
    bits = powers(lax.axis_size("ctx"))[len(line_bits()) :]
    for bit in bits[:-1]:
        vectors = vectors + after(flip_ctx(vectors, bit), self_traded)
    self_pieces = gather_pieces(self_traded, (lines, 1), vectors)
    g_fo, g_fi = finish_ffn(spot, out_pieces[:3], in_pieces[:3])
    self_early = place_mixed(spot, self_pieces[3], 0, True, True)
    output = settle(result, self_piece)[None]
    last = after(self_pieces[2], g_fi, output, cross_early[0], self_early[0])
    g_qkv, g_so = place_mixed(spot, last, 1, True, True, self_early)
    g_cq, g_ckv, g_co = place_mixed(spot, cross_pieces[2], 1, False, False, cross_early)
    d_bias, d_gain, d_inner = sort_vectors(vectors, after(flip_ctx(vectors, bits[-1]), g_fi))
    d_inner = d_inner.reshape(-1)
    return (
        output,
        hidden_grad,
        encoded_grad,
        g_qkv,
        g_so,
        g_cq,
        g_ckv,
        g_co,
        g_fi,
        g_fo,
        d_bias,
        d_gain,
        d_inner,
    )


def solution(mesh):
    whole = P("fsdp", "ctx", None)
    matrix = P("fsdp", None)
    ids = P("fsdp", "ctx")
    table = P(None, "fsdp")
    return jax.shard_map(
        body,
        mesh=mesh,
        in_specs=(whole, whole, whole, ids, ids) + (matrix,) * 7 + (table, table, P("fsdp")),
        out_specs=(whole,) * 3 + (matrix,) * 7 + (table, table, P("fsdp")),
        check_vma=False,
    )
```

```python
import jax
import jax.numpy as jnp
from jax import lax
from jax.experimental import pallas as pl
from jax.experimental.pallas import tpu as pltpu
from jax.sharding import PartitionSpec as P

H = 12
HD = 64
EPSILON = 1e-05
FLOOR_SCORE = -1e30
SCALE = float(HD) ** (-0.5)
LOW = jnp.bfloat16
WIDE = jnp.float32


def mm(left, right):
    return jnp.dot(left, right, preferred_element_type=WIDE)


def mm_tn(left, right):
    return lax.dot_general(left, right, (((0,), (0,)), ((), ())), preferred_element_type=WIDE)


def mm_nt(left, right):
    return lax.dot_general(left, right, (((1,), (1,)), ((), ())), preferred_element_type=WIDE)


def flip_model(value, bit):
    count = lax.axis_size("fsdp")
    return lax.ppermute(value, "fsdp", [(i, i ^ bit) for i in range(count)])


def flip_ctx(value, bit):
    count = lax.axis_size("ctx")
    return lax.ppermute(value, "ctx", [(i, i ^ bit) for i in range(count)])


def swap_places(value):
    model = lax.axis_size("fsdp")
    ctx = lax.axis_size("ctx")
    lines = ctx // model
    route = []
    for f in range(model):
        for z in range(model):
            for r in range(lines):
                route.append((f * ctx + z * lines + r, z * ctx + f * lines + r))
    return lax.ppermute(value, ("fsdp", "ctx"), route)


def powers(limit):
    bits = []
    bit = 1
    while bit < limit:
        bits.append(bit)
        bit *= 2
    return bits


def line_bits():
    return powers(lax.axis_size("ctx") // lax.axis_size("fsdp"))


def after(value, *others):
    return lax.optimization_barrier((value,) + others)[0]


def shape(dims, kind):
    return jax.ShapeDtypeStruct(tuple(dims), kind)


COST = 5.0


def cost(flops, *arrays):
    count = 0
    for array in arrays:
        count += array.size * array.dtype.itemsize
    return pl.CostEstimate(
        flops=int(flops * COST), transcendentals=0, bytes_accessed=int(count * COST)
    )


def call(kernel, outs, spot, operands, flops=0, scratch=(), limit=12, piped=False, cold=(), parked=(), saved=()):
    many = isinstance(outs, tuple)
    listed = list(outs) if many else [outs]
    count = len(operands)
    if saved:
        first = operands[saved[0]]
        height = sum(operands[at].shape[0] for at in saved)
        listed.append(shape((height,) + first.shape[1:], first.dtype))
        many = True
    body = kernel
    if cold or parked or saved:
        place = pl.BlockSpec(memory_space=pltpu.VMEM)
        far = pl.BlockSpec(memory_space=pltpu.HBM)
        own = count + len(listed) + len(scratch)

        def body(spot_ref, *all_refs):
            refs, buffers, done = list(all_refs[:own]), list(all_refs[own:-1]), all_refs[-1]
            used = 0
            ending = []

            def copy(source, target):
                nonlocal used
                moving = pltpu.make_async_copy(source, target, done.at[used])
                used += 1
                return moving

            incoming = []
            for at in cold:
                buffer = buffers.pop(0)
                incoming.append(copy(refs[at], buffer))
                incoming[-1].start()
                refs[at] = buffer
            row = 0
            for at in saved:
                target = refs[count + len(listed) - 1].at[pl.ds(row, operands[at].shape[0])]
                row += operands[at].shape[0]
                ending.append(copy(refs[at], target))
                ending[-1].start()
            for moving in incoming:
                moving.wait()
            outgoing = []
            for at in parked:
                buffer = buffers.pop(0)
                outgoing.append(copy(buffer, refs[count + at]))
                refs[count + at] = buffer
            if saved:
                refs.pop(count + len(listed) - 1)
            kernel(spot_ref, *refs)
            for moving in outgoing:
                moving.start()
            for moving in outgoing + ending:
                moving.wait()

        buffers = [pltpu.VMEM(operands[at].shape, operands[at].dtype) for at in cold]
        buffers += [pltpu.VMEM(listed[at].shape, listed[at].dtype) for at in parked]
        held = set(parked) | ({len(listed) - 1} if saved else set())
        out_specs = [far if at in held else place for at in range(len(listed))]
        moves = len(cold) + len(parked) + len(saved)
        spec = dict(
            in_specs=[pl.BlockSpec(memory_space=pltpu.SMEM)]
            + [far if at in cold else place for at in range(count)],
            out_specs=tuple(out_specs) if many else out_specs[0],
            scratch_shapes=list(scratch) + buffers + [pltpu.SemaphoreType.DMA((moves,))],
        )
        limit = limit + 8
    elif piped:
        place = lambda value: pl.BlockSpec(value.shape, lambda i, spot: (0,) * len(value.shape))
        spec = dict(
            grid_spec=pltpu.PrefetchScalarGridSpec(
                num_scalar_prefetch=1,
                grid=(1,),
                in_specs=[place(value) for value in operands],
                out_specs=tuple(place(value) for value in listed) if many else place(outs),
                scratch_shapes=list(scratch),
            )
        )
        limit = limit + 12
    else:
        place = pl.BlockSpec(memory_space=pltpu.VMEM)
        spec = dict(
            in_specs=[pl.BlockSpec(memory_space=pltpu.SMEM)] + [place] * count,
            out_specs=tuple(place for _ in listed) if many else place,
            scratch_shapes=list(scratch),
        )
    return pl.pallas_call(
        body,
        out_shape=tuple(listed) if many else outs,
        cost_estimate=cost(flops, *operands, *listed),
        compiler_params=pltpu.CompilerParams(vmem_limit_bytes=limit << 20),
        **spec,
    )(spot, *operands)


def pack_rows(tokens, sources, token_marks, source_marks):
    count, width = tokens.shape
    more = sources.shape[0]

    def kernel(spot_ref, x_ref, e_ref, m_ref, s_ref, out_ref):
        out_ref[:count] = x_ref[...]
        out_ref[count : count + more] = e_ref[...]
        out_ref[count + more :] = jnp.zeros((16, width), LOW)
        first = jnp.broadcast_to(m_ref[...], (16, count)).astype(WIDE).astype(LOW)
        second = jnp.broadcast_to(s_ref[...], (16, more)).astype(WIDE).astype(LOW)
        out_ref[count + more :, :count] = first
        out_ref[count + more :, count : count + more] = second

    return call(
        kernel,
        shape((count + more + 16, width), LOW),
        jnp.zeros((1,), jnp.int32),
        (tokens, sources, token_marks, source_marks),
        piped=True,
    )


def prepare_qkv(spot, weight, small):
    rows = weight.shape[0]

    def kernel(spot_ref, w_ref, small_ref, own_ref, near_ref, far_ref, all_ref):
        me = spot_ref[0]
        side = spot_ref[2]
        small = small_ref[...].astype(LOW)
        tail = jnp.zeros((16, 2 * rows), LOW)
        for d in range(4):
            for p in range(3):
                piece = w_ref[:, p * 4 * rows + d * rows : p * 4 * rows + (d + 1) * rows]
                all_ref[me ^ d, :, p * rows : (p + 1) * rows] = piece.astype(LOW)
        own_ref[:rows] = all_ref[0]
        near_ref[:rows] = all_ref[1]
        far_ref[:rows] = all_ref[2 + side]
        for ref in (own_ref, near_ref, far_ref):
            ref[rows:, :rows] = small
            ref[rows:, rows:] = tail

    piece = (rows + 16, 3 * rows)
    return call(
        kernel,
        (shape(piece, LOW),) * 3,
        spot,
        (weight, small),
        scratch=[pltpu.VMEM((4, rows, 3 * rows), LOW)],
    )


def prepare_rest(spot, cross_q, cross_kv, ffn_in, self_out, cross_out, ffn_out):
    rows = cross_q.shape[0]
    wide = ffn_in.shape[1] // 4
    piece = (rows, 3 * rows + wide)

    def kernel(spot_ref, q_ref, kv_ref, fi_ref, so_ref, co_ref, fo_ref, *outs):
        own_ref, near_ref, far_ref, so_out, co_out, fo_out, all_ref = outs
        me = spot_ref[0]
        side = spot_ref[2]
        for d in range(4):
            all_ref[me ^ d, :, :rows] = q_ref[:, d * rows : (d + 1) * rows].astype(LOW)
            for p in range(2):
                part = kv_ref[:, (p * 4 + d) * rows : (p * 4 + d + 1) * rows]
                all_ref[me ^ d, :, (1 + p) * rows : (2 + p) * rows] = part.astype(LOW)
            all_ref[me ^ d, :, 3 * rows :] = fi_ref[:, d * wide : (d + 1) * wide].astype(LOW)
        own_ref[...] = all_ref[0]
        near_ref[...] = all_ref[1]
        far_ref[...] = all_ref[2 + side]
        so_out[...] = so_ref[...].astype(LOW)
        co_out[...] = co_ref[...].astype(LOW)
        fo_out[...] = fo_ref[...].astype(LOW)

    return call(
        kernel,
        (shape(piece, LOW),) * 3
        + (shape(self_out.shape, LOW), shape(cross_out.shape, LOW), shape(ffn_out.shape, LOW)),
        spot,
        (cross_q, cross_kv, ffn_in, self_out, cross_out, ffn_out),
        scratch=[pltpu.VMEM((4,) + piece, LOW)],
        limit=16,
        piped=True,
    )


def ordered_blocks(spot_ref, refs, pair_ref):
    side = spot_ref[2]
    pair_ref[0, side] = refs[2][...]
    pair_ref[0, 1 - side] = refs[3][...]
    pair_ref[1, side] = refs[4][...]
    pair_ref[1, 1 - side] = refs[5][...]
    return refs[0][...], refs[1][...], pair_ref[0, 0], pair_ref[1, 1]


def arrange_rest(spot, blocks, source_rows, table):
    rows = blocks[0].shape[0]
    wide = blocks[0].shape[1] - 3 * rows
    count, width = source_rows.shape

    def kernel(spot_ref, *refs):
        x_ref, table_ref, q_ref, kv_ref, fi_ref, *outs = refs[6:]
        keys_ref, values_ref, rel_ref, pair_ref = outs
        me = spot_ref[0]
        parts = ordered_blocks(spot_ref, refs[:6], pair_ref)
        for k in range(4):
            start = pl.multiple_of((me ^ k) * rows, 64)
            q_ref[pl.ds(start, rows), :] = parts[k][:, :rows]
            kv_ref[pl.ds(start, rows), :] = parts[k][:, rows : 3 * rows]
            fi_ref[pl.ds(start, rows), :] = parts[k][:, 3 * rows :]
        for j in range(4):
            rel_ref[j] = table_ref[:, j * rows : (j + 1) * rows]
        shift = rel_ref[me][7:8]
        out = mm(x_ref[...], kv_ref[...])
        keys_ref[...] = out[:, :rows].astype(LOW)
        values_ref[...] = (out[:, rows:] + shift).astype(LOW)

    return call(
        kernel,
        (
            shape((4 * rows, rows), LOW),
            shape((4 * rows, 2 * rows), LOW),
            shape((4 * rows, wide), LOW),
            shape((count, rows), LOW),
            shape((count, rows), LOW),
        ),
        spot,
        tuple(blocks) + (source_rows, table),
        flops=4 * count * width * rows,
        scratch=[pltpu.VMEM((4, 16, rows), WIDE), pltpu.VMEM((2, 2) + blocks[0].shape, LOW)],
        limit=16,
    )


def project(spot, near_rows, far_rows, blocks, tokens, sources):
    lines = near_rows.shape[0]
    width = near_rows.shape[-1]
    local = width // 4
    span = near_rows.shape[2]
    rows = 4 * tokens

    def kernel(spot_ref, a_ref, b_ref, *refs):
        x_ref, e_ref, q_ref, k_ref, v_ref, wq_ref, wkv_ref, table_ref, *outs = refs[6:]
        marks_ref, emarks_ref, rel_ref, w_ref, pair_ref = outs
        me = spot_ref[0]

        @pl.when(pl.program_id(0) == 0)
        def _():
            parts = ordered_blocks(spot_ref, refs[:6], pair_ref)
            for k in range(4):
                start = pl.multiple_of((me ^ k) * local, 64)
                w_ref[pl.ds(start, local), :] = parts[k][:local]
                rel_ref[k] = parts[k][local:, :local].astype(WIDE)
            for j in range(4):
                table_ref[:, j * local : (j + 1) * local] = rel_ref[me ^ j]
            wq_ref[...] = w_ref[:, :local]
            wkv_ref[...] = w_ref[:, local:]

        lane = lax.broadcasted_iota(jnp.int32, (1, 128), 1)
        emarks = jnp.zeros((1, 128), WIDE)
        for kc, ref in enumerate((a_ref, b_ref)):
            for kx in range(2):
                at = 2 * kc + kx
                start = at * tokens
                x_ref[start : start + tokens, :] = ref[0, kx, :tokens, :]
                e_ref[at * sources : (at + 1) * sources, :] = ref[0, kx, tokens : tokens + sources, :]
                marks = ref[0, kx, tokens + sources : tokens + sources + 16, :256].astype(WIDE)
                marks_ref[:, start : start + tokens] = marks[0:1, :tokens]
                moved = pltpu.roll(marks[:8, 128:], at * sources, 1)[0:1]
                emarks = emarks + jnp.where((lane // sources) == at, moved, 0.0)
        emarks_ref[...] = emarks
        own_small = rel_ref[0]
        out = mm(x_ref[...], w_ref[...])
        k_ref[...] = out[:, local : 2 * local].astype(LOW)
        v_ref[...] = (out[:, 2 * local :] + own_small[4:5]).astype(LOW)

        @pl.when(pl.program_id(0) == 0)
        def _():
            q_ref[...] = ((out[:, :local] + own_small[3:4]) * SCALE).astype(LOW)

    full = lambda *dims: pl.BlockSpec(dims, lambda i, spot: (0,) * len(dims))
    band = lambda w: pl.BlockSpec((rows, w), lambda i, spot: (i, 0))
    part = pl.BlockSpec((1, 2, span, width), lambda i, spot: (i, 0, 0, 0))
    piece = (local + 16, 3 * local)
    outs = (
        shape((lines * rows, width), LOW),
        shape((lines * 4 * sources, width), LOW),
        shape((rows, local), LOW),
        shape((lines * rows, local), LOW),
        shape((lines * rows, local), LOW),
        shape((width, local), LOW),
        shape((width, 2 * local), LOW),
        shape((16, width), WIDE),
        shape((1, lines * rows), WIDE),
        shape((1, lines * 4 * sources), WIDE),
    )
    operands = (near_rows, far_rows) + tuple(blocks)
    return pl.pallas_call(
        kernel,
        out_shape=outs,
        grid_spec=pltpu.PrefetchScalarGridSpec(
            num_scalar_prefetch=1,
            grid=(lines,),
            in_specs=[part, part] + [full(*piece)] * 6,
            out_specs=(
                band(width),
                pl.BlockSpec((4 * sources, width), lambda i, spot: (i, 0)),
                full(rows, local),
                band(local),
                band(local),
                full(width, local),
                full(width, 2 * local),
                full(16, width),
                pl.BlockSpec((1, rows), lambda i, spot: (0, i)),
                pl.BlockSpec((1, 4 * sources), lambda i, spot: (0, i)),
            ),
            scratch_shapes=[
                pltpu.VMEM((4, 16, local), WIDE),
                pltpu.VMEM((width, 3 * local), LOW),
                pltpu.VMEM((2, 2) + piece, LOW),
            ],
        ),
        cost_estimate=cost(6 * lines * rows * width * local, *operands, *outs),
        compiler_params=pltpu.CompilerParams(vmem_limit_bytes=20 << 20),
    )(spot, *operands)


def block_start(spot_ref, index, tokens, lines):
    me = spot_ref[0]
    line = spot_ref[3]
    kr, kc, kx = index // 4, (index // 2) % 2, index % 2
    return ((me ^ (kc + 2 * kx)) * lines + (line ^ kr)) * tokens


def upright(row):
    return jnp.transpose(jnp.broadcast_to(row, (128, row.shape[1])))


def self_floor(spot_ref, marks_ref, query_blocks, tokens, turned):
    blocks = marks_ref.shape[1] // tokens
    lines = blocks // 4
    down = lax.broadcasted_iota(jnp.int32, (tokens, tokens), 0)
    right = lax.broadcasted_iota(jnp.int32, (tokens, tokens), 1)
    outer, inner = (range(blocks), query_blocks) if turned else (query_blocks, range(blocks))
    table = []
    for i in outer:
        tall = upright(marks_ref[:, i * tokens : (i + 1) * tokens])
        line = []
        for j in inner:
            flat = marks_ref[:, j * tokens : (j + 1) * tokens]
            gap = block_start(spot_ref, j, tokens, lines) - block_start(spot_ref, i, tokens, lines)
            ahead = (right + gap) - down
            near = (ahead >= 0) if turned else (ahead <= 0)
            line.append(jnp.where((tall == flat) & near, 0.0, FLOOR_SCORE))
        table.append(jnp.concatenate(line, axis=1))
    return jnp.concatenate(table, axis=0)


def head_lanes(value, head):
    lane = lax.broadcasted_iota(jnp.int32, (1, value.shape[1]), 1) // HD
    return jnp.where(lane == head, value, jnp.zeros_like(value))


def attend_rows(queries, keys, values, floor):
    heads = queries.shape[1] // HD
    total = None
    for h in range(heads):
        scores = mm_nt(head_lanes(queries, h), keys) + floor
        top = jnp.max(scores, axis=1, keepdims=True)
        weights = jnp.exp(scores - top)
        prob = weights * (1.0 / jnp.sum(weights, axis=1, keepdims=True))
        part = head_lanes(mm(prob.astype(LOW), values), h)
        total = part if total is None else total + part
    return total.astype(LOW)


def attend_rows_back(queries, keys, values, grads, floor):
    heads = queries.shape[1] // HD
    query_grad = key_grad = value_grad = None
    for h in range(heads):
        own_queries = head_lanes(queries, h)
        own_grads = head_lanes(grads, h)
        scores = mm_nt(keys, own_queries) + floor
        top = jnp.max(scores, axis=0, keepdims=True)
        weights = jnp.exp(scores - top)
        prob = weights * (1.0 / jnp.sum(weights, axis=0, keepdims=True))
        prob_grad = mm_nt(values, own_grads)
        inner = jnp.sum(prob * prob_grad, axis=0, keepdims=True)
        score_grad = (prob * (prob_grad - inner)).astype(LOW)
        part_q = head_lanes(mm_tn(score_grad, keys), h)
        part_k = mm(score_grad, own_queries)
        part_v = mm(prob.astype(LOW), own_grads)
        query_grad = part_q if query_grad is None else query_grad + part_q
        key_grad = part_k if key_grad is None else key_grad + part_k
        value_grad = part_v if value_grad is None else value_grad + part_v
    return query_grad, key_grad, value_grad


def block_rows(keys):
    return 256 if keys <= 1024 else 128


def self_forward(spot, marks, queries, keys, values, weight, tokens):
    rows, local = queries.shape
    width = weight.shape[1]
    size = block_rows(keys.shape[0])

    def kernel(spot_ref, marks_ref, q_ref, k_ref, v_ref, w_ref, o_ref, keep_ref, send_ref):
        for begin in range(0, rows, size):
            blocks = range(begin // tokens, (begin + size) // tokens)
            floor = self_floor(spot_ref, marks_ref, blocks, tokens, False)
            low = attend_rows(q_ref[begin : begin + size], k_ref[...], v_ref[...], floor)
            o_ref[begin : begin + size] = low
            part = mm(low, w_ref[...])
            if begin < rows // 2:
                keep_ref[begin : begin + size] = part
            else:
                send_ref[begin - rows // 2 : begin - rows // 2 + size] = part.astype(LOW)

    return call(
        kernel,
        (shape((rows, local), LOW), shape((rows // 2, width), WIDE), shape((rows // 2, width), LOW)),
        spot,
        (marks, queries, keys, values, weight),
        flops=4 * rows * keys.size + 2 * rows * weight.size,
        limit=20,
    )


def plain_floor(marks, places, rows):
    same = marks.reshape(-1)[:rows, None] == marks
    return jnp.where(same & (places[None, :] <= places[:rows, None]), 0.0, FLOOR_SCORE)


def plain_forward(marks, places, queries, keys, values, weight):
    rows = queries.shape[0]
    low = attend_rows(queries, keys, values, plain_floor(marks, places, rows))
    part = mm(low, weight)
    return low, part[: rows // 2], part[rows // 2 :].astype(LOW)


def plain_back(marks, places, low, other, w_so, queries, keys, values):
    grads = mm_nt(jnp.concatenate([low, other], axis=0), w_so).astype(LOW)
    floor = plain_floor(marks, places, queries.shape[0])
    dq, dk, dv = attend_rows_back(queries, keys, values, grads, floor.T)
    pre = (dq.astype(LOW).astype(WIDE) * SCALE).astype(LOW)
    sums = jnp.concatenate(column_rows(pre, dv), axis=0)
    return pre, jnp.concatenate([dk, dv], axis=1).astype(LOW), sums


def norm_rows(values):
    center = values - jnp.mean(values, axis=-1, keepdims=True)
    spread = jnp.mean(center * center, axis=-1, keepdims=True)
    rate = lax.rsqrt(spread + EPSILON)
    return center * rate, rate


def turned_halves(ref):
    half = ref.shape[0] // 2
    return jnp.concatenate([ref[half:], ref[:half]], axis=0).astype(WIDE)


def residual_norm(residual, mine, other, table, bias_row, norm_row):
    rows, width = mine.shape

    def kernel(spot_ref, r_ref, mine_ref, other_ref, table_ref, h_ref, low_ref, n_ref, rate_ref):
        total = r_ref[:rows].astype(WIDE) + mine_ref[...] + turned_halves(other_ref)
        normal, rate = norm_rows(total + table_ref[bias_row : bias_row + 1])
        gain = table_ref[10 + norm_row : 11 + norm_row]
        result = normal * gain + table_ref[norm_row : norm_row + 1]
        h_ref[...] = result
        low_ref[...] = result.astype(LOW)
        n_ref[...] = normal
        rate_ref[...] = rate

    return call(
        kernel,
        (
            shape((rows, width), WIDE),
            shape((rows, width), LOW),
            shape((rows, width), WIDE),
            shape((rows, 1), WIDE),
        ),
        jnp.zeros((1,), jnp.int32),
        (residual, mine, other, table),
    )


def cross_forward(spot, marks, emarks, low, other, w_cq, keys, values, w_co, small, tokens):
    half, width = low.shape
    local = w_cq.shape[1]

    def kernel(spot_ref, marks_ref, emarks_ref, a_ref, b_ref, w_ref, k_ref, v_ref, o_ref, small_ref, *outs):
        q_out, c_out, keep_ref, send_ref = outs
        for place, ref in enumerate((a_ref, b_ref)):
            at = slice(place * half, (place + 1) * half)
            low = ((mm(ref[...], w_ref[...]) + small_ref[6:7]) * SCALE).astype(LOW)
            q_out[at] = low
            tall = []
            for i in range(place * half // tokens, (place + 1) * half // tokens):
                tall.append(upright(marks_ref[:, i * tokens : (i + 1) * tokens])[:, :1])
            tall = jnp.concatenate(tall, axis=0)
            floor = jnp.where(tall == emarks_ref[...], 0.0, FLOOR_SCORE)
            crossed = attend_rows(low, k_ref[...], v_ref[...], floor)
            c_out[at] = crossed
            part = mm(crossed, o_ref[...])
            if place == 0:
                keep_ref[...] = part
            else:
                send_ref[...] = part.astype(LOW)

    return call(
        kernel,
        (
            shape((2 * half, local), LOW),
            shape((2 * half, local), LOW),
            shape((half, width), WIDE),
            shape((half, width), LOW),
        ),
        spot,
        (marks, emarks, low, other, w_cq, keys, values, w_co, small),
        flops=8 * half * width * local,
        limit=16,
        parked=(1,),
        saved=(2, 3),
    )


def ffn_forward(low, other, w_fi, w_fo, shift):
    half, width = low.shape
    wide = w_fi.shape[1]

    def kernel(spot_ref, a_ref, b_ref, w_ref, o_ref, shift_ref, g_ref, slope_ref, keep_ref, send_ref):
        for place, ref in enumerate((a_ref, b_ref)):
            at = slice(place * half, (place + 1) * half)
            pre = mm(ref[...], w_ref[...]) + shift_ref[...]
            bell = 0.5 * (1.0 + lax.erf(pre * (0.5**0.5)))
            act = (pre * bell).astype(LOW)
            g_ref[at] = act
            slope_ref[at] = bell + pre * jnp.exp(-0.5 * pre * pre) * 0.3989422804014327
            part = mm(act, o_ref[...])
            if place == 0:
                keep_ref[...] = part
            else:
                send_ref[...] = part.astype(LOW)

    return call(
        kernel,
        (
            shape((2 * half, wide), LOW),
            shape((2 * half, wide), WIDE),
            shape((half, width), WIDE),
            shape((half, width), LOW),
        ),
        jnp.zeros((1,), jnp.int32),
        (low, other, w_fi, w_fo, shift),
        flops=8 * half * width * wide,
    )


def norm_back(grad, normal, rate, gain):
    up = grad * gain
    mean_up = jnp.mean(up, axis=-1, keepdims=True)
    mean_both = jnp.mean(up * normal, axis=-1, keepdims=True)
    return rate * (up - mean_up - normal * mean_both)


def column_rows(*values):
    rows = [jnp.sum(value.astype(WIDE), axis=0, keepdims=True) for value in values]
    return rows


def turn_around(residual, mine, other, table, own_grad, other_grad, tokens):
    rows, width = mine.shape

    def kernel(spot_ref, r_ref, mine_ref, other_ref, table_ref, a_ref, b_ref, out_ref, d_ref, low_ref, sum_ref):
        total = r_ref[...] + mine_ref[...] + turned_halves(other_ref) + table_ref[9:10]
        normal, rate = norm_rows(total)
        gain = table_ref[12:13]
        out_ref[...] = (normal[:tokens] * gain + table_ref[2:3]).astype(LOW)
        grad = jnp.concatenate([a_ref[:tokens], b_ref[:tokens]], axis=0).astype(WIDE)
        back = norm_back(grad, normal, rate, gain)
        low = back.astype(LOW)
        d_ref[...] = back
        low_ref[...] = low
        rows = column_rows(grad, grad * normal, low)
        for i in range(3):
            sum_ref[i : i + 1] = rows[i]

    return call(
        kernel,
        (
            shape((tokens, width), LOW),
            shape((rows, width), WIDE),
            shape((rows, width), LOW),
            shape((3, width), WIDE),
        ),
        jnp.zeros((1,), jnp.int32),
        (residual, mine, other, table, own_grad, other_grad),
        piped=True,
    )


def residual_back(previous, mine, other, normal, rate, table, norm_row, tokens):
    rows, width = mine.shape

    def kernel(spot_ref, p_ref, mine_ref, other_ref, n_ref, rate_ref, table_ref, d_ref, low_ref, sum_ref):
        grad = p_ref[...] + mine_ref[...] + turned_halves(other_ref)
        normal = n_ref[...]
        back = norm_back(grad, normal, rate_ref[...], table_ref[10 + norm_row : 11 + norm_row])
        low = back.astype(LOW)
        d_ref[...] = back
        low_ref[...] = low
        rows = column_rows(grad, grad * normal, low)
        for i in range(3):
            sum_ref[i : i + 1] = rows[i]

    return call(
        kernel,
        (shape((rows, width), WIDE), shape((rows, width), LOW), shape((3, width), WIDE)),
        jnp.zeros((1,), jnp.int32),
        (previous, mine, other, normal, rate, table),
    )


def ffn_back(low, other, w_fo, w_fi, slope):
    half, width = low.shape
    wide = w_fi.shape[1]

    def kernel(spot_ref, a_ref, b_ref, o_ref, w_ref, slope_ref, u_ref, keep_ref, send_ref, sum_ref):
        total = None
        for place, ref in enumerate((a_ref, b_ref)):
            at = slice(place * half, (place + 1) * half)
            inner = (mm_nt(ref[...], o_ref[...]) * slope_ref[at]).astype(LOW)
            u_ref[at] = inner
            row = column_rows(inner)[0]
            total = row if total is None else total + row
            part = mm_nt(inner, w_ref[...])
            if place == 0:
                keep_ref[...] = part
            else:
                send_ref[...] = part.astype(LOW)
        sum_ref[...] = total

    return call(
        kernel,
        (
            shape((2 * half, wide), LOW),
            shape((half, width), WIDE),
            shape((half, width), LOW),
            shape((1, wide), WIDE),
        ),
        jnp.zeros((1,), jnp.int32),
        (low, other, w_fo, w_fi, slope),
        flops=8 * half * width * wide,
        piped=True,
    )


def cross_back(spot, marks, emarks, low, other, w_co, queries, keys, values, w_cq, tokens):
    half, width = low.shape
    count, local = keys.shape

    def kernel(spot_ref, marks_ref, emarks_ref, a_ref, b_ref, co_ref, q_ref, k_ref, v_ref, cq_ref, *outs):
        dq_ref, dkv_ref, keep_ref, send_ref, sum_ref = outs
        key_grad = value_grad = None
        tall = []
        for i in range(count // 128):
            tall.append(upright(emarks_ref[:, i * 128 : (i + 1) * 128])[:, :1])
        tall = jnp.concatenate(tall, axis=0)
        totals = None
        for place, ref in enumerate((a_ref, b_ref)):
            at = slice(place * half, (place + 1) * half)
            grads = mm_nt(ref[...], co_ref[...]).astype(LOW)
            floor = jnp.where(tall == marks_ref[:, at], 0.0, FLOOR_SCORE)
            dq, dk, dv = attend_rows_back(q_ref[at], k_ref[...], v_ref[...], grads, floor)
            pre = (dq.astype(LOW).astype(WIDE) * SCALE).astype(LOW)
            dq_ref[at] = pre
            key_grad = dk if key_grad is None else key_grad + dk
            value_grad = dv if value_grad is None else value_grad + dv
            row = column_rows(pre)[0]
            totals = row if totals is None else totals + row
            part = mm_nt(pre, cq_ref[...])
            if place == 0:
                keep_ref[...] = part
            else:
                send_ref[...] = part.astype(LOW)
        dkv_ref[:, :local] = key_grad.astype(LOW)
        dkv_ref[:, local:] = value_grad.astype(LOW)
        sum_ref[0:1] = totals
        sum_ref[1:2] = column_rows(value_grad)[0]

    return call(
        kernel,
        (
            shape((2 * half, local), LOW),
            shape((count, 2 * local), LOW),
            shape((half, width), WIDE),
            shape((half, width), LOW),
            shape((2, local), WIDE),
        ),
        spot,
        (marks, emarks, low, other, w_co, queries, keys, values, w_cq),
        flops=8 * half * width * local,
        limit=16,
        cold=(4, 5, 6, 7, 8),
        saved=(2, 3),
    )


def self_back(spot, marks, low, other, w_so, queries, keys, values, tokens):
    half, width = low.shape
    count, local = keys.shape
    rows = 2 * half
    size = block_rows(count)

    def kernel(spot_ref, marks_ref, a_ref, b_ref, so_ref, q_ref, k_ref, v_ref, dq_ref, dkv_ref, sum_ref, dk_ref, dv_ref):
        totals = None
        for begin in range(0, rows, size):
            source = a_ref if begin < half else b_ref
            local_at = begin % half
            grads = mm_nt(source[local_at : local_at + size], so_ref[...]).astype(LOW)
            blocks = range(begin // tokens, (begin + size) // tokens)
            floor = self_floor(spot_ref, marks_ref, blocks, tokens, True)
            at = slice(begin, begin + size)
            dq, dk, dv = attend_rows_back(q_ref[at], k_ref[...], v_ref[...], grads, floor)
            pre = (dq.astype(LOW).astype(WIDE) * SCALE).astype(LOW)
            dq_ref[at] = pre
            row = column_rows(pre)[0]
            totals = row if totals is None else totals + row
            if begin == 0:
                dk_ref[...] = dk
                dv_ref[...] = dv
            else:
                dk_ref[...] += dk
                dv_ref[...] += dv
        dkv_ref[:, :local] = dk_ref[...].astype(LOW)
        dkv_ref[:, local:] = dv_ref[...].astype(LOW)
        sum_ref[0:1] = totals
        sum_ref[1:2] = column_rows(dv_ref[...])[0]

    return call(
        kernel,
        (shape((rows, local), LOW), shape((count, 2 * local), LOW), shape((2, local), WIDE)),
        spot,
        (marks, low, other, w_so, queries, keys, values),
        flops=10 * rows * keys.size,
        scratch=[pltpu.VMEM((count, local), WIDE), pltpu.VMEM((count, local), WIDE)],
        limit=24,
        cold=(3, 4, 5, 6),
    )


def input_back(query_grad, pair_grad, source_grad, w_q, w_kv, w_ckv, tokens, sources):
    width = w_q.shape[0]
    span = tokens + sources

    def kernel(spot_ref, q_ref, kv_ref, s_ref, wq_ref, wkv_ref, ws_ref, keep_ref, send_ref):
        part = mm_nt(q_ref[...], wq_ref[...]) + mm_nt(kv_ref[...], wkv_ref[...])
        more = mm_nt(s_ref[...], ws_ref[...])
        for kc, ref in enumerate((keep_ref, send_ref)):
            for kx in range(2):
                at = 2 * kc + kx
                start = kx * span
                piece = part[at * tokens : (at + 1) * tokens]
                ref[start : start + tokens] = piece.astype(ref.dtype)
                piece = more[at * sources : (at + 1) * sources]
                ref[start + tokens : start + span] = piece.astype(ref.dtype)

    return call(
        kernel,
        (shape((2 * span, width), WIDE), shape((2 * span, width), LOW)),
        jnp.zeros((1,), jnp.int32),
        (query_grad, pair_grad, source_grad, w_q, w_kv, w_ckv),
        flops=2 * query_grad.shape[0] * (w_q.size + w_kv.size),
        piped=True,
    )


def produce_ffn(spot, activated, grad_low, grad_other, low, other, inner_grad):
    wide = activated.shape[1]
    half, width = grad_low.shape
    part = width // 16

    def kernel(spot_ref, a_ref, g0_ref, g1_ref, x0_ref, x1_ref, u_ref, *refs):
        outs, all_ref = refs[:4], refs[4]
        me = spot_ref[0]
        high = spot_ref[1]
        low = spot_ref[2]
        for place in range(2):
            if place == 0:
                result = mm_tn(a_ref[:half], g0_ref[...]) + mm_tn(a_ref[half:], g1_ref[...])
            else:
                result = mm_tn(x0_ref[...], u_ref[:half]) + mm_tn(x1_ref[...], u_ref[half:])
            for d in range(4):
                for z in range(2):
                    for y in range(2):
                        at = (4 * d + 2 * z + y) * part
                        piece = result[at : at + part]
                        if place == 0:
                            all_ref[low ^ y, high ^ z, d] = piece
                        else:
                            all_ref[high ^ z, low ^ y, me ^ d] = piece
            outs[2 * place][...] = all_ref[0]
            outs[2 * place + 1][...] = all_ref[1].astype(LOW)

    piece = (2, 4, part, width)
    return call(
        kernel,
        (shape(piece, WIDE), shape(piece, LOW)) * 2,
        spot,
        (activated, grad_low, grad_other, low, other, inner_grad),
        flops=8 * half * width * wide,
        scratch=[pltpu.VMEM((2,) + piece, WIDE)],
        limit=16,
        piped=True,
    )


def join_ffn(out_half, out_got, in_half, in_got):
    def kernel(spot_ref, a_ref, b_ref, c_ref, d_ref, out_ref):
        out_ref[0] = (a_ref[0] + b_ref[...].astype(WIDE)).astype(LOW)
        out_ref[1] = (c_ref[0] + d_ref[...].astype(WIDE)).astype(LOW)

    return call(
        kernel,
        shape((2,) + out_got.shape, LOW),
        jnp.zeros((1,), jnp.int32),
        (out_half, out_got, in_half, in_got),
    )


def finish_ffn(spot, out_pieces, in_pieces):
    part, width = out_pieces[0].shape[1:]
    rows = 4 * part

    def kernel(spot_ref, oa_ref, ob_ref, oc_ref, ia_ref, ib_ref, ic_ref, fo_ref, fi_ref):
        me = spot_ref[0]
        high = spot_ref[1]
        low = spot_ref[2]
        for kz in range(2):
            for ky in range(2):
                quarter = ((kz ^ high) * 2 + (ky ^ low)) * part
                source = oc_ref.at[ky] if kz else (ob_ref if ky else oa_ref)
                for d in range(4):
                    row = pl.multiple_of(d * rows + quarter, 16)
                    fo_ref[pl.ds(row, part), :] = source[d].astype(WIDE)
                source = ic_ref.at[kz] if ky else (ib_ref if kz else ia_ref)
                row = pl.multiple_of(quarter, 16)
                for j in range(4):
                    fi_ref[pl.ds(row, part), j * width : (j + 1) * width] = source[me ^ j].astype(WIDE)

    return call(
        kernel,
        (shape((4 * rows, width), WIDE), shape((rows, 4 * width), WIDE)),
        spot,
        tuple(out_pieces) + tuple(in_pieces),
        limit=16,
        piped=True,
    )


def produce_mixed(spot, one_in, one_grad, two_in, two_grad, heads, heads_grads):
    rows, local = one_grad.shape
    width = one_in.shape[1]
    part = local // 4
    pieces = len(heads_grads)
    half = rows // pieces

    def kernel(spot_ref, a_ref, ag_ref, b_ref, bg_ref, o_ref, *refs):
        g_refs, (keep_ref, send_ref, all_ref) = refs[:pieces], refs[pieces:]
        me = spot_ref[0]
        high = spot_ref[1]
        low = spot_ref[2]
        one = mm_tn(a_ref[:rows], ag_ref[...])
        two = mm_tn(b_ref[...], bg_ref[...])
        three = mm_tn(o_ref[:half], g_refs[0][...])
        if pieces == 2:
            three = three + mm_tn(o_ref[half:], g_refs[1][...])
        for z in range(2):
            for y in range(2):
                quarter = (2 * z + y) * part
                for d in range(4):
                    at = d * local + quarter
                    all_ref[low ^ y, high ^ z, me ^ d, :, :local] = one[at : at + part]
                    all_ref[low ^ y, high ^ z, me ^ d, :, local : 3 * local] = two[at : at + part]
                    piece = three[quarter : quarter + part, d * local : (d + 1) * local]
                    all_ref[low ^ y, high ^ z, d, :, 3 * local :] = piece
        keep_ref[...] = all_ref[0]
        send_ref[...] = all_ref[1].astype(LOW)

    operands = (one_in, one_grad, two_in, two_grad, heads) + tuple(heads_grads)
    wide = two_in.shape[0] > 2048
    return call(
        kernel,
        (shape((2, 4, part, width), WIDE), shape((2, 4, part, width), LOW)),
        spot,
        operands,
        flops=2 * width * (one_grad.size + two_grad.size + heads.size),
        scratch=[pltpu.VMEM((2, 2, 4, part, width), WIDE)],
        cold=() if wide else (0, 2, 4) + ((5,) if pieces == 1 else ()),
        piped=wide,
    )


def place_mixed(spot, pieces, late, far_first, fused, earlier=()):
    part, width = pieces.shape[2:]
    local = 4 * part

    def kernel(spot_ref, piece_ref, *refs):
        outs = refs[len(earlier) :]
        me = spot_ref[0]
        for j in range(4):
            block = piece_ref[0, me ^ j].astype(WIDE)
            for p in range(3):
                piece = block[:, p * local : (p + 1) * local]
                if fused:
                    out, at = outs[0], p * width + j * local
                elif p == 0:
                    out, at = outs[0], j * local
                else:
                    out, at = outs[1], (p - 1) * width + j * local
                out[:, at : at + local] = piece
            outs[-1][:, j * local : (j + 1) * local] = piece_ref[0, j, :, 3 * local :].astype(WIDE)

    def source(i, spot):
        return (i ^ spot[1] if far_first else i ^ spot[2], 0, 0, 0)

    def target(i, spot):
        return (2 * i + (spot[2] ^ late) if far_first else 2 * (spot[1] ^ late) + i, 0)

    widths = (3 * width, width) if fused else (width, 2 * width, width)
    outs = tuple(shape((local, w), WIDE) for w in widths)
    return pl.pallas_call(
        kernel,
        out_shape=outs,
        grid_spec=pltpu.PrefetchScalarGridSpec(
            num_scalar_prefetch=1,
            grid=(2,),
            in_specs=[pl.BlockSpec((1, 4, part, width), source)]
            + [pl.BlockSpec(memory_space=pl.ANY) for _ in earlier],
            out_specs=tuple(pl.BlockSpec((part, w), target) for w in widths),
        ),
        input_output_aliases={2 + at: at for at in range(len(earlier))},
        cost_estimate=cost(0, pieces, *outs),
        compiler_params=pltpu.CompilerParams(vmem_limit_bytes=12 << 20),
    )(spot, pieces, *earlier)


def widen_rows(value, tokens):
    rows, width = value.shape

    def kernel(spot_ref, x_ref, top_ref, rest_ref):
        top_ref[...] = x_ref[:tokens].astype(WIDE)
        rest_ref[...] = x_ref[tokens:].astype(WIDE)

    return call(
        kernel,
        (shape((tokens, width), WIDE), shape((rows - tokens, width), WIDE)),
        jnp.zeros((1,), jnp.int32),
        (value,),
    )


def settle(value, *holds):
    def kernel(spot_ref, x_ref, out_ref):
        out_ref[...] = x_ref[...]

    return call(kernel, shape(value.shape, value.dtype), jnp.zeros((1,), jnp.int32), (after(value, *holds),))


def sort_vectors(value, got):
    rows, width = value.shape
    order = (0, 3, 6, 9, 10, 2, 11, 12, 5, 8)

    def kernel(spot_ref, a_ref, b_ref, bias_ref, gain_ref, inner_ref):
        total = a_ref[...] + b_ref[...]
        for at, source in enumerate(order):
            bias_ref[at : at + 1] = total[source : source + 1]
        for at, source in enumerate((1, 4, 7)):
            gain_ref[at : at + 1] = total[source : source + 1]
        for at in range(4):
            inner_ref[at : at + 1] = total[13 + at : 14 + at]

    return call(
        kernel,
        (shape((10, width), WIDE), shape((3, width), WIDE), shape((4, width), WIDE)),
        jnp.zeros((1,), jnp.int32),
        (value, got),
    )


def exchange_sum(keep, send, bit, *holds):
    got = flip_ctx(send, bit)
    if holds:
        got = after(got, *holds)
    return keep + got.astype(WIDE)


def sum_rest(total, *holds):
    lines = lax.axis_size("ctx") // lax.axis_size("fsdp")
    for bit in powers(lax.axis_size("ctx")):
        if bit not in (1, lines):
            low = total.astype(LOW)
            total = low.astype(WIDE) + after(flip_ctx(low, bit), *holds).astype(WIDE)
    return total.astype(LOW)


def trade_columns(low):
    part = low.shape[1]
    local = 4 * part
    far = flip_model(low[2:], 2)
    near = flip_model(jnp.stack([low[1], far[1]]), 1)
    columns = jnp.stack([low[0], near[0], far[0], near[1]])
    return jnp.concatenate([columns[..., : 3 * local], low[..., 3 * local :]], axis=-1)


def gather_pieces(piece, bits, *holds):
    first = after(flip_ctx(piece, bits[0]), *holds)
    both = jnp.stack([piece, first])
    return piece, first, flip_ctx(both, bits[1]), both


def move_columns(mate, cross, *holds):
    line = flip_ctx(after(cross, *holds), 1)
    return flip_model(mate, 1), cross, line, flip_model(cross, 1), flip_model(line, 1)


def core_sum(keep, send):
    mine = keep + flip_model(send, 1).astype(WIDE)
    return mine, flip_model(mine.astype(LOW), 2)


def sum_lines(value):
    for bit in reversed(line_bits()):
        value = value[:bit].astype(WIDE) + flip_ctx(value[bit:], bit).astype(WIDE)
        value = value.astype(LOW)
    return value[0]


def body(
    hidden,
    encoded,
    cotangent,
    dec_seg,
    enc_seg,
    self_qkv,
    self_out,
    cross_q,
    cross_kv,
    cross_out,
    ffn_in,
    ffn_out,
    biases,
    gains,
    ffn_bias,
):
    tokens = hidden.shape[1]
    rows = 4 * tokens
    width = hidden.shape[2]
    sources = encoded.shape[1]
    model = lax.axis_size("fsdp")
    lines = lax.axis_size("ctx") // model
    own = lax.axis_index("fsdp")
    ctx_index = lax.axis_index("ctx")
    local = width // model
    spot = jnp.stack([own, (ctx_index // lines) % 2, ctx_index % 2, ctx_index % lines])
    spot = spot.astype(jnp.int32)

    block = pack_rows(hidden[0], encoded[0], dec_seg, enc_seg)
    self_qkv = after(self_qkv, block)
    block = swap_places(block)
    small = jnp.concatenate([biases, gains, jnp.zeros((3, local), WIDE)], axis=0)
    qkv_own, qkv_mate, qkv_away = prepare_qkv(spot, self_qkv, small)
    qkv_cross = flip_model(qkv_away, 2)
    rest_own, rest_mate, rest_away, w_so, w_co, w_fo = prepare_rest(
        spot, cross_q, cross_kv, ffn_in, self_out, cross_out, ffn_out
    )
    block = after(block, rest_away)
    block_far = flip_model(block, 2)
    qkv_blocks = (qkv_own,) + move_columns(qkv_mate, qkv_cross, block)
    near_rows = jnp.stack([block, block_far])[None]
    near_rows = after(near_rows, qkv_blocks[3])
    rest_cross = flip_model(after(rest_away, block_far), 2)
    for bit in line_bits():
        near_rows = jnp.concatenate([near_rows, flip_ctx(near_rows, bit)], axis=0)
    near_rows = after(near_rows, rest_cross, *qkv_blocks[1:])
    far_rows = flip_model(near_rows, 1)
    rest_blocks = (rest_own,) + move_columns(rest_mate, rest_cross, near_rows)

    inputs, source_rows, queries, keys, values, w_q, w_kv, table, marks, emarks = project(
        spot, near_rows, far_rows, qkv_blocks, tokens, sources
    )
    other = swap_places(after(cotangent[0], rest_cross))
    plain = keys.shape[0] > 2048
    line_ids = (ctx_index % lines) ^ jnp.arange(lines, dtype=jnp.int32)[:, None]
    model_ids = own ^ jnp.array([0, 2, 1, 3], jnp.int32)[None, :]
    starts = (model_ids * lines + line_ids) * tokens
    places = (starts[:, :, None] + jnp.arange(tokens, dtype=jnp.int32)).reshape(-1)
    if plain:
        attended, keep, send = plain_forward(marks, places, queries, keys, values, w_so)
    else:
        attended, keep, send = self_forward(spot, marks, queries, keys, values, w_so, tokens)
    keep, send = after(keep, other), after(send, other)
    mine, away = core_sum(keep, send)
    w_cq, w_ckv, w_fi, source_keys, source_values = arrange_rest(
        spot, rest_blocks, source_rows, table
    )
    away = after(away, w_cq)
    first, first_low, first_normal, first_rate = residual_norm(inputs, mine, away, table, 5, 0)
    first_other = flip_model(first_low, 1)
    other_far = flip_model(after(other, away), 2)
    small_low = small.astype(LOW).astype(WIDE)
    cross_queries, crossed, keep, send, first_all = cross_forward(
        spot, marks, emarks, first_low, first_other, w_cq, source_keys, source_values, w_co, small_low, tokens
    )
    keep, send = after(keep, other_far), after(send, other_far)
    mine, away = core_sum(keep, send)
    second, second_low, second_normal, second_rate = residual_norm(first, mine, away, table, 8, 1)
    second_other = flip_model(second_low, 1)
    inner_bias = ffn_bias.astype(LOW).astype(WIDE)[None]
    activated, slope, keep, send = ffn_forward(second_low, second_other, w_fi, w_fo, inner_bias)
    mine, away = core_sum(keep, send)
    result, third_grad, ffn_low, third_sums = turn_around(
        second, mine, away, table, other, other_far, tokens
    )

    ffn_other = flip_model(ffn_low, 1)
    inner_grad, keep, send, inner_sum = ffn_back(ffn_low, ffn_other, w_fo, w_fi, slope)
    mine, away = core_sum(keep, send)
    out_keep, out_send, in_keep, in_send = produce_ffn(
        spot, activated, ffn_low, ffn_other, second_low, second_other, inner_grad
    )
    away = after(away, in_keep)
    out_got = flip_ctx(out_send, 1)
    in_got = flip_ctx(in_send, lines)
    second_grad, cross_low, second_sums = residual_back(
        third_grad, mine, away, second_normal, second_rate, table, 1, tokens
    )
    cross_other = flip_model(cross_low, 1)
    result = swap_places(after(result, cross_low))
    cross_query_pre, source_grad, keep, send, cross_sums, cross_all = cross_back(
        spot, marks, emarks, cross_low, cross_other, w_co, cross_queries, source_keys, source_values, w_cq, tokens
    )
    keep, send = after(keep, out_got, in_got), after(send, out_got, in_got)
    mine, away = core_sum(keep, send)
    out_half = out_keep + after(out_got, mine).astype(WIDE)
    in_half = in_keep + after(in_got, mine).astype(WIDE)
    out_got = flip_ctx(out_half[1].astype(LOW), lines)
    in_got = flip_ctx(in_half[1].astype(LOW), 1)
    cross_keep, cross_send = produce_mixed(
        spot, after(first_all, result), cross_query_pre, source_rows, source_grad, crossed, (cross_all,)
    )
    away = after(away, cross_keep, out_got, in_got)
    first_grad, self_low, first_sums = residual_back(
        second_grad, mine, away, first_normal, first_rate, table, 0, tokens
    )
    self_other = flip_model(self_low, 1)
    cross_got = flip_ctx(cross_send, 1)
    ffn_total = join_ffn(out_half, after(out_got, self_low), in_half, after(in_got, self_low))
    self_low = after(self_low, ffn_total)
    if plain:
        self_query_pre, pair_grad, self_sums = plain_back(
            marks, places, self_low, self_other, w_so, queries, keys, values
        )
    else:
        self_query_pre, pair_grad, self_sums = self_back(
            spot, marks, self_low, self_other, w_so, queries, keys, values, tokens
        )
    self_keep, self_send = produce_mixed(
        spot, inputs, self_query_pre, inputs, pair_grad, attended, (self_low, self_other)
    )
    self_half = exchange_sum(self_keep, self_send, 1)
    cross_half = cross_keep + after(cross_got, self_keep).astype(WIDE)
    wide_rows = jnp.concatenate([first_sums, second_sums, third_sums], axis=0)
    wide_rows = wide_rows + after(flip_model(wide_rows, 1), cross_half)
    wide_rows = lax.dynamic_slice_in_dim(wide_rows, own * local, local, axis=1)
    vectors = jnp.concatenate(
        [wide_rows, after(self_sums, cross_half), after(cross_sums, cross_half), after(inner_sum, cross_half).reshape(-1, local)], axis=0
    )
    vectors = jnp.pad(vectors, ((0, 32 - vectors.shape[0]), (0, 0))).reshape(16, 2 * local)
    cross_total = exchange_sum(cross_half[0], cross_half[1].astype(LOW), lines, self_half)
    ffn_total = sum_rest(ffn_total, self_half)
    lined = jnp.concatenate(
        [
            pair_grad.reshape(lines, rows, 2 * local),
            source_grad.reshape(lines, 4 * sources, 2 * local),
            jnp.broadcast_to(vectors.astype(LOW)[None], (lines,) + vectors.shape),
        ],
        axis=1,
    )
    lined = sum_lines(after(lined, self_half))
    pair_own = lined[:rows]
    source_own = lined[rows : rows + 4 * sources]
    vectors = lined[rows + 4 * sources :].astype(WIDE)
    keep, send = input_back(
        self_query_pre, pair_own, source_own, w_q, w_kv, w_ckv, tokens, sources
    )
    both_half = keep + flip_model(send, 1).astype(WIDE)
    span = tokens + sources
    both = both_half[:span] + flip_model(both_half[span:].astype(LOW), 2).astype(WIDE)
    both = jnp.concatenate([both[:tokens] + first_grad[:tokens], both[tokens:]], axis=0)
    both = both.astype(LOW)
    hidden_grad, encoded_grad = widen_rows(swap_places(both), tokens)
    hidden_grad = hidden_grad[None]
    encoded_grad = encoded_grad[None]

    cross_total = after(cross_total, ffn_total)
    self_total = exchange_sum(self_half[0], self_half[1].astype(LOW), lines, lined, cross_total)
    ffn_far = flip_model(ffn_total[1, 2:], 2)
    ffn_near = flip_model(jnp.stack([ffn_total[1, 1], ffn_far[1]]), 1)
    ffn_piece = jnp.stack([ffn_total[1, 0], ffn_near[0], ffn_far[0], ffn_near[1]])
    out_pieces = gather_pieces(ffn_total[0], (1, lines))
    in_pieces = gather_pieces(ffn_piece, (lines, 1))
    cross_piece = sum_rest(cross_total, self_total)
    self_piece = sum_rest(self_total, out_pieces[1])
    self_traded = trade_columns(self_piece)
    cross_pieces = gather_pieces(trade_columns(cross_piece), (1, lines), self_traded)
    cross_early = place_mixed(spot, cross_pieces[3], 0, False, False)
    vectors = vectors.reshape(-1, local)
    bits = powers(lax.axis_size("ctx"))[len(line_bits()) :]
    for bit in bits[:-1]:
        vectors = vectors + after(flip_ctx(vectors, bit), self_traded)
    self_pieces = gather_pieces(self_traded, (lines, 1), vectors)
    g_fo, g_fi = finish_ffn(spot, out_pieces[:3], in_pieces[:3])
    self_early = place_mixed(spot, self_pieces[3], 0, True, True)
    output = settle(result, self_piece)[None]
    last = after(self_pieces[2], g_fi, output, cross_early[0], self_early[0])
    g_qkv, g_so = place_mixed(spot, last, 1, True, True, self_early)
    g_cq, g_ckv, g_co = place_mixed(spot, cross_pieces[2], 1, False, False, cross_early)
    d_bias, d_gain, d_inner = sort_vectors(vectors, after(flip_ctx(vectors, bits[-1]), g_fi))
    d_inner = d_inner.reshape(-1)
    return (
        output,
        hidden_grad,
        encoded_grad,
        g_qkv,
        g_so,
        g_cq,
        g_ckv,
        g_co,
        g_fi,
        g_fo,
        d_bias,
        d_gain,
        d_inner,
    )


def solution(mesh):
    whole = P("fsdp", "ctx", None)
    matrix = P("fsdp", None)
    ids = P("fsdp", "ctx")
    table = P(None, "fsdp")
    return jax.shard_map(
        body,
        mesh=mesh,
        in_specs=(whole, whole, whole, ids, ids) + (matrix,) * 7 + (table, table, P("fsdp")),
        out_specs=(whole,) * 3 + (matrix,) * 7 + (table, table, P("fsdp")),
        check_vma=False,
    )
```
